128 devices in a mesh: gx: 4 (over x), gy: 32 (over y, z, core).
Axes of the slice: x: 4, y: 4, z: 4, core: 2. Of those that a mesh axis runs over, the one named last changes fastest.
Arguments:
- old_state: float32 [1024, 6, 32768], P(('gx', 'gy')), may hold values from -6 to 6
- old_owner: int32 [512], replicated, may hold values from 0 to 127, as said below
- old_slot: int32 [512], replicated, may hold values from 0 to 7, as said below
- diffusivity: float32 [6], replicated, may hold values from 0.01 to 0.08
Outputs:
- new_state: float32 [512, 6, 32768], P(('gx', 'gy'))
The draws below stay inside these ranges and needn't reach their ends.
Inputs may be any that keep to these rules, and one draw needn't show every extreme that they name: The curve is closed: with n = g // 4 the new owner of box g, old_owner[g] is n, or n - 1 modulo the device count for one of the first 2 boxes of n, or n + 1 modulo the device count for one of the last 2 boxes of n. `old_slot`: A box kept by its owner sits in slot 2 + g % 4; the j-th of the first 2 boxes of a device, when held by the device below, sat in that device's slot 6 + j; the j-th of the last 2 boxes, when held by the device above, sat in its slot j. Slots that hold no box hold anything. Some device takes over 2 boxes from each neighbour in every draw.
All inputs are finite; a program needn't handle non-finite values.
Results may differ from the reference program's by a relative error of at most 0.0003.
Values sent between devices are 32-bit elements; how exact they have to be, the bound alone decides.
No kernel may reach another device: no remote copies, remote signals or barrier semaphores. Data moves between devices by JAX's collectives and lax.ppermute only.
A program may use at most 128 MiB of HBM per device.

```python
import math
import jax
import jax.numpy as jnp
from jax import lax

B = 32
F = 6
CAP = 4
DRIFT = 2
OLD_CAP = 8
NBOX = 512
SLOTS = 1024
CELLS = 32768
N_GX = 4
N_GY = 32


def owner_and_slot(key):
    devices = NBOX // CAP
    coins = jax.random.randint(jax.random.fold_in(key, 17), (devices, CAP), 0, 2).astype(jnp.int32)
    device = jnp.arange(devices, dtype=jnp.int32)
    forced = (device == 0) | (device == 1) | (device == devices // 2 - 1) | (device == devices // 2) | (device == devices // 2 + 1) | (device == devices - 2) | (device == devices - 1)
    coins = jnp.where(forced[:, None], 1, coins).astype(jnp.int32)
    column = jnp.arange(CAP, dtype=jnp.int32)[None, :]
    owner_home = jnp.broadcast_to(device[:, None], (devices, CAP)).astype(jnp.int32)
    from_below = (column < DRIFT) & (coins == 1)
    from_above = (column >= CAP - DRIFT) & (coins == 1)
    owner = jnp.where(from_below, (owner_home - 1 + devices) % devices, jnp.where(from_above, (owner_home + 1) % devices, owner_home))
    kept_slot = jnp.broadcast_to(DRIFT + column, (devices, CAP))
    slot = jnp.where(from_below, OLD_CAP - DRIFT + column, jnp.where(from_above, column - (CAP - DRIFT), kept_slot))
    return (owner.reshape(NBOX).astype(jnp.int32), slot.reshape(NBOX).astype(jnp.int32))


def draw_old_owner(key, part):
    return owner_and_slot(key)[0]


def draw_old_slot(key, part):
    return owner_and_slot(key)[1]


def levels(stream_key, dims, split, smallest, top_value):
    level = 1.0
    for dim, parts in split:
        heights = jax.random.uniform(jax.random.fold_in(jax.random.fold_in(stream_key, 6), dim), (parts,), jnp.float32, smallest / len(split), top_value / len(split))
        level = level * jnp.repeat(jnp.exp(heights), dims[dim] // parts).reshape((-1,) + (1,) * (len(dims) - 1 - dim))
    return level


def gaussian(rng, shape, scale, most, pieces=(), kind=jnp.bfloat16):
    gain = levels(rng, shape, pieces, -0.22, 0.18) if pieces else 1.0
    result = jax.random.normal(rng, shape, jnp.float32) * scale * gain
    return jnp.minimum(jnp.maximum(result, -most), most).astype(kind)


def setup_inputs(seed: int = 0) -> dict:
    splits = jax.random.split(jax.random.key(seed), 5)
    old_state = gaussian(splits[0], (SLOTS, F, CELLS), 1.0, 6.0, ((0, 128),), jnp.float32)
    old_owner = draw_old_owner(jax.random.fold_in(splits[4], 71), 0)
    old_slot = draw_old_slot(jax.random.fold_in(splits[4], 71), 0)
    diffusivity = jnp.clip(jnp.exp(jax.random.uniform(splits[3], (F,), jnp.float32, math.log(0.01), math.log(0.08))), 0.01, 0.08)
    return dict(old_state=old_state, old_owner=old_owner, old_slot=old_slot, diffusivity=diffusivity)


courant = 0.25


def minmod(former, latter):
    return 0.5 * (jnp.sign(former) + jnp.sign(latter)) * jnp.minimum(jnp.abs(former), jnp.abs(latter))


def part_of(values, bottom, ceiling, dimension):
    return lax.slice_in_dim(values, bottom, ceiling, axis=dimension)


def along(stripe, dimension, velocity_index, spread):
    length = stripe.shape[dimension]
    differ = part_of(stripe, 1, length, dimension) - part_of(stripe, 0, length - 1, dimension)
    slopes = minmod(part_of(differ, 0, length - 2, dimension), part_of(differ, 1, length - 1, dimension))
    left_side = part_of(stripe, 1, length - 2, dimension) + 0.5 * part_of(slopes, 0, length - 3, dimension)
    rights = part_of(stripe, 2, length - 1, dimension) - 0.5 * part_of(slopes, 1, length - 2, dimension)
    velocity = stripe[velocity_index:velocity_index + 1]
    face_speed = 0.5 * (part_of(velocity, 1, length - 2, dimension) + part_of(velocity, 2, length - 1, dimension))
    conduct = jnp.exp(0.5 * jnp.tanh(stripe[5:6]))
    face_conduct = 0.5 * (part_of(conduct, 1, length - 2, dimension) + part_of(conduct, 2, length - 1, dimension))
    fluxes = jnp.maximum(face_speed, 0.0) * left_side + jnp.minimum(face_speed, 0.0) * rights
    gradient = spread * face_conduct * part_of(differ, 1, length - 2, dimension)
    net_flux = gradient - courant * fluxes
    return part_of(net_flux, 1, length - 3, dimension) - part_of(net_flux, 0, length - 4, dimension)


def advance(zstripe, ystripe, xstripe, diffusivity):
    spread = diffusivity.reshape(-1, 1, 1, 1)
    center = part_of(xstripe, 2, xstripe.shape[3] - 2, 3)
    total = center + along(zstripe, 1, 2, spread)
    total = total + along(ystripe, 2, 1, spread)
    return total + along(xstripe, 3, 0, spread)


def reference(old_state, old_owner, old_slot, diffusivity):
    rows = (old_owner * OLD_CAP + old_slot).astype(jnp.int32)
    gathered = old_state[rows]
    domain = gathered.reshape(N_GX, N_GY, CAP, F, B, B, B).transpose(3, 0, 4, 1, 5, 2, 6)
    domain = domain.reshape(F, N_GX * B, N_GY * B, CAP * B)
    padded = jnp.pad(domain, ((0, 0), (2, 2), (2, 2), (2, 2)), mode="edge")

    def advance_device(device):
        row_z = ((device // N_GY) * B).astype(jnp.int32)
        row_y = ((device % N_GY) * B).astype(jnp.int32)
        window = lax.dynamic_slice(padded, (jnp.int32(0), row_z, row_y, jnp.int32(0)), (F, B + 4, B + 4, CAP * B + 4))
        return advance(window[:, :, 2:-2, 2:-2], window[:, 2:-2, :, 2:-2], window[:, 2:-2, 2:-2, :], diffusivity)

    updated = lax.map(advance_device, jnp.arange(N_GX * N_GY, dtype=jnp.int32))
    updated = updated.reshape(N_GX * N_GY, F, B, B, CAP, B).transpose(0, 4, 1, 2, 3, 5)
    return updated.reshape(NBOX, F, B * B * B)
```

```python
import jax
import jax.numpy as jnp
from jax import lax
from jax.experimental import pallas as pl
from jax.experimental.pallas import tpu as pltpu
from jax.sharding import PartitionSpec as P

B = 32
F = 6
CAP = 4
ROWS = 8
LANES = 128
AXES = ("gx", "gy")
F32 = jnp.float32
HBM = pl.BlockSpec(memory_space=pl.ANY)
SMEM = pl.BlockSpec(memory_space=pltpu.SMEM)
MIB = 1 << 20


def run_all(copies):
    for copy in copies:
        copy.start()
    for copy in copies:
        copy.wait()


def pack_body(x, up, down, sem):
    copies = []
    for j in range(2):
        copies.append(pltpu.make_async_copy(x.at[:, :, :, 6 + j], up.at[j], sem.at[j]))
        copies.append(pltpu.make_async_copy(x.at[:, :, :, j], down.at[j], sem.at[2 + j]))
    run_all(copies)


def pack(x):
    shape = jax.ShapeDtypeStruct((2, F, B, ROWS, 1, LANES), F32)
    return pl.pallas_call(
        pack_body,
        name="pack",
        out_shape=(shape, shape),
        in_specs=[HBM],
        out_specs=(HBM, HBM),
        scratch_shapes=[pltpu.SemaphoreType.DMA((4,))],
    )(x)


def device_number():
    return lax.axis_index("gx") * lax.axis_size("gy") + lax.axis_index("gy")


def kept_flags(owner):
    device = device_number()
    return [owner[device * CAP + c] == device for c in range(CAP)]


def from_box(kept, c, x, up, down, pick, target, sem):
    moved = (up if c < 2 else down).at[c % 2]

    @pl.when(kept)
    def _():
        pltpu.make_async_copy(pick(x.at[:, :, :, 2 + c]), target, sem).start()

    @pl.when(jnp.logical_not(kept))
    def _():
        pltpu.make_async_copy(pick(moved), target, sem).start()

    return pltpu.make_async_copy(pick(moved), target, sem)


def lane_chunk(shape):
    return lax.broadcasted_iota(jnp.int32, shape, len(shape) - 1)


def edges_body(owner, x, up, down, z_low, z_high, y_low, y_high, first, last, sem, sem_y):
    kept = kept_flags(owner)
    waits, waits_y = [], []
    for c in range(CAP):
        part = lambda row: (lambda ref: ref.at[:, :, row, 0])
        waits_y.append(from_box(kept[c], c, x, up, down, part(0), first.at[c], sem_y.at[c]))
        waits_y.append(from_box(kept[c], c, x, up, down, part(7), last.at[c], sem_y.at[4 + c]))
    for c in range(CAP):
        waits.append(
            from_box(kept[c], c, x, up, down, lambda r: r.at[:, 0:2], z_low.at[c], sem.at[c])
        )
        waits.append(
            from_box(kept[c], c, x, up, down, lambda r: r.at[:, 30:32], z_high.at[c], sem.at[4 + c])
        )
    for wait in waits_y:
        wait.wait()
    left = lane_chunk((16, LANES)) < 64
    for c in range(CAP):
        for f in range(F):
            low, high = first[c, f, 0:16], first[c, f, 16:32]
            y_low[c, f] = jnp.where(left, low, pltpu.roll(high, 64, 1))
            low, high = last[c, f, 0:16], last[c, f, 16:32]
            y_high[c, f] = jnp.where(left, pltpu.roll(low, 64, 1), high)
    for wait in waits:
        wait.wait()


def edges(owner, x, up, down):
    z_shape = jax.ShapeDtypeStruct((CAP, F, 2, ROWS, 1, LANES), F32)
    y_shape = jax.ShapeDtypeStruct((CAP, F, 16, LANES), F32)
    vmem = pl.BlockSpec(memory_space=pltpu.VMEM)
    return pl.pallas_call(
        edges_body,
        name="edges",
        out_shape=(z_shape, z_shape, y_shape, y_shape),
        in_specs=[SMEM, HBM, HBM, HBM],
        out_specs=(HBM, HBM, vmem, vmem),
        scratch_shapes=[
            pltpu.VMEM((CAP, F, B, LANES), F32),
            pltpu.VMEM((CAP, F, B, LANES), F32),
            pltpu.SemaphoreType.DMA((8,)),
            pltpu.SemaphoreType.DMA((8,)),
        ],
    )(owner, x, up, down)


def minmod(a, b):
    return jnp.maximum(jnp.minimum(a, b), jnp.minimum(jnp.maximum(a, b), 0.0))


def conduction(v):
    return jnp.exp(0.5 * jnp.tanh(v))


def step_body(
    owner, spread, x, up, down, z_below, z_above, y_below, y_above, out,
    q, result, face_a, face_b, carry_p, carry_n, carry_c, sem, sem_z, sem_y, sem_out, halo_low, halo_high,
):
    kept = kept_flags(owner)
    gx, gy = lax.axis_index("gx"), lax.axis_index("gy")
    last_x, last_y = lax.axis_size("gx") - 1, lax.axis_size("gy") - 1
    copies = [
        pltpu.make_async_copy(z_below, q.at[:, :, 0:2], sem_z.at[0]),
        pltpu.make_async_copy(z_above, q.at[:, :, B + 2 : B + 4], sem_z.at[1]),
        pltpu.make_async_copy(y_below, halo_low, sem_y.at[0]),
        pltpu.make_async_copy(y_above, halo_high, sem_y.at[1]),
    ]
    for copy in copies:
        copy.start()
    for c in range(CAP):
        copies.append(
            from_box(
                kept[c], c, x, up, down, lambda r: r.at[:, :, :, 0], q.at[c, :, 2 : B + 2], sem.at[c]
            )
        )
    for copy in copies:
        copy.wait()

    @pl.when(gx == 0)
    def _():
        for c in range(CAP):
            for f in range(F):
                q[c, f, 0] = q[c, f, 2]
                q[c, f, 1] = q[c, f, 2]

    @pl.when(gx == last_x)
    def _():
        for c in range(CAP):
            for f in range(F):
                q[c, f, B + 2] = q[c, f, B + 1]
                q[c, f, B + 3] = q[c, f, B + 1]

    lane = lax.broadcasted_iota(jnp.int32, (8, LANES), 1)
    sub = lax.broadcasted_iota(jnp.int32, (8, LANES), 0)
    chunk = lane // 32
    x_in = lane % 32
    scale = [0.5 * spread[f] for f in range(F)]

    def y_faces(c, block):
        z0 = block * 8
        half = z0 // 16
        left = lane < 64

        def rows(f):
            below = halo_low[c, f, pl.ds(z0 - 16 * half, 8)]
            above = halo_high[c, f, pl.ds(z0 - 16 * half, 8)]
            row0 = q[c, f, z0 + 2 : z0 + 10, 0, :]
            row7 = q[c, f, z0 + 2 : z0 + 10, 7, :]
            r70, r71 = pltpu.roll(row7, 32, 1), pltpu.roll(row7, 64, 1)
            r02, r03 = pltpu.roll(row0, 64, 1), pltpu.roll(row0, 96, 1)
            if half == 0:
                below = pltpu.roll(below, 64, 1)
            else:
                above = pltpu.roll(above, 64, 1)
            above = jnp.where(gy == last_y, jnp.where(chunk == 0, r70, r71), above)
            below = jnp.where(gy == 0, jnp.where(chunk == 3, r03, r02), below)
            r = jnp.where(left, above, below)
            s1 = jnp.where(chunk == 0, r70, r03)
            return r, s1, r02

        r1, s11, _ = rows(1)
        weight = 0.0625 * (r1 + s11)
        r5, s15, _ = rows(5)
        cond = conduction(r5) + conduction(s15)
        for f in range(F):
            r, s1, s2 = rows(f)
            r2 = jnp.where(chunk == 0, pltpu.roll(r, 96, 1), pltpu.roll(r, 32, 1))
            da, db = r - s1, r2 - r
            e = (r + r) - minmod(da, db)
            m0 = (s1 + s1) - minmod(-da, s2 - s1)
            net = -(scale[f] * cond) * da - weight * jnp.where(weight > 0.0, e, m0)
            face_a[c, f, z0 : z0 + 8, :] = jnp.where(chunk == 0, r, -da)
            face_b[c, f, z0 : z0 + 8, :] = jnp.where(chunk == 0, e, net)

    for c in range(CAP):
        for block in range(4):
            y_faces(c, block)

    head = (sub == 0) & (lane < 32)
    tail = (sub == 7) & (lane >= 96)

    def y_next(value, row):
        m = pltpu.roll(jnp.where(head, row, value), 96, 1)
        return jnp.where(lane < 96, m, pltpu.roll(m, 7, 0))

    def y_last(value, row):
        m = pltpu.roll(jnp.where(tail, row, value), 32, 1)
        return jnp.where(lane >= 32, m, pltpu.roll(m, 1, 0))

    next_index = (lane & 96) | ((lane + 1) & 31)
    last_index = (lane & 96) | ((lane + 31) & 31)

    def x_next(values, ends):
        result = []
        for c in range(CAP):
            if c < CAP - 1:
                m = jnp.where(x_in == 0, values[c + 1], values[c])
                result.append(jnp.take_along_axis(m, next_index, axis=1))
            else:
                m = jnp.take_along_axis(values[c], next_index, axis=1)
                result.append(jnp.where(x_in == 31, ends, m))
        return result

    def x_last(values, ends):
        result = []
        for c in range(CAP):
            if c > 0:
                m = jnp.where(x_in == 31, values[c - 1], values[c])
                result.append(jnp.take_along_axis(m, last_index, axis=1))
            else:
                m = jnp.take_along_axis(values[c], last_index, axis=1)
                result.append(jnp.where(x_in == 0, ends, m))
        return result

    def z_face(c, f, z, weight, cond):
        here, after, more = q[c, f, z + 2], q[c, f, z + 3], q[c, f, z + 4]
        d = after - here
        slope = minmod(d, more - after)
        twice = after + after
        state = jnp.where(weight > 0.0, carry_p[c, f], twice - slope)
        carry_p[c, f] = twice + slope
        return (scale[f] * cond) * d - weight * state

    for c in range(CAP):
        carry_c[c] = conduction(q[c, 5, 2])
        cond = conduction(q[c, 5, 1]) + carry_c[c]
        weight = 0.0625 * (q[c, 2, 1] + q[c, 2, 2])
        for f in range(F):
            one, two, three = q[c, f, 0], q[c, f, 1], q[c, f, 2]
            carry_p[c, f] = (two + two) + minmod(two - one, three - two)
            carry_n[c, f] = z_face(c, f, -1, weight, cond)

    boxes = range(CAP)

    def plane(z, _):
        here = [carry_c[c] for c in boxes]
        above = [conduction(q[c, 5, z + 3]) for c in boxes]
        cond_z = [here[c] + above[c] for c in boxes]
        for c in boxes:
            carry_c[c] = above[c]
        cond_x = [a + b for a, b in zip(here, x_next(here, here[-1]))]
        edge5 = [face_a[c, 5, pl.ds(z, 1), :] for c in boxes]
        cond_y = [here[c] + y_next(here[c], conduction(edge5[c])) for c in boxes]
        u = [q[c, 0, z + 2] for c in boxes]
        weight_x = [0.0625 * (a + b) for a, b in zip(u, x_next(u, u[-1]))]
        v = [q[c, 1, z + 2] for c in boxes]
        weight_y = [0.0625 * (v[c] + y_next(v[c], face_a[c, 1, pl.ds(z, 1), :])) for c in boxes]
        weight_z = [0.0625 * (q[c, 2, z + 2] + q[c, 2, z + 3]) for c in boxes]
        for f in range(F):
            value = [q[c, f, z + 2] for c in boxes]
            twice = [a + a for a in value]
            total = []
            for c in boxes:
                net = z_face(c, f, z, weight_z[c], cond_z[c])
                total.append(value[c] + (net - carry_n[c, f]))
                carry_n[c, f] = net
            for c in boxes:
                row_a, row_b = face_a[c, f, pl.ds(z, 1), :], face_b[c, f, pl.ds(z, 1), :]
                d = y_next(value[c], row_a) - value[c]
                slope = minmod(y_last(d, row_a), d)
                right = y_next(twice[c] - slope, row_b)
                state = jnp.where(weight_y[c] > 0.0, twice[c] + slope, right)
                net = (scale[f] * cond_y[c]) * d - weight_y[c] * state
                total[c] = total[c] + (net - y_last(net, row_b))
            d = [b - a for a, b in zip(value, x_next(value, value[-1]))]
            slope = [minmod(a, b) for a, b in zip(x_last(d, 0.0), d)]
            right = x_next([a - b for a, b in zip(twice, slope)], twice[-1])
            net = []
            for c in boxes:
                state = jnp.where(weight_x[c] > 0.0, twice[c] + slope[c], right[c])
                net.append((scale[f] * cond_x[c]) * d[c] - weight_x[c] * state)
            before = x_last(net, -0.125 * u[0] * twice[0])
            for c in boxes:
                result[c, f, z] = total[c] + (net[c] - before[c])
        return 0

    lax.fori_loop(0, B, plane, 0)
    run_all(
        [
            pltpu.make_async_copy(result.at[c], out.at[:, :, :, c, 0], sem_out.at[c])
            for c in boxes
        ]
    )


def step(owner, spread, x, up, down, z_below, z_above, y_below, y_above):
    return pl.pallas_call(
        step_body,
        name="step",
        out_shape=jax.ShapeDtypeStruct((F, B, ROWS, CAP, 1, LANES), F32),
        in_specs=[SMEM, SMEM] + [HBM] * 7,
        out_specs=HBM,
        scratch_shapes=[
            pltpu.VMEM((CAP, F, B + 4, ROWS, LANES), F32),
            pltpu.VMEM((CAP, F, B, ROWS, LANES), F32),
            pltpu.VMEM((CAP, F, B, LANES), F32),
            pltpu.VMEM((CAP, F, B, LANES), F32),
            pltpu.VMEM((CAP, F, ROWS, LANES), F32),
            pltpu.VMEM((CAP, F, ROWS, LANES), F32),
            pltpu.VMEM((CAP, ROWS, LANES), F32),
            pltpu.SemaphoreType.DMA((CAP,)),
            pltpu.SemaphoreType.DMA((2,)),
            pltpu.SemaphoreType.DMA((2,)),
            pltpu.SemaphoreType.DMA((CAP,)),
            pltpu.VMEM((CAP, F, 16, LANES), F32),
            pltpu.VMEM((CAP, F, 16, LANES), F32),
        ],
        compiler_params=pltpu.CompilerParams(vmem_limit_bytes=24 * MIB),
    )(owner, spread, x, up, down, z_below, z_above, y_below, y_above)


def along_curve(block, distance):
    count = lax.axis_size(AXES)
    return lax.ppermute(block, AXES, [(i, (i + distance) % count) for i in range(count)])


def along_axis(block, axis, distance):
    count = lax.axis_size(axis)
    pairs = [(i, i + distance) for i in range(count) if 0 <= i + distance < count]
    return lax.ppermute(block, axis, pairs)


def local(old_state, old_owner, old_slot, diffusivity):
    x = old_state.reshape(8, F, B, ROWS, LANES).transpose(1, 2, 3, 0, 4)[..., None, :]
    up, down = pack(x)
    up = along_curve(up, 1)
    down = along_curve(down, -1)
    z_low, z_high, y_low, y_high = edges(old_owner, x, up, down)
    z_below = along_axis(z_high, "gx", 1)[:, :, :, :, 0]
    z_above = along_axis(z_low, "gx", -1)[:, :, :, :, 0]
    y_below = along_axis(y_high, "gy", 1)
    y_above = along_axis(y_low, "gy", -1)
    out = step(old_owner, diffusivity, x, up, down, z_below, z_above, y_below, y_above)
    return out[..., 0, :].transpose(3, 0, 1, 2, 4).reshape(CAP, F, B * B * B)


def solution(mesh):
    placed = (P(AXES, None, None), P(), P(), P())
    return jax.shard_map(
        local, mesh=mesh, in_specs=placed, out_specs=P(AXES, None, None), check_vma=False
    )
```

```python
import jax
import jax.numpy as jnp
from jax import lax
from jax.experimental import pallas as pl
from jax.experimental.pallas import tpu as pltpu
from jax.sharding import PartitionSpec as P

B = 32
F = 6
CAP = 4
ROWS = 8
LANES = 128
AXES = ("gx", "gy")
F32 = jnp.float32
HBM = pl.BlockSpec(memory_space=pl.ANY)
VMEM = pl.BlockSpec(memory_space=pltpu.VMEM)
SMEM = pl.BlockSpec(memory_space=pltpu.SMEM)
WIDE = 56 << 20


def run_all(copies):
    for copy in copies:
        copy.start()
    for copy in copies:
        copy.wait()


def pack_body(x, up, down, sem):
    copies = []
    for j in range(2):
        copies.append(pltpu.make_async_copy(x.at[:, :, :, 6 + j, 0], up.at[j], sem.at[j]))
        copies.append(pltpu.make_async_copy(x.at[:, :, :, j, 0], down.at[j], sem.at[2 + j]))
    run_all(copies)


def pack(x):
    shape = jax.ShapeDtypeStruct((2, F, B, ROWS, LANES), F32)
    return pl.pallas_call(
        pack_body,
        name="pack",
        out_shape=(shape, shape),
        in_specs=[HBM],
        out_specs=(VMEM, VMEM),
        scratch_shapes=[pltpu.SemaphoreType.DMA((4,))],
        compiler_params=pltpu.CompilerParams(vmem_limit_bytes=WIDE),
    )(x)


def device_number():
    return lax.axis_index("gx") * lax.axis_size("gy") + lax.axis_index("gy")


def kept_flags(owner):
    device = device_number()
    return [owner[device * CAP + c] == device for c in range(CAP)]


def from_box(kept, c, x, up, down, pick, target, sem):
    moved = (up if c < 2 else down).at[c % 2]

    @pl.when(kept)
    def _():
        pltpu.make_async_copy(pick(x.at[:, :, :, 2 + c]), target, sem).start()

    @pl.when(jnp.logical_not(kept))
    def _():
        pltpu.make_async_copy(pick(moved), target, sem).start()

    return pltpu.make_async_copy(pick(moved), target, sem)


def chunk_of_lane(shape):
    return lax.broadcasted_iota(jnp.int32, shape, len(shape) - 1) // 32


def layers(rows, j):
    chunk = chunk_of_lane(rows[0].shape)
    parts = [row if c == j else pltpu.roll(row, 32 * (c - j) % 128, 1) for c, row in enumerate(rows)]
    low = jnp.where(chunk == 0, parts[0], parts[1])
    high = jnp.where(chunk == 2, parts[2], parts[3])
    return jnp.where(chunk < 2, low, high)


def edges_body(owner, x, up, down, z_low, z_high, y_low, y_high, first, last, sem, sem_y):
    kept = kept_flags(owner)
    waits, waits_y = [], []
    for c in range(CAP):
        part = lambda row: (lambda ref: ref.at[:, :, row, 0])
        waits_y.append(from_box(kept[c], c, x, up, down, part(0), first.at[c], sem_y.at[c]))
        waits_y.append(from_box(kept[c], c, x, up, down, part(7), last.at[c], sem_y.at[4 + c]))
    for c in range(CAP):
        part = lambda z: (lambda ref: ref.at[:, z : z + 2, :, 0])
        waits.append(from_box(kept[c], c, x, up, down, part(0), z_low.at[c], sem.at[c]))
        waits.append(from_box(kept[c], c, x, up, down, part(30), z_high.at[c], sem.at[4 + c]))
    for wait in waits_y:
        wait.wait()
    for f in range(F):
        rows = [first[c, f] for c in range(CAP)]
        y_low[f, 0], y_low[f, 1] = layers(rows, 0), layers(rows, 1)
        rows = [last[c, f] for c in range(CAP)]
        y_high[f, 0], y_high[f, 1] = layers(rows, 2), layers(rows, 3)
    for wait in waits:
        wait.wait()


def edges(owner, x, up, down):
    z_shape = jax.ShapeDtypeStruct((CAP, F, 2, ROWS, LANES), F32)
    y_shape = jax.ShapeDtypeStruct((F, 2, B, LANES), F32)
    return pl.pallas_call(
        edges_body,
        name="edges",
        out_shape=(z_shape, z_shape, y_shape, y_shape),
        in_specs=[SMEM, HBM, HBM, HBM],
        out_specs=(VMEM, VMEM, VMEM, VMEM),
        scratch_shapes=[
            pltpu.VMEM((CAP, F, B, LANES), F32),
            pltpu.VMEM((CAP, F, B, LANES), F32),
            pltpu.SemaphoreType.DMA((8,)),
            pltpu.SemaphoreType.DMA((8,)),
        ],
        compiler_params=pltpu.CompilerParams(vmem_limit_bytes=WIDE),
    )(owner, x, up, down)


def minmod(a, b):
    return jnp.maximum(jnp.minimum(a, b), jnp.minimum(jnp.maximum(a, b), 0.0))


def conduction(v):
    return jnp.exp(0.5 * jnp.tanh(v))


def swap_64(a, b, lane):
    low = lane < 64
    m = pltpu.roll(jnp.where(low, b, a), 64, 1)
    return jnp.where(low, a, m), jnp.where(low, m, b)


def swap_32(a, b, lane):
    even = (lane & 32) == 0
    m = jnp.where(even, b, a)
    return jnp.where(even, a, pltpu.roll(m, 32, 1)), jnp.where(even, pltpu.roll(m, 96, 1), b)


LEAD = 5
J = range(4)


def step_body(
    owner, spread, x, up, down, z_below, z_above, y_below, y_above, out,
    box, q, result, left_d, left_n, right_q, right_m, right_c, carry_p, carry_n, carry_c,
    half, dx, dx_old, cx, cx_old, px, mx, nx, done, turned, sem, sem_z, sem_out,
):
    kept = kept_flags(owner)
    gx, gy = lax.axis_index("gx"), lax.axis_index("gy")
    last_x, last_y = lax.axis_size("gx") - 1, lax.axis_size("gy") - 1
    copies = [
        pltpu.make_async_copy(z_below, box.at[:, :, 0:2], sem_z.at[0]),
        pltpu.make_async_copy(z_above, box.at[:, :, B + 2 : B + 4], sem_z.at[1]),
    ]
    for copy in copies:
        copy.start()
    for c in range(CAP):
        copies.append(
            from_box(
                kept[c], c, x, up, down, lambda r: r.at[:, :, :, 0], box.at[c, :, 2 : B + 2], sem.at[c]
            )
        )
    for copy in copies:
        copy.wait()

    lane = lax.broadcasted_iota(jnp.int32, (8, LANES), 1)
    sub = lax.broadcasted_iota(jnp.int32, (8, LANES), 0)
    scale = [0.5 * spread[f] for f in range(F)]

    def turn_first(p):
        for f in range(F):
            v = [box[c, f, p] for c in range(CAP)]
            half[f, 0], half[f, 2] = swap_64(v[0], v[2], lane)
            half[f, 1], half[f, 3] = swap_64(v[1], v[3], lane)

    def turn(p, _):
        for f in range(F):
            q[f, p, 0], q[f, p, 1] = swap_32(half[f, 0], half[f, 1], lane)
            q[f, p, 2], q[f, p, 3] = swap_32(half[f, 2], half[f, 3], lane)
        turn_first(p)
        return 0

    turn_first(0)
    lax.fori_loop(1, B + 5, turn, 0)

    @pl.when(gx == 0)
    def _():
        for f in range(F):
            q[f, 1] = q[f, 3]
            q[f, 2] = q[f, 3]

    @pl.when(gx == last_x)
    def _():
        for f in range(F):
            q[f, B + 3] = q[f, B + 2]
            q[f, B + 4] = q[f, B + 2]

    for block in range(4):
        z0 = 8 * block
        span, rows = slice(z0, z0 + 8), slice(z0 + 8, z0 + 16)
        layer = lambda f, j, s: q[f, z0 + 3 : z0 + 11, j, s, :]

        def low(f):
            q0 = layer(f, 0, 0)
            first = gy == 0
            return (
                jnp.where(first, q0, y_below[f, 0, span, :]),
                jnp.where(first, q0, y_below[f, 1, span, :]),
                q0,
                layer(f, 1, 0),
            )

        def high(f):
            q31 = layer(f, 3, 7)
            end = gy == last_y
            return (
                q31,
                jnp.where(end, q31, y_above[f, 0, span, :]),
                jnp.where(end, q31, y_above[f, 1, span, :]),
            )

        _, v1, v0, _ = low(1)
        weight = 0.0625 * (v1 + v0)
        _, v1, v0, _ = low(5)
        cond = conduction(v1) + conduction(v0)
        right_c[rows, :] = conduction(high(5)[1])
        for f in range(F):
            qm2, qm1, q0, q1 = low(f)
            d = q0 - qm1
            p = (qm1 + qm1) + minmod(qm1 - qm2, d)
            m = (q0 + q0) - minmod(d, q1 - q0)
            left_d[f, rows, :] = d
            left_n[f, rows, :] = (scale[f] * cond) * d - weight * jnp.where(weight > 0.0, p, m)
            q31, q32, q33 = high(f)
            right_q[f, rows, :] = q32
            right_m[f, rows, :] = (q32 + q32) - minmod(q32 - q31, q33 - q32)

    def y_next(value, row):
        return pltpu.roll(jnp.where(sub == 0, row, value), 7, 0)

    def y_last(value, row):
        return pltpu.roll(jnp.where(sub == 7, row, value), 1, 0)

    def x_next(value, ends):
        return jnp.where(lane == 127, ends, pltpu.roll(value, 127, 1))

    def x_last(value, ends):
        return jnp.where(lane == 0, ends, pltpu.roll(value, 1, 1))

    def plane(i, _):
        for f in range(F):
            for j in (0, 2):
                result[j, f, i], result[j + 1, f, i] = swap_32(turned[f, j], turned[f, j + 1], lane)
        for f in range(F):
            for j in (0, 1):
                turned[f, j], turned[f, j + 2] = swap_64(done[f, j], done[f, j + 2], lane)

        row = pl.ds(i + 5, 1)
        here = [carry_c[j] for j in J]
        above = [conduction(q[5, i + 1, j]) for j in J]
        cond_z = [a + b for a, b in zip(here, above)]
        for j in J:
            carry_c[j] = above[j]
        beyond = here[1:] + [y_next(here[0], right_c[row, :])]
        cond_y = [a + b for a, b in zip(here, beyond)]
        v = [q[1, i, j] for j in J]
        beyond = v[1:] + [y_next(v[0], right_q[1, row, :])]
        weight_y = [0.0625 * (a + b) for a, b in zip(v, beyond)]
        weight_z = [0.0625 * (q[2, i, j] + q[2, i + 1, j]) for j in J]
        edge_x = [-0.125 * q[0, i, j] for j in J]
        for f in range(F):
            value = [q[f, i, j] for j in J]
            twice = [a + a for a in value]
            total = []
            for j in J:
                after = q[f, i + 1, j]
                d = after - value[j]
                slope = minmod(d, q[f, i + 2, j] - after)
                double = after + after
                state = jnp.where(weight_z[j] > 0.0, carry_p[f, j], double - slope)
                carry_p[f, j] = double + slope
                net = (scale[f] * cond_z[j]) * d - weight_z[j] * state
                total.append(value[j] + (net - carry_n[f, j]))
                carry_n[f, j] = net
            beyond = value[1:] + [y_next(value[0], right_q[f, row, :])]
            d = [b - a for a, b in zip(value, beyond)]
            before = [y_last(d[3], left_d[f, row, :])] + d[:3]
            slope = [minmod(a, b) for a, b in zip(before, d)]
            right = [a - b for a, b in zip(twice, slope)]
            right = right[1:] + [y_next(right[0], right_m[f, row, :])]
            net = []
            for j in J:
                state = jnp.where(weight_y[j] > 0.0, twice[j] + slope[j], right[j])
                net.append((scale[f] * cond_y[j]) * d[j] - weight_y[j] * state)
            before = [y_last(net[3], left_n[f, row, :])] + net[:3]
            for j in J:
                n = nx[f, j]
                t = total[j] + (net[j] - before[j])
                done[f, j] = t + (n - x_last(n, edge_x[j] * twice[j]))
        for j in J:
            u = q[0, i + 1, j]
            weight = 0.0625 * ((u + u) + dx_old[0, j])
            cond = cx_old[j]
            for f in range(F):
                a = q[f, i + 1, j]
                state = jnp.where(weight > 0.0, px[f, j], x_next(mx[f, j], a + a))
                nx[f, j] = (scale[f] * cond) * dx_old[f, j] - weight * state
        for j in J:
            cx_old[j] = cx[j]
            for f in range(F):
                a, d = q[f, i + 2, j], dx[f, j]
                slope = minmod(x_last(d, 0.0), d)
                px[f, j], mx[f, j] = (a + a) + slope, (a + a) - slope
                dx_old[f, j] = d
        for j in J:
            c = conduction(q[5, i + 3, j])
            cx[j] = c + x_next(c, c)
            for f in range(F):
                a = q[f, i + 3, j]
                dx[f, j] = x_next(a, a) - a
        return 0

    lax.fori_loop(0, B + LEAD, plane, 0)
    run_all(
        [
            pltpu.make_async_copy(result.at[c, :, LEAD:], out.at[:, :, :, c, 0], sem_out.at[c])
            for c in range(CAP)
        ]
    )


def step(owner, spread, x, up, down, z_below, z_above, y_below, y_above):
    planes = lambda *lead: pltpu.VMEM((*lead, ROWS, LANES), F32)
    rows = pltpu.VMEM((F, B + 16, LANES), F32)
    return pl.pallas_call(
        step_body,
        name="step",
        out_shape=jax.ShapeDtypeStruct((F, B, ROWS, CAP, 1, LANES), F32),
        in_specs=[SMEM, SMEM, HBM, HBM, HBM, HBM, HBM, VMEM, VMEM],
        out_specs=HBM,
        scratch_shapes=[
            planes(CAP, F, B + 5),
            planes(F, B + 8, 4),
            planes(CAP, F, B + LEAD),
            rows,
            rows,
            rows,
            rows,
            pltpu.VMEM((B + 16, LANES), F32),
            planes(F, 4),
            planes(F, 4),
            planes(4),
            planes(F, 4),
            planes(F, 4),
            planes(F, 4),
            planes(4),
            planes(4),
            planes(F, 4),
            planes(F, 4),
            planes(F, 4),
            planes(F, 4),
            planes(F, 4),
            pltpu.SemaphoreType.DMA((CAP,)),
            pltpu.SemaphoreType.DMA((2,)),
            pltpu.SemaphoreType.DMA((CAP,)),
        ],
        compiler_params=pltpu.CompilerParams(vmem_limit_bytes=WIDE),
    )(owner, spread, x, up, down, z_below, z_above, y_below, y_above)


def along_curve(block, distance):
    count = lax.axis_size(AXES)
    return lax.ppermute(block, AXES, [(i, (i + distance) % count) for i in range(count)])


def along_axis(block, axis, distance):
    count = lax.axis_size(axis)
    pairs = [(i, i + distance) for i in range(count) if 0 <= i + distance < count]
    return lax.ppermute(block, axis, pairs)


def local(old_state, old_owner, old_slot, diffusivity):
    x = old_state.reshape(8, F, B, ROWS, LANES).transpose(1, 2, 3, 0, 4)[..., None, :]
    up, down = pack(x)
    up = along_curve(up, 1)[..., None, :]
    down = along_curve(down, -1)[..., None, :]
    z_low, z_high, y_low, y_high = edges(old_owner, x, up, down)
    z_below = along_axis(z_high, "gx", 1)
    z_above = along_axis(z_low, "gx", -1)
    y_below = along_axis(y_high, "gy", 1)
    y_above = along_axis(y_low, "gy", -1)
    out = step(old_owner, diffusivity, x, up, down, z_below, z_above, y_below, y_above)
    return out[..., 0, :].transpose(3, 0, 1, 2, 4).reshape(CAP, F, B * B * B)


def solution(mesh):
    placed = (P(AXES, None, None), P(), P(), P())
    return jax.shard_map(
        local, mesh=mesh, in_specs=placed, out_specs=P(AXES, None, None), check_vma=False
    )
```

```python
import jax
import jax.numpy as jnp
from jax import lax
from jax.experimental import pallas as pl
from jax.experimental.pallas import tpu as pltpu
from jax.sharding import PartitionSpec as P

B = 32
F = 6
CAP = 4
ROWS = 8
LANES = 128
AXES = ("gx", "gy")
F32 = jnp.float32
HBM = pl.BlockSpec(memory_space=pl.ANY)
VMEM = pl.BlockSpec(memory_space=pltpu.VMEM)
SMEM = pl.BlockSpec(memory_space=pltpu.SMEM)
WIDE = 56 << 20


def run_all(copies):
    for copy in copies:
        copy.start()
    for copy in copies:
        copy.wait()


def shell_body(x, up, down, first, last, sem, sem_y):
    waits, waits_y = [], []
    for k in range(4):
        target, slot = (up, 6 + k) if k < 2 else (down, k - 2)
        shell = target.at[k % 2]
        waits_y.append(pltpu.make_async_copy(x.at[:, :, 0, slot, 0], first.at[k], sem_y.at[k]))
        waits_y.append(pltpu.make_async_copy(x.at[:, :, 7, slot, 0], last.at[k], sem_y.at[4 + k]))
        waits.append(pltpu.make_async_copy(x.at[:, 0:2, :, slot, 0], shell.at[:, 0:2], sem.at[k]))
        waits.append(
            pltpu.make_async_copy(x.at[:, 30:32, :, slot, 0], shell.at[:, 2:4], sem.at[4 + k])
        )
    for copy in waits_y + waits:
        copy.start()
    for copy in waits_y:
        copy.wait()
    left = lax.broadcasted_iota(jnp.int32, (8, LANES), 1) < 64
    for k in range(4):
        target = up if k < 2 else down
        for f in range(F):
            for b in range(4):
                span = slice(8 * b, 8 * b + 8)
                target[k % 2, f, 4 + b] = jnp.where(left, first[k, f, span, :], last[k, f, span, :])
    for copy in waits:
        copy.wait()


def inner_body(x, up, down, sem):
    copies = []
    for j in range(2):
        copies.append(pltpu.make_async_copy(x.at[:, 2:30, :, 6 + j, 0], up.at[j], sem.at[j]))
        copies.append(pltpu.make_async_copy(x.at[:, 2:30, :, j, 0], down.at[j], sem.at[2 + j]))
    run_all(copies)


def hold_body(x, hold, sem):
    run_all(
        [pltpu.make_async_copy(x.at[:, :, :, 2 + c, 0], hold.at[c], sem.at[c]) for c in range(CAP)]
    )


def from_slots(body, name, x, shapes, scratch, micros):
    shapes = tuple(jax.ShapeDtypeStruct(shape, F32) for shape in shapes)
    return pl.pallas_call(
        body,
        name=name,
        out_shape=shapes,
        in_specs=[HBM],
        out_specs=(VMEM,) * len(shapes),
        scratch_shapes=scratch,
        compiler_params=pltpu.CompilerParams(vmem_limit_bytes=WIDE),
        cost_estimate=pl.CostEstimate(flops=0, bytes_accessed=micros * 3000000, transcendentals=0),
    )(x)


def shell(x):
    rows = pltpu.VMEM((4, F, B, LANES), F32)
    sems = pltpu.SemaphoreType.DMA((8,))
    return from_slots(shell_body, "shell", x, [(2, F, 8, ROWS, LANES)] * 2, [rows, rows, sems, sems], 2)


def inner(x):
    sems = pltpu.SemaphoreType.DMA((4,))
    return from_slots(inner_body, "inner", x, [(2, F, 28, ROWS, LANES)] * 2, [sems], 3)


def held(x):
    sems = pltpu.SemaphoreType.DMA((4,))
    return from_slots(hold_body, "held", x, [(CAP, F, B, ROWS, LANES)], [sems], 4)[0]


def device_number():
    return lax.axis_index("gx") * lax.axis_size("gy") + lax.axis_index("gy")


def kept_flags(owner):
    device = device_number()
    return [owner[device * CAP + c] == device for c in range(CAP)]


def swap_64(a, b, lane):
    low = lane < 64
    m = pltpu.roll(jnp.where(low, b, a), 64, 1)
    return jnp.where(low, a, m), jnp.where(low, m, b)


def swap_32(a, b, lane):
    even = (lane & 32) == 0
    m = jnp.where(even, b, a)
    return jnp.where(even, a, pltpu.roll(m, 32, 1)), jnp.where(even, pltpu.roll(m, 96, 1), b)


def turned_to_layers(v, lane):
    a, c = swap_64(v[0], v[2], lane)
    b, d = swap_64(v[1], v[3], lane)
    return *swap_32(a, b, lane), *swap_32(c, d, lane)


def edges_body(owner, hold, up, down, z_low, z_high, y_low, y_high):
    kept = kept_flags(owner)
    moved = [(up if c < 2 else down).at[c % 2] for c in range(CAP)]
    lane = lax.broadcasted_iota(jnp.int32, (8, LANES), 1)
    for f in range(F):
        for k, z in enumerate((0, 1, 30, 31)):
            v = [jnp.where(kept[c], hold[c, f, z], moved[c][f, k]) for c in range(CAP)]
            target = (z_low if k < 2 else z_high).at[f, k % 2]
            for j, value in enumerate(turned_to_layers(v, lane)):
                target[j] = value
        for b in range(4):
            span = slice(8 * b, 8 * b + 8)
            rows = []
            for c in range(CAP):
                here = jnp.where(lane < 64, hold[c, f, span, 0, :], hold[c, f, span, 7, :])
                rows.append(jnp.where(kept[c], here, moved[c][f, 4 + b]))
            for j, value in enumerate(turned_to_layers(rows, lane)):
                (y_low if j < 2 else y_high)[f, j % 2, span, :] = value


def edges(owner, hold, up, down):
    z_shape = jax.ShapeDtypeStruct((F, 2, 4, ROWS, LANES), F32)
    y_shape = jax.ShapeDtypeStruct((F, 2, B, LANES), F32)
    return pl.pallas_call(
        edges_body,
        name="edges",
        out_shape=(z_shape, z_shape, y_shape, y_shape),
        in_specs=[SMEM, VMEM, VMEM, VMEM],
        out_specs=(VMEM, VMEM, VMEM, VMEM),
        compiler_params=pltpu.CompilerParams(vmem_limit_bytes=16 << 20),
        cost_estimate=pl.CostEstimate(flops=0, bytes_accessed=6000000, transcendentals=0),
    )(owner, hold, up, down)


def minmod(a, b):
    return jnp.maximum(jnp.minimum(a, b), jnp.minimum(jnp.maximum(a, b), 0.0))


def conduction(v):
    return jnp.exp(0.5 * jnp.tanh(v))


LEAD = 5
J = range(4)


def step_body(
    owner, spread, hold, shell_up, shell_down, up, down, z_below, z_above, y_below, y_above, out,
    q, result, left_d, left_n, right_q, right_m, right_c, carry_p, carry_n, carry_c,
    half, dx, dx_old, cx, cx_old, px, mx, nx, done, turned, sem_out,
):
    kept = kept_flags(owner)
    gx, gy = lax.axis_index("gx"), lax.axis_index("gy")
    last_x, last_y = lax.axis_size("gx") - 1, lax.axis_size("gy") - 1
    lane = lax.broadcasted_iota(jnp.int32, (8, LANES), 1)
    sub = lax.broadcasted_iota(jnp.int32, (8, LANES), 0)
    scale = [0.5 * spread[f] for f in range(F)]

    moved = [(up if c < 2 else down).at[c % 2] for c in range(CAP)]
    shells = [(shell_up if c < 2 else shell_down).at[c % 2] for c in range(CAP)]

    def turn_first(k, z):
        for f in range(F):
            v = [jnp.where(kept[c], hold[c, f, z], moved[c][f, z - 2]) for c in range(CAP)]
            half[k, f, 0], half[k, f, 2] = swap_64(v[0], v[2], lane)
            half[k, f, 1], half[k, f, 3] = swap_64(v[1], v[3], lane)

    def turn_last(k, z):
        for f in range(F):
            q[f, z + 3, 0], q[f, z + 3, 1] = swap_32(half[k, f, 0], half[k, f, 1], lane)
            q[f, z + 3, 2], q[f, z + 3, 3] = swap_32(half[k, f, 2], half[k, f, 3], lane)

    def turn(i, _):
        for k in range(4):
            turn_last(k, 4 * i - 2 + k)
        for k in range(4):
            turn_first(k, 4 * i + 2 + k)
        return 0

    for k in range(4):
        turn_first(k, 2 + k)
    lax.fori_loop(1, 7, turn, 0)
    for k in range(4):
        turn_last(k, 26 + k)
    for f in range(F):
        for k, z in enumerate((0, 1, 30, 31)):
            v = [jnp.where(kept[c], hold[c, f, z], shells[c][f, k]) for c in range(CAP)]
            for j, value in enumerate(turned_to_layers(v, lane)):
                q[f, z + 3, j] = value
    for f in range(F):
        for j in J:
            for k in range(2):
                q[f, 1 + k, j] = jnp.where(gx == 0, q[f, 3, j], z_below[f, k, j])
                q[f, B + 3 + k, j] = jnp.where(gx == last_x, q[f, B + 2, j], z_above[f, k, j])

    for block in range(4):
        z0 = 8 * block
        span, rows = slice(z0, z0 + 8), slice(z0 + 8, z0 + 16)
        layer = lambda f, j, s: q[f, z0 + 3 : z0 + 11, j, s, :]

        def low(f):
            q0 = layer(f, 0, 0)
            first = gy == 0
            return (
                jnp.where(first, q0, y_below[f, 0, span, :]),
                jnp.where(first, q0, y_below[f, 1, span, :]),
                q0,
                layer(f, 1, 0),
            )

        def high(f):
            q31 = layer(f, 3, 7)
            end = gy == last_y
            return (
                q31,
                jnp.where(end, q31, y_above[f, 0, span, :]),
                jnp.where(end, q31, y_above[f, 1, span, :]),
            )

        _, v1, v0, _ = low(1)
        weight = 0.0625 * (v1 + v0)
        _, v1, v0, _ = low(5)
        cond = conduction(v1) + conduction(v0)
        right_c[rows, :] = conduction(high(5)[1])
        for f in range(F):
            qm2, qm1, q0, q1 = low(f)
            d = q0 - qm1
            p = (qm1 + qm1) + minmod(qm1 - qm2, d)
            m = (q0 + q0) - minmod(d, q1 - q0)
            left_d[f, rows, :] = d
            left_n[f, rows, :] = (scale[f] * cond) * d - weight * jnp.where(weight > 0.0, p, m)
            q31, q32, q33 = high(f)
            right_q[f, rows, :] = q32
            right_m[f, rows, :] = (q32 + q32) - minmod(q32 - q31, q33 - q32)

    def y_next(value, row):
        return pltpu.roll(jnp.where(sub == 0, row, value), 7, 0)

    def y_last(value, row):
        return pltpu.roll(jnp.where(sub == 7, row, value), 1, 0)

    def x_next(value, ends):
        return jnp.where(lane == 127, ends, pltpu.roll(value, 127, 1))

    def x_last(value, ends):
        return jnp.where(lane == 0, ends, pltpu.roll(value, 1, 1))

    def plane(i, _):
        for f in range(F):
            for j in (0, 2):
                result[j, f, i], result[j + 1, f, i] = swap_32(turned[f, j], turned[f, j + 1], lane)
        for f in range(F):
            for j in (0, 1):
                turned[f, j], turned[f, j + 2] = swap_64(done[f, j], done[f, j + 2], lane)

        row = pl.ds(i + 5, 1)
        here = [carry_c[j] for j in J]
        above = [conduction(q[5, i + 1, j]) for j in J]
        cond_z = [a + b for a, b in zip(here, above)]
        for j in J:
            carry_c[j] = above[j]
        beyond = here[1:] + [y_next(here[0], right_c[row, :])]
        cond_y = [a + b for a, b in zip(here, beyond)]
        v = [q[1, i, j] for j in J]
        beyond = v[1:] + [y_next(v[0], right_q[1, row, :])]
        weight_y = [0.0625 * (a + b) for a, b in zip(v, beyond)]
        weight_z = [0.0625 * (q[2, i, j] + q[2, i + 1, j]) for j in J]
        edge_x = [-0.125 * q[0, i, j] for j in J]
        for f in range(F):
            value = [q[f, i, j] for j in J]
            twice = [a + a for a in value]
            total = []
            for j in J:
                after = q[f, i + 1, j]
                d = after - value[j]
                slope = minmod(d, q[f, i + 2, j] - after)
                double = after + after
                state = jnp.where(weight_z[j] > 0.0, carry_p[f, j], double - slope)
                carry_p[f, j] = double + slope
                net = (scale[f] * cond_z[j]) * d - weight_z[j] * state
                total.append(value[j] + (net - carry_n[f, j]))
                carry_n[f, j] = net
            beyond = value[1:] + [y_next(value[0], right_q[f, row, :])]
            d = [b - a for a, b in zip(value, beyond)]
            before = [y_last(d[3], left_d[f, row, :])] + d[:3]
            slope = [minmod(a, b) for a, b in zip(before, d)]
            right = [a - b for a, b in zip(twice, slope)]
            right = right[1:] + [y_next(right[0], right_m[f, row, :])]
            net = []
            for j in J:
                state = jnp.where(weight_y[j] > 0.0, twice[j] + slope[j], right[j])
                net.append((scale[f] * cond_y[j]) * d[j] - weight_y[j] * state)
            before = [y_last(net[3], left_n[f, row, :])] + net[:3]
            for j in J:
                n = nx[f, j]
                t = total[j] + (net[j] - before[j])
                done[f, j] = t + (n - x_last(n, edge_x[j] * twice[j]))
        for j in J:
            u = q[0, i + 1, j]
            weight = 0.0625 * ((u + u) + dx_old[0, j])
            cond = cx_old[j]
            for f in range(F):
                a = q[f, i + 1, j]
                state = jnp.where(weight > 0.0, px[f, j], x_next(mx[f, j], a + a))
                nx[f, j] = (scale[f] * cond) * dx_old[f, j] - weight * state
        for j in J:
            cx_old[j] = cx[j]
            for f in range(F):
                a, d = q[f, i + 2, j], dx[f, j]
                slope = minmod(x_last(d, 0.0), d)
                px[f, j], mx[f, j] = (a + a) + slope, (a + a) - slope
                dx_old[f, j] = d
        for j in J:
            c = conduction(q[5, i + 3, j])
            cx[j] = c + x_next(c, c)
            for f in range(F):
                a = q[f, i + 3, j]
                dx[f, j] = x_next(a, a) - a
        return 0

    lax.fori_loop(0, B + LEAD, plane, 0)
    run_all(
        [
            pltpu.make_async_copy(result.at[c, :, LEAD:], out.at[:, :, :, c, 0], sem_out.at[c])
            for c in range(CAP)
        ]
    )


def step(owner, spread, *arrays):
    planes = lambda *lead: pltpu.VMEM((*lead, ROWS, LANES), F32)
    rows = pltpu.VMEM((F, B + 16, LANES), F32)
    return pl.pallas_call(
        step_body,
        name="step",
        out_shape=jax.ShapeDtypeStruct((F, B, ROWS, CAP, 1, LANES), F32),
        in_specs=[SMEM, SMEM] + [VMEM] * len(arrays),
        out_specs=HBM,
        scratch_shapes=[
            planes(F, B + 8, 4),
            planes(CAP, F, B + LEAD),
            rows,
            rows,
            rows,
            rows,
            pltpu.VMEM((B + 16, LANES), F32),
            planes(F, 4),
            planes(F, 4),
            planes(4),
            planes(4, F, 4),
            planes(F, 4),
            planes(F, 4),
            planes(4),
            planes(4),
            planes(F, 4),
            planes(F, 4),
            planes(F, 4),
            planes(F, 4),
            planes(F, 4),
            pltpu.SemaphoreType.DMA((CAP,)),
        ],
        compiler_params=pltpu.CompilerParams(vmem_limit_bytes=24 << 20),
        cost_estimate=pl.CostEstimate(flops=0, bytes_accessed=40000000, transcendentals=0),
    )(owner, spread, *arrays)


def along_curve(block, distance):
    count = lax.axis_size(AXES)
    return lax.ppermute(block, AXES, [(i, (i + distance) % count) for i in range(count)])


def along_axis(block, axis, distance):
    count = lax.axis_size(axis)
    pairs = [(i, i + distance) for i in range(count) if 0 <= i + distance < count]
    return lax.ppermute(block, axis, pairs)


def local(old_state, old_owner, old_slot, diffusivity):
    x = old_state.reshape(8, F, B, ROWS, LANES).transpose(1, 2, 3, 0, 4)[..., None, :]
    shell_up, shell_down = shell(x)
    up, down = inner(x)
    shell_up = along_curve(shell_up, 1)
    up = along_curve(up, 1)
    shell_down = along_curve(shell_down, -1)
    down = along_curve(down, -1)
    hold = held(x)
    z_low, z_high, y_low, y_high = edges(old_owner, hold, shell_up, shell_down)
    y_below = along_axis(y_high, "gy", 1)
    y_above = along_axis(y_low, "gy", -1)
    z_below = along_axis(z_high, "gx", 1)
    z_above = along_axis(z_low, "gx", -1)
    out = step(
        old_owner, diffusivity, hold, shell_up, shell_down, up, down, z_below, z_above, y_below, y_above
    )
    return out[..., 0, :].transpose(3, 0, 1, 2, 4).reshape(CAP, F, B * B * B)


def solution(mesh):
    placed = (P(AXES, None, None), P(), P(), P())
    return jax.shard_map(
        local, mesh=mesh, in_specs=placed, out_specs=P(AXES, None, None), check_vma=False
    )
```

```python
import jax
import jax.numpy as jnp
from jax import lax
from jax.experimental import pallas as pl
from jax.experimental.pallas import tpu as pltpu
from jax.sharding import PartitionSpec as P

B = 32
F = 6
CAP = 4
ROWS = 8
LANES = 128
AXES = ("gx", "gy")
F32 = jnp.float32
HBM = pl.BlockSpec(memory_space=pl.ANY)
VMEM = pl.BlockSpec(memory_space=pltpu.VMEM)
SMEM = pl.BlockSpec(memory_space=pltpu.SMEM)
WIDE = 56 << 20


def run_all(copies):
    for copy in copies:
        copy.start()
    for copy in copies:
        copy.wait()


def odd(axis):
    return lax.axis_index(axis) % 2 == 1


def leave_body(near, x, leaving, sem):
    first = jnp.where(odd("gy"), 0, 6) if near else jnp.where(odd("gy"), 6, 0)
    run_all(
        [
            pltpu.make_async_copy(x.at[:, :, :, first + j, 0], leaving.at[j], sem.at[j])
            for j in range(2)
        ]
    )


def leave_far(x, leaving, sem):
    leave_body(False, x, leaving, sem)


def leave_near(x, after, leaving, sem):
    leave_body(True, x, leaving, sem)


def hold_body(x, after, hold, rim, sem):
    run_all(
        [pltpu.make_async_copy(x.at[:, :, :, 2 + c, 0], hold.at[c], sem.at[c]) for c in range(CAP)]
    )
    left = lax.broadcasted_iota(jnp.int32, (8, LANES), 1) < 64
    for c in range(CAP):
        for f in range(F):
            for k, z in enumerate((0, 1, 30, 31)):
                rim[c, f, k] = hold[c, f, z]
            for b in range(4):
                span = slice(8 * b, 8 * b + 8)
                rim[c, f, 4 + b] = jnp.where(left, hold[c, f, span, 0, :], hold[c, f, span, 7, :])


def from_slots(body, name, arrays, shapes, scratch, micros):
    shapes = tuple(jax.ShapeDtypeStruct(shape, F32) for shape in shapes)
    return pl.pallas_call(
        body,
        name=name,
        out_shape=shapes,
        in_specs=[HBM] * len(arrays),
        out_specs=(VMEM,) * len(shapes),
        scratch_shapes=scratch,
        compiler_params=pltpu.CompilerParams(vmem_limit_bytes=WIDE),
        cost_estimate=pl.CostEstimate(flops=0, bytes_accessed=1000, transcendentals=0),
    )(*arrays)


def far_boxes(x):
    sems = pltpu.SemaphoreType.DMA((2,))
    return from_slots(leave_far, "far", [x], [(2, F, B, ROWS, LANES)], [sems], 2)[0]


def near_boxes(x, after):
    sems = pltpu.SemaphoreType.DMA((2,))
    return from_slots(leave_near, "near", [x, after], [(2, F, B, ROWS, LANES)], [sems], 2)[0]


def held(x, after):
    sems = pltpu.SemaphoreType.DMA((4,))
    shapes = [(CAP, F, B, ROWS, LANES), (CAP, F, 8, ROWS, LANES)]
    return from_slots(hold_body, "held", [x, after], shapes, [sems], 4)


def device_number():
    return lax.axis_index("gx") * lax.axis_size("gy") + lax.axis_index("gy")


def kept_flags(owner):
    device = device_number()
    return [owner[device * CAP + c] == device for c in range(CAP)]


def arrived(kept, here, c, far, near):
    from_far = odd("gy") if c >= 2 else jnp.logical_not(odd("gy"))
    return jnp.where(kept, here, jnp.where(from_far, far, near))


def swap_64(a, b, lane):
    low = lane < 64
    m = pltpu.roll(jnp.where(low, b, a), 64, 1)
    return jnp.where(low, a, m), jnp.where(low, m, b)


def swap_32(a, b, lane):
    even = (lane & 32) == 0
    m = jnp.where(even, b, a)
    return jnp.where(even, a, pltpu.roll(m, 32, 1)), jnp.where(even, pltpu.roll(m, 96, 1), b)


def turned_to_layers(v, lane):
    a, c = swap_64(v[0], v[2], lane)
    b, d = swap_64(v[1], v[3], lane)
    return *swap_32(a, b, lane), *swap_32(c, d, lane)


def edges_body(owner, rim, far, near, z_pair, z_cross, y_near, y_far):
    kept = kept_flags(owner)
    lane = lax.broadcasted_iota(jnp.int32, (8, LANES), 1)
    odd_z, odd_y = odd("gx"), odd("gy")

    def strip(ref, j, f, span):
        return jnp.where(lane < 64, ref[j, f, span, 0, :], ref[j, f, span, 7, :])

    for f in range(F):
        z_layers = []
        for k, z in enumerate((0, 1, 30, 31)):
            v = [
                arrived(kept[c], rim[c, f, k], c, far[c % 2, f, z], near[c % 2, f, z])
                for c in range(CAP)
            ]
            z_layers.append(turned_to_layers(v, lane))
        for k in range(2):
            for j in range(4):
                low, high = z_layers[k][j], z_layers[2 + k][j]
                z_pair[f, k, j] = jnp.where(odd_z, low, high)
                z_cross[f, k, j] = jnp.where(odd_z, high, low)
        for b in range(4):
            span = slice(8 * b, 8 * b + 8)
            v = [
                arrived(
                    kept[c], rim[c, f, 4 + b], c, strip(far, c % 2, f, span), strip(near, c % 2, f, span)
                )
                for c in range(CAP)
            ]
            layers = turned_to_layers(v, lane)
            for k in range(2):
                low, high = layers[k], layers[2 + k]
                y_near[f, k, span, :] = jnp.where(odd_y, low, high)
                y_far[f, k, span, :] = jnp.where(odd_y, high, low)


def edges(owner, rim, far, near):
    z_shape = jax.ShapeDtypeStruct((F, 2, 4, ROWS, LANES), F32)
    y_shape = jax.ShapeDtypeStruct((F, 2, B, LANES), F32)
    return pl.pallas_call(
        edges_body,
        name="edges",
        out_shape=(z_shape, z_shape, y_shape, y_shape),
        in_specs=[SMEM, VMEM, VMEM, VMEM],
        out_specs=(VMEM, VMEM, VMEM, VMEM),
        compiler_params=pltpu.CompilerParams(vmem_limit_bytes=16 << 20),
        cost_estimate=pl.CostEstimate(flops=0, bytes_accessed=6000000, transcendentals=0),
    )(owner, rim, far, near)


def minmod(a, b):
    return jnp.maximum(jnp.minimum(a, b), jnp.minimum(jnp.maximum(a, b), 0.0))


def conduction(v):
    return jnp.exp(0.5 * jnp.tanh(v))


LEAD = 5
J = range(4)


def step_body(
    owner, spread, hold, far, near, z_pair, z_cross, y_near, y_far, out,
    q, result, left_d, left_n, right_q, right_m, right_c, carry_p, carry_n, carry_c,
    half, dx, dx_old, cx, cx_old, px, mx, nx, done, turned, sem_out,
):
    kept = kept_flags(owner)
    gx, gy = lax.axis_index("gx"), lax.axis_index("gy")
    last_x, last_y = lax.axis_size("gx") - 1, lax.axis_size("gy") - 1
    lane = lax.broadcasted_iota(jnp.int32, (8, LANES), 1)
    sub = lax.broadcasted_iota(jnp.int32, (8, LANES), 0)
    scale = [0.5 * spread[f] for f in range(F)]

    odd_z, odd_y = odd("gx"), odd("gy")

    def turn_first(k, z):
        for f in range(F):
            v = [
                arrived(kept[c], hold[c, f, z], c, far[c % 2, f, z], near[c % 2, f, z])
                for c in range(CAP)
            ]
            half[k, f, 0], half[k, f, 2] = swap_64(v[0], v[2], lane)
            half[k, f, 1], half[k, f, 3] = swap_64(v[1], v[3], lane)

    def turn_last(k, z):
        for f in range(F):
            q[f, z + 3, 0], q[f, z + 3, 1] = swap_32(half[k, f, 0], half[k, f, 1], lane)
            q[f, z + 3, 2], q[f, z + 3, 3] = swap_32(half[k, f, 2], half[k, f, 3], lane)

    def turn(i, _):
        for k in range(4):
            turn_last(k, 4 * i - 4 + k)
        for k in range(4):
            turn_first(k, 4 * i + k)
        return 0

    for k in range(4):
        turn_first(k, k)
    lax.fori_loop(1, 8, turn, 0)
    for k in range(4):
        turn_last(k, 28 + k)
    for f in range(F):
        for j in J:
            for k in range(2):
                q[f, 1 + k, j] = jnp.where(
                    gx == 0, q[f, 3, j], jnp.where(odd_z, z_pair[f, k, j], z_cross[f, k, j])
                )
                q[f, B + 3 + k, j] = jnp.where(
                    gx == last_x, q[f, B + 2, j], jnp.where(odd_z, z_cross[f, k, j], z_pair[f, k, j])
                )

    def below(f, k, span):
        return jnp.where(odd_y, y_near[f, k, span, :], y_far[f, k, span, :])

    def above(f, k, span):
        return jnp.where(odd_y, y_far[f, k, span, :], y_near[f, k, span, :])

    for block in range(4):
        z0 = 8 * block
        span, rows = slice(z0, z0 + 8), slice(z0 + 8, z0 + 16)
        layer = lambda f, j, s: q[f, z0 + 3 : z0 + 11, j, s, :]

        def low(f):
            q0 = layer(f, 0, 0)
            first = gy == 0
            return (
                jnp.where(first, q0, below(f, 0, span)),
                jnp.where(first, q0, below(f, 1, span)),
                q0,
                layer(f, 1, 0),
            )

        def high(f):
            q31 = layer(f, 3, 7)
            end = gy == last_y
            return (
                q31,
                jnp.where(end, q31, above(f, 0, span)),
                jnp.where(end, q31, above(f, 1, span)),
            )

        _, v1, v0, _ = low(1)
        weight = 0.0625 * (v1 + v0)
        _, v1, v0, _ = low(5)
        cond = conduction(v1) + conduction(v0)
        right_c[rows, :] = conduction(high(5)[1])
        for f in range(F):
            qm2, qm1, q0, q1 = low(f)
            d = q0 - qm1
            p = (qm1 + qm1) + minmod(qm1 - qm2, d)
            m = (q0 + q0) - minmod(d, q1 - q0)
            left_d[f, rows, :] = d
            left_n[f, rows, :] = (scale[f] * cond) * d - weight * jnp.where(weight > 0.0, p, m)
            q31, q32, q33 = high(f)
            right_q[f, rows, :] = q32
            right_m[f, rows, :] = (q32 + q32) - minmod(q32 - q31, q33 - q32)

    def y_next(value, row):
        return pltpu.roll(jnp.where(sub == 0, row, value), 7, 0)

    def y_last(value, row):
        return pltpu.roll(jnp.where(sub == 7, row, value), 1, 0)

    def x_next(value, ends):
        return jnp.where(lane == 127, ends, pltpu.roll(value, 127, 1))

    def x_last(value, ends):
        return jnp.where(lane == 0, ends, pltpu.roll(value, 1, 1))

    def leaving(k):
        z = 8 * k
        return [
            pltpu.make_async_copy(
                result.at[c, :, pl.ds(z + LEAD, 8)], out.at[:, pl.ds(z, 8), :, c, 0], sem_out.at[k, c]
            )
            for c in range(CAP)
        ]

    def plane(i, _):
        for f in range(F):
            for j in (0, 2):
                result[j, f, i], result[j + 1, f, i] = swap_32(turned[f, j], turned[f, j + 1], lane)
        for f in range(F):
            for j in (0, 1):
                turned[f, j], turned[f, j + 2] = swap_64(done[f, j], done[f, j + 2], lane)

        row = pl.ds(i + 5, 1)
        here = [carry_c[j] for j in J]
        above = [conduction(q[5, i + 1, j]) for j in J]
        cond_z = [a + b for a, b in zip(here, above)]
        for j in J:
            carry_c[j] = above[j]
        beyond = here[1:] + [y_next(here[0], right_c[row, :])]
        cond_y = [a + b for a, b in zip(here, beyond)]
        v = [q[1, i, j] for j in J]
        beyond = v[1:] + [y_next(v[0], right_q[1, row, :])]
        weight_y = [0.0625 * (a + b) for a, b in zip(v, beyond)]
        weight_z = [0.0625 * (q[2, i, j] + q[2, i + 1, j]) for j in J]
        edge_x = [-0.125 * q[0, i, j] for j in J]
        for f in range(F):
            value = [q[f, i, j] for j in J]
            twice = [a + a for a in value]
            total = []
            for j in J:
                after = q[f, i + 1, j]
                d = after - value[j]
                slope = minmod(d, q[f, i + 2, j] - after)
                double = after + after
                state = jnp.where(weight_z[j] > 0.0, carry_p[f, j], double - slope)
                carry_p[f, j] = double + slope
                net = (scale[f] * cond_z[j]) * d - weight_z[j] * state
                total.append(value[j] + (net - carry_n[f, j]))
                carry_n[f, j] = net
            beyond = value[1:] + [y_next(value[0], right_q[f, row, :])]
            d = [b - a for a, b in zip(value, beyond)]
            before = [y_last(d[3], left_d[f, row, :])] + d[:3]
            slope = [minmod(a, b) for a, b in zip(before, d)]
            right = [a - b for a, b in zip(twice, slope)]
            right = right[1:] + [y_next(right[0], right_m[f, row, :])]
            net = []
            for j in J:
                state = jnp.where(weight_y[j] > 0.0, twice[j] + slope[j], right[j])
                net.append((scale[f] * cond_y[j]) * d[j] - weight_y[j] * state)
            before = [y_last(net[3], left_n[f, row, :])] + net[:3]
            for j in J:
                n = nx[f, j]
                t = total[j] + (net[j] - before[j])
                done[f, j] = t + (n - x_last(n, edge_x[j] * twice[j]))
        for j in J:
            u = q[0, i + 1, j]
            weight = 0.0625 * ((u + u) + dx_old[0, j])
            cond = cx_old[j]
            for f in range(F):
                a = q[f, i + 1, j]
                state = jnp.where(weight > 0.0, px[f, j], x_next(mx[f, j], a + a))
                nx[f, j] = (scale[f] * cond) * dx_old[f, j] - weight * state
        for j in J:
            cx_old[j] = cx[j]
            for f in range(F):
                a, d = q[f, i + 2, j], dx[f, j]
                slope = minmod(x_last(d, 0.0), d)
                px[f, j], mx[f, j] = (a + a) + slope, (a + a) - slope
                dx_old[f, j] = d
        for j in J:
            c = conduction(q[5, i + 3, j])
            cx[j] = c + x_next(c, c)
            for f in range(F):
                a = q[f, i + 3, j]
                dx[f, j] = x_next(a, a) - a

        @pl.when((i >= 12) & (i % 8 == 4))
        def _():
            for copy in leaving((i - 12) // 8):
                copy.start()

        return 0

    lax.fori_loop(0, B + LEAD, plane, 0)
    for k in range(4):
        for copy in leaving(k):
            copy.wait()


def step(owner, spread, *arrays):
    planes = lambda *lead: pltpu.VMEM((*lead, ROWS, LANES), F32)
    rows = pltpu.VMEM((F, B + 16, LANES), F32)
    return pl.pallas_call(
        step_body,
        name="step",
        out_shape=jax.ShapeDtypeStruct((F, B, ROWS, CAP, 1, LANES), F32),
        in_specs=[SMEM, SMEM] + [VMEM] * len(arrays),
        out_specs=HBM,
        scratch_shapes=[
            planes(F, B + 8, 4),
            planes(CAP, F, B + LEAD),
            rows,
            rows,
            rows,
            rows,
            pltpu.VMEM((B + 16, LANES), F32),
            planes(F, 4),
            planes(F, 4),
            planes(4),
            planes(4, F, 4),
            planes(F, 4),
            planes(F, 4),
            planes(4),
            planes(4),
            planes(F, 4),
            planes(F, 4),
            planes(F, 4),
            planes(F, 4),
            planes(F, 4),
            pltpu.SemaphoreType.DMA((4, CAP)),
        ],
        compiler_params=pltpu.CompilerParams(vmem_limit_bytes=24 << 20),
        cost_estimate=pl.CostEstimate(flops=0, bytes_accessed=40000000, transcendentals=0),
    )(owner, spread, *arrays)


def exchange(block, axes, first, wrap=False):
    count = lax.axis_size(axes)
    pairs = []
    for i in range(first, count, 2):
        j = (i + 1) % count
        if i + 1 < count or wrap:
            pairs += [(i, j), (j, i)]
    return lax.ppermute(block, axes, pairs)


def local(old_state, old_owner, old_slot, diffusivity):
    x = old_state.reshape(8, F, B, ROWS, LANES).transpose(1, 2, 3, 0, 4)[..., None, :]
    far = far_boxes(x)
    near = near_boxes(x, far)
    near_sent = near
    far = exchange(far, AXES, 1, wrap=True)
    near = exchange(near, AXES, 0)
    hold, rim = held(x, near_sent)
    z_pair, z_cross, y_near, y_far = edges(old_owner, rim, far, near)
    y_far = exchange(y_far, "gy", 1)
    z_pair = exchange(z_pair, "gx", 0)
    z_cross = exchange(z_cross, "gx", 1)
    y_near = exchange(y_near, "gy", 0)
    out = step(old_owner, diffusivity, hold, far, near, z_pair, z_cross, y_near, y_far)
    return out[..., 0, :].transpose(3, 0, 1, 2, 4).reshape(CAP, F, B * B * B)


def solution(mesh):
    placed = (P(AXES, None, None), P(), P(), P())
    return jax.shard_map(
        local, mesh=mesh, in_specs=placed, out_specs=P(AXES, None, None), check_vma=False
    )
```

```python
import functools

import jax
import jax.numpy as jnp
from jax import lax
from jax.experimental import pallas as pl
from jax.experimental.pallas import tpu as pltpu
from jax.sharding import PartitionSpec as P

B = 32
F = 6
CAP = 4
PARTS = 4
HALF = 16
ROWS = 8
LANES = 128
AXES = ("gx", "gy")
F32 = jnp.float32
HBM = pl.BlockSpec(memory_space=pl.ANY)
VMEM = pl.BlockSpec(memory_space=pltpu.VMEM)
SMEM = pl.BlockSpec(memory_space=pltpu.SMEM)
WIDE = 56 << 20


def run_all(copies):
    for copy in copies:
        copy.start()
    for copy in copies:
        copy.wait()


def odd(axis):
    return lax.axis_index(axis) % 2 == 1


def leaving_copies(x, near, target, planes, sem):
    first = jnp.where(odd("gy"), 0, 6) if near else jnp.where(odd("gy"), 6, 0)
    return [
        pltpu.make_async_copy(x.at[:, planes, :, first + j, 0], target.at[j], sem.at[j])
        for j in range(2)
    ]


def far_body(x, low, high, sem):
    run_all(
        leaving_copies(x, False, low, slice(0, HALF), sem.at[0])
        + leaving_copies(x, False, high, slice(HALF, B), sem.at[1])
    )


def near_body(x, after, *rest):
    nears, (hold_low, hold_high, sem) = rest[:PARTS], rest[PARTS:]
    copies = []
    for k, near in enumerate(nears):
        copies += leaving_copies(x, True, near, slice(8 * k, 8 * k + 8), sem.at[2 + k])
    for k, hold in enumerate((hold_low, hold_high)):
        for c in range(CAP):
            planes = slice(HALF * k, HALF * k + HALF)
            copies.append(
                pltpu.make_async_copy(
                    x.at[:, planes, :, 2 + c, 0], hold.at[c], sem.at[k, c]
                )
            )
    run_all(copies)


def from_slots(body, name, arrays, shapes, sems):
    shapes = tuple(jax.ShapeDtypeStruct(shape, F32) for shape in shapes)
    return pl.pallas_call(
        body,
        name=name,
        out_shape=shapes,
        in_specs=[HBM] * len(arrays),
        out_specs=(VMEM,) * len(shapes),
        scratch_shapes=[pltpu.SemaphoreType.DMA(sems)],
        compiler_params=pltpu.CompilerParams(vmem_limit_bytes=WIDE),
        cost_estimate=pl.CostEstimate(flops=0, bytes_accessed=1000, transcendentals=0),
    )(*arrays)


def far_boxes(x):
    return from_slots(far_body, "far", [x], [(2, F, HALF, ROWS, LANES)] * 2, (2, 2))


def near_boxes(x, after):
    half = (CAP, F, HALF, ROWS, LANES)
    part = (2, F, B // PARTS, ROWS, LANES)
    return from_slots(
        near_body, "near", [x, after], [part] * PARTS + [half, half], (2 + PARTS, CAP)
    )


def device_number():
    return lax.axis_index("gx") * lax.axis_size("gy") + lax.axis_index("gy")


def kept_flags(owner):
    device = device_number()
    return [owner[device * CAP + c] == device for c in range(CAP)]


def arrived(kept, here, c, far, near):
    from_far = odd("gy") if c >= 2 else jnp.logical_not(odd("gy"))
    return jnp.where(kept, here, jnp.where(from_far, far, near))


def swap_64(a, b, lane):
    low = lane < 64
    m = pltpu.roll(jnp.where(low, b, a), 64, 1)
    return jnp.where(low, a, m), jnp.where(low, m, b)


def swap_32(a, b, lane):
    even = (lane & 32) == 0
    m = jnp.where(even, b, a)
    return jnp.where(even, a, pltpu.roll(m, 32, 1)), jnp.where(even, pltpu.roll(m, 96, 1), b)


def turned_to_layers(v, lane):
    a, c = swap_64(v[0], v[2], lane)
    b, d = swap_64(v[1], v[3], lane)
    return *swap_32(a, b, lane), *swap_32(c, d, lane)


def turn_half(kept, hold, nears, far, target, index):
    lane = lax.broadcasted_iota(jnp.int32, (8, LANES), 1)
    for near, z0 in ((nears[0], 0), (nears[1], 8)):

        def group(g, _):
            for z in (2 * g, 2 * g + 1):
                for f in range(F):
                    v = [
                        arrived(
                            kept[c], hold[c, f, z0 + z], c, far[c % 2, f, z0 + z], near[c % 2, f, z]
                        )
                        for c in range(CAP)
                    ]
                    for j, value in enumerate(turned_to_layers(v, lane)):
                        target[f, index + z0 + z, j] = value
            return 0

        lax.fori_loop(0, 4, group, 0)


def turn_low_body(owner, hold, near_0, near_1, far, q):
    turn_half(kept_flags(owner), hold, (near_0, near_1), far, q, 3)
    for f in range(F):
        q[f, 0] = q[f, 3]
        q[f, 1] = q[f, 3]
        q[f, 2] = q[f, 3]


def turn_high_body(
    owner, hold, near_0, near_1, far, q_low, after, q, z_own, y_own, z_pair, z_cross, y_near, y_far
):
    turn_half(kept_flags(owner), hold, (near_0, near_1), far, q, 5)
    odd_z, odd_y = odd("gx"), odd("gy")
    for f in range(F):
        for k in range(5):
            q[f, k] = q_low[f, k + 14]
        q[f, 21] = q[f, 20]
        q[f, 22] = q[f, 20]
        ends = [q_low[f, 3], q_low[f, 4], q[f, 19], q[f, 20]]
        for k in range(4):
            z_own[f, k] = ends[k]
        for k in range(2):
            z_pair[f, k] = jnp.where(odd_z, ends[k], ends[2 + k])
            z_cross[f, k] = jnp.where(odd_z, ends[2 + k], ends[k])
        for b in range(4):
            span = slice(8 * b, 8 * b + 8)
            source, z = (q_low, 8 * b + 3) if b < 2 else (q, 8 * b - 11)
            ends = [source[f, z : z + 8, j, 0 if j < 2 else 7, :] for j in range(4)]
            for k in range(4):
                y_own[f, k, span, :] = ends[k]
            for k in range(2):
                y_near[f, k, span, :] = jnp.where(odd_y, ends[k], ends[2 + k])
                y_far[f, k, span, :] = jnp.where(odd_y, ends[2 + k], ends[k])


def turn(body, name, planes, owner, arrays, others, after=()):
    shapes = [(F, planes, 4, ROWS, LANES)] + others
    return pl.pallas_call(
        body,
        name=name,
        out_shape=tuple(jax.ShapeDtypeStruct(shape, F32) for shape in shapes),
        in_specs=[SMEM] + [VMEM] * len(arrays) + [HBM] * len(after),
        out_specs=(VMEM,) * len(shapes),
        compiler_params=pltpu.CompilerParams(vmem_limit_bytes=24 << 20),
        cost_estimate=pl.CostEstimate(flops=0, bytes_accessed=6000000, transcendentals=0),
    )(owner, *arrays, *after)


def turn_low(owner, *arrays):
    return turn(turn_low_body, "turn_low", LOW + 10, owner, arrays, [])[0]


def turn_high(owner, after, *arrays):
    z_own, y_own = (F, 4, 4, ROWS, LANES), (F, 4, B, LANES)
    z_half, y_half = (F, 2, 4, ROWS, LANES), (F, 2, B, LANES)
    others = [z_own, y_own, z_half, z_half, y_half, y_half]
    return turn(turn_high_body, "turn_high", B - LOW + 10, owner, arrays, others, (after,))


def minmod(a, b):
    return jnp.maximum(jnp.minimum(a, b), jnp.minimum(jnp.maximum(a, b), 0.0))


def conduction(v):
    return jnp.exp(0.5 * jnp.tanh(v))


LEAD = 5
J = range(4)
LOW = 14


def step_body(
    first, count, chunk, spread, q, *rest,
):
    (
        out, result, carry_p, carry_n, carry_c, dx, dx_old, cx, cx_old, px, mx, nx, done, turned, sem_out,
    ) = rest[-15:]
    lane = lax.broadcasted_iota(jnp.int32, (8, LANES), 1)
    sub = lax.broadcasted_iota(jnp.int32, (8, LANES), 0)
    scale = [0.5 * spread[f] for f in range(F)]

    def y_next(value, end):
        return jnp.where(sub == 7, end, pltpu.roll(value, 7, 0))

    def y_last(value, end):
        return jnp.where(sub == 0, end, pltpu.roll(value, 1, 0))

    def leaving(k):
        z = chunk * k
        return [
            pltpu.make_async_copy(
                result.at[c, :, pl.ds(z + LEAD, chunk)],
                out.at[:, pl.ds(first + z, chunk), :, c, 0],
                sem_out.at[k, c],
            )
            for c in range(CAP)
        ]

    def plane(i, _):
        for f in range(F):
            for j in (0, 2):
                result[j, f, i], result[j + 1, f, i] = swap_32(turned[f, j], turned[f, j + 1], lane)
        for f in range(F):
            for j in (0, 1):
                turned[f, j], turned[f, j + 2] = swap_64(done[f, j], done[f, j + 2], lane)

        here = [carry_c[j] for j in J]
        above = [conduction(q[5, i + 1, j]) for j in J]
        cond_z = [a + b for a, b in zip(here, above)]
        for j in J:
            carry_c[j] = above[j]
        beyond = here[1:] + [y_next(here[0], here[3])]
        cond_y = [a + b for a, b in zip(here, beyond)]
        v = [q[1, i, j] for j in J]
        beyond = v[1:] + [y_next(v[0], v[3])]
        weight_y = [0.0625 * (a + b) for a, b in zip(v, beyond)]
        weight_z = [0.0625 * (q[2, i, j] + q[2, i + 1, j]) for j in J]
        edge_y = -0.125 * v[0]
        edge_x = [-0.125 * q[0, i, j] for j in J]
        for f in range(F):
            value = [q[f, i, j] for j in J]
            twice = [a + a for a in value]
            total = []
            for j in J:
                after = q[f, i + 1, j]
                d = after - value[j]
                slope = minmod(d, q[f, i + 2, j] - after)
                double = after + after
                state = jnp.where(weight_z[j] > 0.0, carry_p[f, j], double - slope)
                carry_p[f, j] = double + slope
                net = (scale[f] * cond_z[j]) * d - weight_z[j] * state
                total.append(value[j] + (net - carry_n[f, j]))
                carry_n[f, j] = net
            beyond = value[1:] + [y_next(value[0], value[3])]
            d = [b - a for a, b in zip(value, beyond)]
            before = [y_last(d[3], 0.0)] + d[:3]
            slope = [minmod(a, b) for a, b in zip(before, d)]
            right = [a - b for a, b in zip(twice, slope)]
            right = right[1:] + [y_next(right[0], twice[3])]
            net = []
            for j in J:
                state = jnp.where(weight_y[j] > 0.0, twice[j] + slope[j], right[j])
                net.append((scale[f] * cond_y[j]) * d[j] - weight_y[j] * state)
            before = [y_last(net[3], edge_y * twice[0])] + net[:3]
            for j in J:
                n = nx[f, j]
                t = total[j] + (net[j] - before[j])
                before_x = jnp.where(lane == 0, edge_x[j] * twice[j], pltpu.roll(n, 1, 1))
                done[f, j] = t + (n - before_x)
        for j in J:
            u = q[0, i + 1, j]
            weight = 0.0625 * ((u + u) + dx_old[0, j])
            from_left = (weight > 0.0) | (lane == 127)
            cond = cx_old[j]
            for f in range(F):
                state = jnp.where(from_left, px[f, j], pltpu.roll(mx[f, j], 127, 1))
                nx[f, j] = (scale[f] * cond) * dx_old[f, j] - weight * state
        for j in J:
            cx_old[j] = cx[j]
            for f in range(F):
                a, d = q[f, i + 2, j], dx[f, j]
                slope = minmod(pltpu.roll(d, 1, 1), d)
                px[f, j], mx[f, j] = (a + a) + slope, (a + a) - slope
                dx_old[f, j] = d
        for j in J:
            c = conduction(q[5, i + 3, j])
            cx[j] = c + jnp.where(lane == 127, c, pltpu.roll(c, 127, 1))
            for f in range(F):
                a = q[f, i + 3, j]
                dx[f, j] = jnp.where(lane == 127, 0.0, pltpu.roll(a, 127, 1) - a)

        @pl.when((i >= chunk + 4) & ((i - 4) % chunk == 0))
        def _():
            for copy in leaving((i - 4) // chunk - 1):
                copy.start()

        return 0

    lax.fori_loop(0, count + LEAD, plane, 0)
    for k in range(count // chunk):
        for copy in leaving(k):
            copy.wait()


def step(first, count, chunk, spread, q, out=None):
    planes = lambda *lead: pltpu.VMEM((*lead, ROWS, LANES), F32)
    return pl.pallas_call(
        functools.partial(step_body, first, count, chunk),
        name="step",
        out_shape=jax.ShapeDtypeStruct((F, B, ROWS, CAP, 1, LANES), F32),
        in_specs=[SMEM, VMEM] + ([] if out is None else [HBM]),
        out_specs=HBM,
        input_output_aliases={} if out is None else {2: 0},
        scratch_shapes=[
            planes(CAP, F, count + LEAD),
            planes(F, 4),
            planes(F, 4),
            planes(4),
            planes(F, 4),
            planes(F, 4),
            planes(4),
            planes(4),
            planes(F, 4),
            planes(F, 4),
            planes(F, 4),
            planes(F, 4),
            planes(F, 4),
            pltpu.SemaphoreType.DMA((count // chunk, CAP)),
        ],
        compiler_params=pltpu.CompilerParams(vmem_limit_bytes=24 << 20),
        cost_estimate=pl.CostEstimate(flops=0, bytes_accessed=20000000, transcendentals=0),
    )(spread, q, *(() if out is None else (out,)))


def change(far, out_1, in_0, in_1, u_out, u_0, u_1, c_out, c_0, scale):
    d = in_0 - out_1
    slope = minmod(d, in_1 - in_0)
    inner = -jnp.maximum(0.0625 * (u_0 + u_1), 0.0) * slope
    weight = 0.0625 * (u_out + u_0)
    left = (out_1 + out_1) + minmod(out_1 - far, d)
    right = (in_0 + in_0) - slope
    net = (scale * (c_out + c_0)) * d - weight * jnp.where(weight > 0.0, left, right)
    outer = net + (0.125 * u_0) * (in_0 + in_0)
    return inner - outer, -inner


def both_ends(below, own, above, velocity, has_below, has_above, scale):
    u = [below(velocity, 1)] + [own(velocity, k) for k in range(4)] + [above(velocity, 0)]
    c = [conduction(v) for v in (below(5, 1), own(5, 0), own(5, 3), above(5, 0))]
    result = []
    for f in range(F):
        layers = [own(f, k) for k in range(4)]
        a, b = change(
            below(f, 0), below(f, 1), layers[0], layers[1], u[0], u[1], u[2], c[0], c[1], scale[f]
        )
        e, d = change(
            above(f, 1), above(f, 0), layers[3], layers[2], -u[5], -u[4], -u[3], c[3], c[2], scale[f]
        )
        a, b = jnp.where(has_below, a, 0.0), jnp.where(has_below, b, 0.0)
        d, e = jnp.where(has_above, d, 0.0), jnp.where(has_above, e, 0.0)
        result.append([a, b, d, e])
    return result


def ends_body(
    spread, z_own, y_own, z_pair, z_cross, y_near, y_far, before, out,
    z_add, y_add, planes, first, last, sem, sem_in, sem_out,
):
    gx, gy = lax.axis_index("gx"), lax.axis_index("gy")
    odd_z, odd_y = odd("gx"), odd("gy")
    lane = lax.broadcasted_iota(jnp.int32, (8, LANES), 1)
    sub = lax.broadcasted_iota(jnp.int32, (8, LANES), 0)
    scale = [0.5 * spread[f] for f in range(F)]

    def moves(inward):
        rows, whole = [], []
        for c in range(CAP):
            parts = [
                (out.at[:, :, 0, c, 0], first.at[c], rows),
                (out.at[:, :, 7, c, 0], last.at[c], rows),
                (out.at[:, 0:2, :, c, 0], planes.at[c, :, 0:2], whole),
                (out.at[:, 30:32, :, c, 0], planes.at[c, :, 2:4], whole),
            ]
            for k, (there, here, kind) in enumerate(parts):
                source, target = (there, here) if inward else (here, there)
                kind.append(
                    pltpu.make_async_copy(source, target, (sem_in if inward else sem_out).at[c, k])
                )
        return rows, whole

    rows, whole = moves(True)
    for copy in rows + whole:
        copy.start()

    for j in range(4):
        changes = both_ends(
            lambda f, k: jnp.where(odd_z, z_pair[f, k, j], z_cross[f, k, j]),
            lambda f, k: z_own[f, k, j],
            lambda f, k: jnp.where(odd_z, z_cross[f, k, j], z_pair[f, k, j]),
            2, gx > 0, gx < lax.axis_size("gx") - 1, scale,
        )
        for f in range(F):
            for k in range(4):
                z_add[f, k, j] = changes[f][k]
    for b in range(4):
        span = slice(8 * b, 8 * b + 8)
        changes = both_ends(
            lambda f, k: jnp.where(odd_y, y_near[f, k, span, :], y_far[f, k, span, :]),
            lambda f, k: y_own[f, k, span, :],
            lambda f, k: jnp.where(odd_y, y_far[f, k, span, :], y_near[f, k, span, :]),
            1, gy > 0, gy < lax.axis_size("gy") - 1, scale,
        )
        for f in range(F):
            for c, value in enumerate(turned_to_layers(changes[f], lane)):
                y_add[c, f, span, :] = value

    for copy in rows + whole:
        copy.wait()
    corner = ((sub == 0) & (lane < 64)) | ((sub == 7) & (lane >= 64))
    for f in range(F):
        for c in range(CAP):
            for b in range(4):
                span = slice(8 * b, 8 * b + 8)
                value = y_add[c, f, span, :]
                first[c, f, span, :] += jnp.where(lane < 64, value, 0.0)
                last[c, f, span, :] += jnp.where(lane >= 64, value, 0.0)
        for k, z in enumerate((0, 1, 30, 31)):
            values = turned_to_layers([z_add[f, k, j] for j in range(4)], lane)
            for c in range(CAP):
                planes[c, f, k] += values[c] + jnp.where(corner, y_add[c, f, z : z + 1, :], 0.0)
    rows, whole = moves(False)
    run_all(rows)
    run_all(whole)


def ends(spread, *arrays):
    rows = pltpu.VMEM((CAP, F, B, LANES), F32)
    planes = pltpu.VMEM((CAP, F, 4, ROWS, LANES), F32)
    return pl.pallas_call(
        ends_body,
        name="ends",
        out_shape=jax.ShapeDtypeStruct((F, B, ROWS, CAP, 1, LANES), F32),
        in_specs=[SMEM] + [VMEM] * (len(arrays) - 1) + [HBM],
        out_specs=HBM,
        input_output_aliases={len(arrays): 0},
        scratch_shapes=[
            pltpu.VMEM((F, 4, 4, ROWS, LANES), F32),
            rows,
            planes,
            rows,
            rows,
            pltpu.SemaphoreType.DMA((1,)),
            pltpu.SemaphoreType.DMA((CAP, 4)),
            pltpu.SemaphoreType.DMA((CAP, 4)),
        ],
        compiler_params=pltpu.CompilerParams(vmem_limit_bytes=24 << 20),
        cost_estimate=pl.CostEstimate(flops=0, bytes_accessed=6000000, transcendentals=0),
    )(spread, *arrays)


def exchange(block, axes, first, wrap=False):
    count = lax.axis_size(axes)
    pairs = []
    for i in range(first, count, 2):
        j = (i + 1) % count
        if i + 1 < count or wrap:
            pairs += [(i, j), (j, i)]
    return lax.ppermute(block, axes, pairs)


def local(old_state, old_owner, old_slot, diffusivity):
    x = old_state.reshape(8, F, B, ROWS, LANES).transpose(1, 2, 3, 0, 4)[..., None, :]
    far_low, far_high = far_boxes(x)
    *nears, hold_low, hold_high = near_boxes(x, far_low)
    far_low = exchange(far_low, AXES, 1, wrap=True)
    far_high = exchange(far_high, AXES, 1, wrap=True)
    nears = [exchange(near, AXES, 0) for near in nears]
    q_low = turn_low(old_owner, hold_low, *nears[:2], far_low)
    out = step(0, LOW, 7, diffusivity, q_low)
    q_high, z_own, y_own, z_pair, z_cross, y_near, y_far = turn_high(
        old_owner, out, hold_high, *nears[2:], far_high, q_low
    )
    y_near = exchange(y_near, "gy", 0)
    y_far = exchange(y_far, "gy", 1)
    z_pair = exchange(z_pair, "gx", 0)
    z_cross = exchange(z_cross, "gx", 1)
    out = step(LOW, B - LOW, 9, diffusivity, q_high, out)
    out = ends(diffusivity, z_own, y_own, z_pair, z_cross, y_near, y_far, out)
    return out[..., 0, :].transpose(3, 0, 1, 2, 4).reshape(CAP, F, B * B * B)


def solution(mesh):
    placed = (P(AXES, None, None), P(), P(), P())
    return jax.shard_map(
        local, mesh=mesh, in_specs=placed, out_specs=P(AXES, None, None), check_vma=False
    )
```

```python
import functools

import jax
import jax.numpy as jnp
from jax import lax
from jax.experimental import pallas as pl
from jax.experimental.pallas import tpu as pltpu
from jax.sharding import PartitionSpec as P

B = 32
F = 6
CAP = 4
PARTS = 4
HALF = 16
ROWS = 8
LANES = 128
AXES = ("gx", "gy")
F32 = jnp.float32
HBM = pl.BlockSpec(memory_space=pl.ANY)
VMEM = pl.BlockSpec(memory_space=pltpu.VMEM)
SMEM = pl.BlockSpec(memory_space=pltpu.SMEM)
WIDE = 56 << 20


def run_all(copies):
    for copy in copies:
        copy.start()
    for copy in copies:
        copy.wait()


def odd(axis):
    return lax.axis_index(axis) % 2 == 1


def leaving_copies(x, near, target, planes, sem):
    first = jnp.where(odd("gy"), 0, 6) if near else jnp.where(odd("gy"), 6, 0)
    return [
        pltpu.make_async_copy(x.at[:, planes, :, first + j, 0], target.at[j], sem.at[j])
        for j in range(2)
    ]


def far_body(x, low, token, sem):
    token[...] = jnp.zeros_like(token)
    run_all(leaving_copies(x, False, low, slice(0, HALF), sem))


def near_body(x, after, high, *rest):
    nears, (hold_low, hold_high, sem) = rest[:PARTS], rest[PARTS:]
    copies = leaving_copies(x, False, high, slice(HALF, B), sem.at[2 + PARTS])
    for k, near in enumerate(nears):
        copies += leaving_copies(x, True, near, slice(8 * k, 8 * k + 8), sem.at[2 + k])
    for k, hold in enumerate((hold_low, hold_high)):
        for c in range(CAP):
            planes = slice(HALF * k, HALF * k + HALF)
            copies.append(
                pltpu.make_async_copy(x.at[:, planes, :, 2 + c, 0], hold.at[c], sem.at[k, c])
            )
    run_all(copies)


def from_slots(body, name, arrays, shapes, sems, limit):
    shapes = tuple(jax.ShapeDtypeStruct(shape, F32) for shape in shapes)
    return pl.pallas_call(
        body,
        name=name,
        out_shape=shapes,
        in_specs=[HBM] * len(arrays),
        out_specs=(VMEM,) * len(shapes),
        scratch_shapes=[pltpu.SemaphoreType.DMA(sems)],
        compiler_params=pltpu.CompilerParams(vmem_limit_bytes=limit),
        cost_estimate=pl.CostEstimate(flops=0, bytes_accessed=1000, transcendentals=0),
    )(*arrays)


def far_boxes(x):
    return from_slots(far_body, "far", [x], [(2, F, HALF, ROWS, LANES), (ROWS, LANES)], (2,), WIDE)


def near_boxes(x, after):
    part = (2, F, B // PARTS, ROWS, LANES)
    half = (CAP, F, HALF, ROWS, LANES)
    shapes = [(2, F, HALF, ROWS, LANES)] + [part] * PARTS + [half, half]
    return from_slots(near_body, "near", [x, after], shapes, (3 + PARTS, CAP), 24 << 20)


def device_number():
    return lax.axis_index("gx") * lax.axis_size("gy") + lax.axis_index("gy")


def kept_flags(owner):
    device = device_number()
    return [owner[device * CAP + c] == device for c in range(CAP)]


def arrived(kept, here, c, far, near):
    from_far = odd("gy") if c >= 2 else jnp.logical_not(odd("gy"))
    return jnp.where(kept, here, jnp.where(from_far, far, near))


def swap_64(a, b, lane):
    low = lane < 64
    m = pltpu.roll(jnp.where(low, b, a), 64, 1)
    return jnp.where(low, a, m), jnp.where(low, m, b)


def swap_32(a, b, lane):
    even = (lane & 32) == 0
    m = jnp.where(even, b, a)
    return jnp.where(even, a, pltpu.roll(m, 32, 1)), jnp.where(even, pltpu.roll(m, 96, 1), b)


def turned_to_layers(v, lane):
    a, c = swap_64(v[0], v[2], lane)
    b, d = swap_64(v[1], v[3], lane)
    return *swap_32(a, b, lane), *swap_32(c, d, lane)


def turn_half(kept, hold, nears, far, target, index, half):
    lane = lax.broadcasted_iota(jnp.int32, (8, LANES), 1)

    def first_half(z):
        near = nears[z // 8]
        for f in range(F):
            v = [
                arrived(kept[c], hold[c, f, z], c, far[c % 2, f, z], near[c % 2, f, z % 8])
                for c in range(CAP)
            ]
            half[z % 8, f, 0], half[z % 8, f, 2] = swap_64(v[0], v[2], lane)
            half[z % 8, f, 1], half[z % 8, f, 3] = swap_64(v[1], v[3], lane)

    def second_half(z):
        for f in range(F):
            a, b, c, d = [half[z % 8, f, j] for j in range(4)]
            target[f, index + z, 0], target[f, index + z, 1] = swap_32(a, b, lane)
            target[f, index + z, 2], target[f, index + z, 3] = swap_32(c, d, lane)

    for z in range(HALF + 4):
        if z < HALF:
            first_half(z)
        if z >= 4:
            second_half(z - 4)


def turn_low_body(owner, hold, near_0, near_1, far, q, half):
    turn_half(kept_flags(owner), hold, (near_0, near_1), far, q, 3, half)
    for f in range(F):
        q[f, 0] = q[f, 3]
        q[f, 1] = q[f, 3]
        q[f, 2] = q[f, 3]


def turn_high_body(
    owner, hold, near_0, near_1, far, q_low, after, q, z_own, y_own, z_pair, z_cross, y_near, y_far, half
):
    turn_half(kept_flags(owner), hold, (near_0, near_1), far, q, 5, half)
    odd_z, odd_y = odd("gx"), odd("gy")
    for f in range(F):
        for k in range(5):
            q[f, k] = q_low[f, k + 14]
        q[f, 21] = q[f, 20]
        q[f, 22] = q[f, 20]
        ends = [q_low[f, 3], q_low[f, 4], q[f, 19], q[f, 20]]
        for k in range(4):
            z_own[f, k] = ends[k]
        for k in range(2):
            z_pair[f, k] = jnp.where(odd_z, ends[k], ends[2 + k])
            z_cross[f, k] = jnp.where(odd_z, ends[2 + k], ends[k])
        for b in range(4):
            span = slice(8 * b, 8 * b + 8)
            source, z = (q_low, 8 * b + 3) if b < 2 else (q, 8 * b - 11)
            ends = [source[f, z : z + 8, j, 0 if j < 2 else 7, :] for j in range(4)]
            for k in range(4):
                y_own[f, k, span, :] = ends[k]
            for k in range(2):
                y_near[f, k, span, :] = jnp.where(odd_y, ends[k], ends[2 + k])
                y_far[f, k, span, :] = jnp.where(odd_y, ends[2 + k], ends[k])


def turn(body, name, planes, owner, arrays, others, after=()):
    shapes = [(F, planes, 4, ROWS, LANES)] + others
    return pl.pallas_call(
        body,
        name=name,
        out_shape=tuple(jax.ShapeDtypeStruct(shape, F32) for shape in shapes),
        in_specs=[SMEM] + [VMEM] * (len(arrays) + len(after)),
        out_specs=(VMEM,) * len(shapes),
        scratch_shapes=[pltpu.VMEM((8, F, 4, ROWS, LANES), F32)],
        compiler_params=pltpu.CompilerParams(vmem_limit_bytes=24 << 20),
        cost_estimate=pl.CostEstimate(flops=0, bytes_accessed=6000000, transcendentals=0),
    )(owner, *arrays, *after)


def turn_low(owner, *arrays):
    return turn(turn_low_body, "turn_low", LOW + 10, owner, arrays, [])[0]


def turn_high(owner, after, *arrays):
    z_own, y_own = (F, 4, 4, ROWS, LANES), (F, 4, B, LANES)
    z_half, y_half = (F, 2, 4, ROWS, LANES), (F, 2, B, LANES)
    others = [z_own, y_own, z_half, z_half, y_half, y_half]
    return turn(turn_high_body, "turn_high", B - LOW + 10, owner, arrays, others, (after,))


def minmod(a, b):
    return jnp.maximum(jnp.minimum(a, b), jnp.minimum(jnp.maximum(a, b), 0.0))


def conduction(v):
    return jnp.exp(0.5 * jnp.tanh(v))


LEAD = 5
J = range(4)
LOW = 14


def step_body(
    first, count, chunk, spread, q, *rest,
):
    (
        out, token, result, carry_p, carry_n, carry_c, dx, dx_old, cx, cx_old, px, mx, nx, done, turned, sem_out,
    ) = rest[-16:]
    token[...] = jnp.zeros_like(token)
    lane = lax.broadcasted_iota(jnp.int32, (8, LANES), 1)
    sub = lax.broadcasted_iota(jnp.int32, (8, LANES), 0)
    scale = [0.5 * spread[f] for f in range(F)]

    def y_next(value, end):
        return jnp.where(sub == 7, end, pltpu.roll(value, 7, 0))

    def y_last(value, end):
        return jnp.where(sub == 0, end, pltpu.roll(value, 1, 0))

    def leaving(k):
        z = chunk * k
        return [
            pltpu.make_async_copy(
                result.at[c, :, pl.ds(z + LEAD, chunk)],
                out.at[:, pl.ds(first + z, chunk), :, c, 0],
                sem_out.at[k, c],
            )
            for c in range(CAP)
        ]

    def plane(i, _):
        for f in range(F):
            for j in (0, 2):
                result[j, f, i], result[j + 1, f, i] = swap_32(turned[f, j], turned[f, j + 1], lane)
        for f in range(F):
            for j in (0, 1):
                turned[f, j], turned[f, j + 2] = swap_64(done[f, j], done[f, j + 2], lane)

        here = [carry_c[j] for j in J]
        above = [conduction(q[5, i + 1, j]) for j in J]
        cond_z = [a + b for a, b in zip(here, above)]
        for j in J:
            carry_c[j] = above[j]
        beyond = here[1:] + [y_next(here[0], here[3])]
        cond_y = [a + b for a, b in zip(here, beyond)]
        v = [q[1, i, j] for j in J]
        beyond = v[1:] + [y_next(v[0], v[3])]
        weight_y = [0.0625 * (a + b) for a, b in zip(v, beyond)]
        weight_z = [0.0625 * (q[2, i, j] + q[2, i + 1, j]) for j in J]
        edge_y = -0.125 * v[0]
        edge_x = [-0.125 * q[0, i, j] for j in J]
        for f in range(F):
            value = [q[f, i, j] for j in J]
            twice = [a + a for a in value]
            total = []
            for j in J:
                after = q[f, i + 1, j]
                d = after - value[j]
                slope = minmod(d, q[f, i + 2, j] - after)
                double = after + after
                state = jnp.where(weight_z[j] > 0.0, carry_p[f, j], double - slope)
                carry_p[f, j] = double + slope
                net = (scale[f] * cond_z[j]) * d - weight_z[j] * state
                total.append(value[j] + (net - carry_n[f, j]))
                carry_n[f, j] = net
            beyond = value[1:] + [y_next(value[0], value[3])]
            d = [b - a for a, b in zip(value, beyond)]
            before = [y_last(d[3], 0.0)] + d[:3]
            slope = [minmod(a, b) for a, b in zip(before, d)]
            right = [a - b for a, b in zip(twice, slope)]
            right = right[1:] + [y_next(right[0], twice[3])]
            net = []
            for j in J:
                state = jnp.where(weight_y[j] > 0.0, twice[j] + slope[j], right[j])
                net.append((scale[f] * cond_y[j]) * d[j] - weight_y[j] * state)
            before = [y_last(net[3], edge_y * twice[0])] + net[:3]
            for j in J:
                n = nx[f, j]
                t = total[j] + (net[j] - before[j])
                before_x = jnp.where(lane == 0, edge_x[j] * twice[j], pltpu.roll(n, 1, 1))
                done[f, j] = t + (n - before_x)
        for j in J:
            u = q[0, i + 1, j]
            weight = 0.0625 * ((u + u) + dx_old[0, j])
            from_left = (weight > 0.0) | (lane == 127)
            cond = cx_old[j]
            for f in range(F):
                state = jnp.where(from_left, px[f, j], pltpu.roll(mx[f, j], 127, 1))
                nx[f, j] = (scale[f] * cond) * dx_old[f, j] - weight * state
        for j in J:
            cx_old[j] = cx[j]
            for f in range(F):
                a, d = q[f, i + 2, j], dx[f, j]
                slope = minmod(pltpu.roll(d, 1, 1), d)
                px[f, j], mx[f, j] = (a + a) + slope, (a + a) - slope
                dx_old[f, j] = d
        for j in J:
            c = conduction(q[5, i + 3, j])
            cx[j] = c + jnp.where(lane == 127, c, pltpu.roll(c, 127, 1))
            for f in range(F):
                a = q[f, i + 3, j]
                dx[f, j] = jnp.where(lane == 127, 0.0, pltpu.roll(a, 127, 1) - a)

        @pl.when((i >= chunk + 4) & ((i - 4) % chunk == 0))
        def _():
            for copy in leaving((i - 4) // chunk - 1):
                copy.start()

        return 0

    lax.fori_loop(0, count + LEAD, plane, 0)
    for k in range(count // chunk):
        for copy in leaving(k):
            copy.wait()


def step(first, count, chunk, spread, q, out=None):
    planes = lambda *lead: pltpu.VMEM((*lead, ROWS, LANES), F32)
    return pl.pallas_call(
        functools.partial(step_body, first, count, chunk),
        name="step",
        out_shape=(
            jax.ShapeDtypeStruct((F, B, ROWS, CAP, 1, LANES), F32),
            jax.ShapeDtypeStruct((ROWS, LANES), F32),
        ),
        in_specs=[SMEM, VMEM] + ([] if out is None else [HBM]),
        out_specs=(HBM, VMEM),
        input_output_aliases={} if out is None else {2: 0},
        scratch_shapes=[
            planes(CAP, F, count + LEAD),
            planes(F, 4),
            planes(F, 4),
            planes(4),
            planes(F, 4),
            planes(F, 4),
            planes(4),
            planes(4),
            planes(F, 4),
            planes(F, 4),
            planes(F, 4),
            planes(F, 4),
            planes(F, 4),
            pltpu.SemaphoreType.DMA((count // chunk, CAP)),
        ],
        compiler_params=pltpu.CompilerParams(vmem_limit_bytes=24 << 20),
        cost_estimate=pl.CostEstimate(flops=0, bytes_accessed=20000000, transcendentals=0),
    )(spread, q, *(() if out is None else (out,)))


def change(far, out_1, in_0, in_1, u_out, u_0, u_1, c_out, c_0, scale):
    d = in_0 - out_1
    slope = minmod(d, in_1 - in_0)
    inner = -jnp.maximum(0.0625 * (u_0 + u_1), 0.0) * slope
    weight = 0.0625 * (u_out + u_0)
    left = (out_1 + out_1) + minmod(out_1 - far, d)
    right = (in_0 + in_0) - slope
    net = (scale * (c_out + c_0)) * d - weight * jnp.where(weight > 0.0, left, right)
    outer = net + (0.125 * u_0) * (in_0 + in_0)
    return inner - outer, -inner


def both_ends(below, own, above, velocity, has_below, has_above, scale):
    u = [below(velocity, 1)] + [own(velocity, k) for k in range(4)] + [above(velocity, 0)]
    c = [conduction(v) for v in (below(5, 1), own(5, 0), own(5, 3), above(5, 0))]
    result = []
    for f in range(F):
        layers = [own(f, k) for k in range(4)]
        a, b = change(
            below(f, 0), below(f, 1), layers[0], layers[1], u[0], u[1], u[2], c[0], c[1], scale[f]
        )
        e, d = change(
            above(f, 1), above(f, 0), layers[3], layers[2], -u[5], -u[4], -u[3], c[3], c[2], scale[f]
        )
        a, b = jnp.where(has_below, a, 0.0), jnp.where(has_below, b, 0.0)
        d, e = jnp.where(has_above, d, 0.0), jnp.where(has_above, e, 0.0)
        result.append([a, b, d, e])
    return result


def ends_body(
    spread, z_own, y_own, z_pair, z_cross, y_near, y_far, before, out,
    z_add, y_add, planes, first, last, sem, sem_in, sem_out,
):
    gx, gy = lax.axis_index("gx"), lax.axis_index("gy")
    odd_z, odd_y = odd("gx"), odd("gy")
    lane = lax.broadcasted_iota(jnp.int32, (8, LANES), 1)
    sub = lax.broadcasted_iota(jnp.int32, (8, LANES), 0)
    scale = [0.5 * spread[f] for f in range(F)]

    def moves(inward):
        rows, whole = [], []
        for c in range(CAP):
            parts = [
                (out.at[:, :, 0, c, 0], first.at[c], rows),
                (out.at[:, :, 7, c, 0], last.at[c], rows),
                (out.at[:, 0:2, :, c, 0], planes.at[c, :, 0:2], whole),
                (out.at[:, 30:32, :, c, 0], planes.at[c, :, 2:4], whole),
            ]
            for k, (there, here, kind) in enumerate(parts):
                source, target = (there, here) if inward else (here, there)
                kind.append(
                    pltpu.make_async_copy(source, target, (sem_in if inward else sem_out).at[c, k])
                )
        return rows, whole

    rows, whole = moves(True)
    for copy in rows + whole:
        copy.start()

    for j in range(4):
        changes = both_ends(
            lambda f, k: jnp.where(odd_z, z_pair[f, k, j], z_cross[f, k, j]),
            lambda f, k: z_own[f, k, j],
            lambda f, k: jnp.where(odd_z, z_cross[f, k, j], z_pair[f, k, j]),
            2, gx > 0, gx < lax.axis_size("gx") - 1, scale,
        )
        for f in range(F):
            for k in range(4):
                z_add[f, k, j] = changes[f][k]
    for b in range(4):
        span = slice(8 * b, 8 * b + 8)
        changes = both_ends(
            lambda f, k: jnp.where(odd_y, y_near[f, k, span, :], y_far[f, k, span, :]),
            lambda f, k: y_own[f, k, span, :],
            lambda f, k: jnp.where(odd_y, y_far[f, k, span, :], y_near[f, k, span, :]),
            1, gy > 0, gy < lax.axis_size("gy") - 1, scale,
        )
        for f in range(F):
            for c, value in enumerate(turned_to_layers(changes[f], lane)):
                y_add[c, f, span, :] = value

    for copy in rows + whole:
        copy.wait()
    rows_out, whole_out = moves(False)
    for c in range(CAP):
        for f in range(F):
            for b in range(4):
                span = slice(8 * b, 8 * b + 8)
                value = y_add[c, f, span, :]
                first[c, f, span, :] += jnp.where(lane < 64, value, 0.0)
                last[c, f, span, :] += jnp.where(lane >= 64, value, 0.0)
        rows_out[2 * c].start()
        rows_out[2 * c + 1].start()
    corner = ((sub == 0) & (lane < 64)) | ((sub == 7) & (lane >= 64))
    for f in range(F):
        for k, z in enumerate((0, 1, 30, 31)):
            values = turned_to_layers([z_add[f, k, j] for j in range(4)], lane)
            for c in range(CAP):
                planes[c, f, k] += values[c] + jnp.where(corner, y_add[c, f, z : z + 1, :], 0.0)
    for copy in rows_out:
        copy.wait()
    run_all(whole_out)


def ends(spread, *arrays):
    rows = pltpu.VMEM((CAP, F, B, LANES), F32)
    planes = pltpu.VMEM((CAP, F, 4, ROWS, LANES), F32)
    return pl.pallas_call(
        ends_body,
        name="ends",
        out_shape=jax.ShapeDtypeStruct((F, B, ROWS, CAP, 1, LANES), F32),
        in_specs=[SMEM] + [VMEM] * (len(arrays) - 1) + [HBM],
        out_specs=HBM,
        input_output_aliases={len(arrays): 0},
        scratch_shapes=[
            pltpu.VMEM((F, 4, 4, ROWS, LANES), F32),
            rows,
            planes,
            rows,
            rows,
            pltpu.SemaphoreType.DMA((1,)),
            pltpu.SemaphoreType.DMA((CAP, 4)),
            pltpu.SemaphoreType.DMA((CAP, 4)),
        ],
        compiler_params=pltpu.CompilerParams(vmem_limit_bytes=24 << 20),
        cost_estimate=pl.CostEstimate(flops=0, bytes_accessed=6000000, transcendentals=0),
    )(spread, *arrays)


def exchange(block, axes, first, wrap=False):
    count = lax.axis_size(axes)
    pairs = []
    for i in range(first, count, 2):
        j = (i + 1) % count
        if i + 1 < count or wrap:
            pairs += [(i, j), (j, i)]
    return lax.ppermute(block, axes, pairs)


def local(old_state, old_owner, old_slot, diffusivity):
    x = old_state.reshape(8, F, B, ROWS, LANES).transpose(1, 2, 3, 0, 4)[..., None, :]
    far_low, token = far_boxes(x)
    far_high, *nears, hold_low, hold_high = near_boxes(x, token)
    far_low = exchange(far_low, AXES, 1, wrap=True)
    far_high = exchange(far_high, AXES, 1, wrap=True)
    nears = [exchange(near, AXES, 0) for near in nears]
    q_low = turn_low(old_owner, hold_low, *nears[:2], far_low)
    out, token = step(0, LOW, 7, diffusivity, q_low)
    q_high, z_own, y_own, z_pair, z_cross, y_near, y_far = turn_high(
        old_owner, token, hold_high, *nears[2:], far_high, q_low
    )
    y_near = exchange(y_near, "gy", 0)
    y_far = exchange(y_far, "gy", 1)
    z_pair = exchange(z_pair, "gx", 0)
    z_cross = exchange(z_cross, "gx", 1)
    out, _ = step(LOW, B - LOW, 9, diffusivity, q_high, out)
    out = ends(diffusivity, z_own, y_own, z_pair, z_cross, y_near, y_far, out)
    return out[..., 0, :].transpose(3, 0, 1, 2, 4).reshape(CAP, F, B * B * B)


def solution(mesh):
    placed = (P(AXES, None, None), P(), P(), P())
    return jax.shard_map(
        local, mesh=mesh, in_specs=placed, out_specs=P(AXES, None, None), check_vma=False
    )
```

```python
import functools

import jax
import jax.numpy as jnp
from jax import lax
from jax.experimental import pallas as pl
from jax.experimental.pallas import tpu as pltpu
from jax.sharding import PartitionSpec as P

B = 32
F = 6
CAP = 4
PARTS = 4
HALF = 16
ROWS = 8
LANES = 128
AXES = ("gx", "gy")
F32 = jnp.float32
HBM = pl.BlockSpec(memory_space=pl.ANY)
VMEM = pl.BlockSpec(memory_space=pltpu.VMEM)
SMEM = pl.BlockSpec(memory_space=pltpu.SMEM)
WIDE = 56 << 20


def run_all(copies):
    for copy in copies:
        copy.start()
    for copy in copies:
        copy.wait()


def odd(axis):
    return lax.axis_index(axis) % 2 == 1


def leaving_copies(x, near, target, planes, sem):
    first = jnp.where(odd("gy"), 0, 6) if near else jnp.where(odd("gy"), 6, 0)
    return [
        pltpu.make_async_copy(x.at[:, planes, :, first + j, 0], target.at[j], sem.at[j])
        for j in range(2)
    ]


def far_body(x, low, token, sem):
    token[...] = jnp.zeros_like(token)
    run_all(leaving_copies(x, False, low, slice(0, HALF), sem))


def near_body(x, after, high, *rest):
    nears, (hold_low, hold_high, sem) = rest[:PARTS], rest[PARTS:]
    copies = leaving_copies(x, False, high, slice(HALF, B), sem.at[2 + PARTS])
    for k, near in enumerate(nears):
        copies += leaving_copies(x, True, near, slice(8 * k, 8 * k + 8), sem.at[2 + k])
    for k, hold in enumerate((hold_low, hold_high)):
        for c in range(CAP):
            planes = slice(HALF * k, HALF * k + HALF)
            copies.append(
                pltpu.make_async_copy(x.at[:, planes, :, 2 + c, 0], hold.at[c], sem.at[k, c])
            )
    run_all(copies)


def from_slots(body, name, arrays, shapes, sems, limit):
    shapes = tuple(jax.ShapeDtypeStruct(shape, F32) for shape in shapes)
    return pl.pallas_call(
        body,
        name=name,
        out_shape=shapes,
        in_specs=[HBM] * len(arrays),
        out_specs=(VMEM,) * len(shapes),
        scratch_shapes=[pltpu.SemaphoreType.DMA(sems)],
        compiler_params=pltpu.CompilerParams(vmem_limit_bytes=limit),
        cost_estimate=pl.CostEstimate(flops=0, bytes_accessed=1000, transcendentals=0),
    )(*arrays)


def far_boxes(x):
    return from_slots(far_body, "far", [x], [(2, F, HALF, ROWS, LANES), (ROWS, LANES)], (2,), WIDE)


def near_boxes(x, after):
    part = (2, F, B // PARTS, ROWS, LANES)
    half = (CAP, F, HALF, ROWS, LANES)
    shapes = [(2, F, HALF, ROWS, LANES)] + [part] * PARTS + [half, half]
    return from_slots(near_body, "near", [x, after], shapes, (3 + PARTS, CAP), 24 << 20)


def device_number():
    return lax.axis_index("gx") * lax.axis_size("gy") + lax.axis_index("gy")


def kept_flags(owner):
    device = device_number()
    return [owner[device * CAP + c] == device for c in range(CAP)]


def arrived(kept, here, c, far, near):
    from_far = odd("gy") if c >= 2 else jnp.logical_not(odd("gy"))
    return jnp.where(kept, here, jnp.where(from_far, far, near))


def swap_64(a, b, lane):
    low = lane < 64
    m = pltpu.roll(jnp.where(low, b, a), 64, 1)
    return jnp.where(low, a, m), jnp.where(low, m, b)


def swap_32(a, b, lane):
    even = (lane & 32) == 0
    m = jnp.where(even, b, a)
    return jnp.where(even, a, pltpu.roll(m, 32, 1)), jnp.where(even, pltpu.roll(m, 96, 1), b)


def turned_to_layers(v, lane):
    a, c = swap_64(v[0], v[2], lane)
    b, d = swap_64(v[1], v[3], lane)
    return *swap_32(a, b, lane), *swap_32(c, d, lane)


def turn_half(kept, hold, nears, far, target, index, half):
    lane = lax.broadcasted_iota(jnp.int32, (8, LANES), 1)

    def first_half(z):
        near = nears[z // 8]
        for f in range(F):
            v = [
                arrived(kept[c], hold[c, f, z], c, far[c % 2, f, z], near[c % 2, f, z % 8])
                for c in range(CAP)
            ]
            half[z % 8, f, 0], half[z % 8, f, 2] = swap_64(v[0], v[2], lane)
            half[z % 8, f, 1], half[z % 8, f, 3] = swap_64(v[1], v[3], lane)

    def second_half(z):
        for f in range(F):
            a, b, c, d = [half[z % 8, f, j] for j in range(4)]
            target[f, index + z, 0], target[f, index + z, 1] = swap_32(a, b, lane)
            target[f, index + z, 2], target[f, index + z, 3] = swap_32(c, d, lane)

    for z in range(HALF + 4):
        if z < HALF:
            first_half(z)
        if z >= 4:
            second_half(z - 4)


def turn_low_body(owner, hold, near_0, near_1, far, q, half):
    turn_half(kept_flags(owner), hold, (near_0, near_1), far, q, 3, half)
    for f in range(F):
        q[f, 0] = q[f, 3]
        q[f, 1] = q[f, 3]
        q[f, 2] = q[f, 3]


def turn_high_body(
    owner, hold, near_0, near_1, far, q_low, after, q, z_own, y_own, z_pair, z_cross, y_near, y_far, half
):
    turn_half(kept_flags(owner), hold, (near_0, near_1), far, q, 5, half)
    odd_z, odd_y = odd("gx"), odd("gy")
    for f in range(F):
        for k in range(5):
            q[f, k] = q_low[f, k + 14]
        q[f, 21] = q[f, 20]
        q[f, 22] = q[f, 20]
        ends = [q_low[f, 3], q_low[f, 4], q[f, 19], q[f, 20]]
        for k in range(4):
            z_own[f, k] = ends[k]
        for k in range(2):
            z_pair[f, k] = jnp.where(odd_z, ends[k], ends[2 + k])
            z_cross[f, k] = jnp.where(odd_z, ends[2 + k], ends[k])
        for b in range(4):
            span = slice(8 * b, 8 * b + 8)
            source, z = (q_low, 8 * b + 3) if b < 2 else (q, 8 * b - 11)
            ends = [source[f, z : z + 8, j, 0 if j < 2 else 7, :] for j in range(4)]
            for k in range(4):
                y_own[f, k, span, :] = ends[k]
            for k in range(2):
                y_near[f, k, span, :] = jnp.where(odd_y, ends[k], ends[2 + k])
                y_far[f, k, span, :] = jnp.where(odd_y, ends[2 + k], ends[k])


def turn(body, name, planes, owner, arrays, others, after=()):
    shapes = [(F, planes, 4, ROWS, LANES)] + others
    return pl.pallas_call(
        body,
        name=name,
        out_shape=tuple(jax.ShapeDtypeStruct(shape, F32) for shape in shapes),
        in_specs=[SMEM] + [VMEM] * (len(arrays) + len(after)),
        out_specs=(VMEM,) * len(shapes),
        scratch_shapes=[pltpu.VMEM((8, F, 4, ROWS, LANES), F32)],
        compiler_params=pltpu.CompilerParams(vmem_limit_bytes=24 << 20),
        cost_estimate=pl.CostEstimate(flops=0, bytes_accessed=6000000, transcendentals=0),
    )(owner, *arrays, *after)


def turn_low(owner, *arrays):
    return turn(turn_low_body, "turn_low", LOW + 10, owner, arrays, [])[0]


def turn_high(owner, after, *arrays):
    z_own, y_own = (F, 4, 4, ROWS, LANES), (F, 4, B, LANES)
    z_half, y_half = (F, 2, 4, ROWS, LANES), (F, 2, B, LANES)
    others = [z_own, y_own, z_half, z_half, y_half, y_half]
    return turn(turn_high_body, "turn_high", B - LOW + 10, owner, arrays, others, (after,))


def minmod(a, b):
    return jnp.maximum(jnp.minimum(a, b), jnp.minimum(jnp.maximum(a, b), 0.0))


def conduction(v):
    return jnp.exp(0.5 * jnp.tanh(v))


LEAD = 5
J = range(4)
LOW = 14


def step_body(
    first, count, chunk, spread, q, *rest,
):
    (
        out, token, result, carry_p, carry_n, carry_c, dx, cx, px, mx, nx, done, turned, sem_out,
    ) = rest[-14:]
    token[...] = jnp.zeros_like(token)
    lane = lax.broadcasted_iota(jnp.int32, (8, LANES), 1)
    sub = lax.broadcasted_iota(jnp.int32, (8, LANES), 0)
    scale = [0.5 * spread[f] for f in range(F)]

    def y_next(value, end):
        return jnp.where(sub == 7, end, pltpu.roll(value, 7, 0))

    def y_last(value, end):
        return jnp.where(sub == 0, end, pltpu.roll(value, 1, 0))

    def leaving(k):
        z = chunk * k
        return [
            pltpu.make_async_copy(
                result.at[c, :, pl.ds(z + LEAD, chunk)],
                out.at[:, pl.ds(first + z, chunk), :, c, 0],
                sem_out.at[k, c],
            )
            for c in range(CAP)
        ]

    def late(i):
        for f in range(F):
            for j in (0, 2):
                result[j, f, i], result[j + 1, f, i] = swap_32(turned[f, j], turned[f, j + 1], lane)
        for f in range(F):
            for j in (0, 1):
                turned[f, j], turned[f, j + 2] = swap_64(done[f, j], done[f, j + 2], lane)

    def middle(i):
        here = [carry_c[j] for j in J]
        above = [conduction(q[5, i + 1, j]) for j in J]
        cond_z = [a + b for a, b in zip(here, above)]
        for j in J:
            carry_c[j] = above[j]
        beyond = here[1:] + [y_next(here[0], here[3])]
        cond_y = [a + b for a, b in zip(here, beyond)]
        v = [q[1, i, j] for j in J]
        beyond = v[1:] + [y_next(v[0], v[3])]
        weight_y = [0.0625 * (a + b) for a, b in zip(v, beyond)]
        weight_z = [0.0625 * (q[2, i, j] + q[2, i + 1, j]) for j in J]
        edge_y = -0.125 * v[0]
        edge_x = [-0.125 * q[0, i, j] for j in J]
        for f in range(F):
            value = [q[f, i, j] for j in J]
            twice = [a + a for a in value]
            total = []
            for j in J:
                after = q[f, i + 1, j]
                d = after - value[j]
                slope = minmod(d, q[f, i + 2, j] - after)
                double = after + after
                state = jnp.where(weight_z[j] > 0.0, carry_p[f, j], double - slope)
                carry_p[f, j] = double + slope
                net = (scale[f] * cond_z[j]) * d - weight_z[j] * state
                total.append(value[j] + (net - carry_n[f, j]))
                carry_n[f, j] = net
            beyond = value[1:] + [y_next(value[0], value[3])]
            d = [b - a for a, b in zip(value, beyond)]
            before = [y_last(d[3], 0.0)] + d[:3]
            slope = [minmod(a, b) for a, b in zip(before, d)]
            right = [a - b for a, b in zip(twice, slope)]
            right = right[1:] + [y_next(right[0], twice[3])]
            net = []
            for j in J:
                state = jnp.where(weight_y[j] > 0.0, twice[j] + slope[j], right[j])
                net.append((scale[f] * cond_y[j]) * d[j] - weight_y[j] * state)
            before = [y_last(net[3], edge_y * twice[0])] + net[:3]
            for j in J:
                n = nx[f, j]
                t = total[j] + (net[j] - before[j])
                before_x = jnp.where(lane == 0, edge_x[j] * twice[j], pltpu.roll(n, 1, 1))
                done[f, j] = t + (n - before_x)
    def early(i):
        here, there = i & 1, (i + 1) & 1
        for j in J:
            u = q[0, i + 1, j]
            weight = 0.0625 * ((u + u) + dx[here, 0, j])
            from_left = (weight > 0.0) | (lane == 127)
            cond = cx[here, j]
            for f in range(F):
                state = jnp.where(from_left, px[f, j], pltpu.roll(mx[f, j], 127, 1))
                nx[f, j] = (scale[f] * cond) * dx[here, f, j] - weight * state
        for j in J:
            for f in range(F):
                a, d = q[f, i + 2, j], dx[there, f, j]
                slope = minmod(pltpu.roll(d, 1, 1), d)
                px[f, j], mx[f, j] = (a + a) + slope, (a + a) - slope
        for j in J:
            c = conduction(q[5, i + 3, j])
            cx[here, j] = c + jnp.where(lane == 127, c, pltpu.roll(c, 127, 1))
            for f in range(F):
                a = q[f, i + 3, j]
                dx[here, f, j] = jnp.where(lane == 127, 0.0, pltpu.roll(a, 127, 1) - a)

    def starting(i, _):
        early(i)
        return 0

    def plane(i, _):
        late(i)
        middle(i)
        early(i)

        @pl.when((i >= chunk + 4) & ((i - 4) % chunk == 0))
        def _():
            for copy in leaving((i - 4) // chunk - 1):
                copy.start()

        return 0

    def ending(i, _):
        late(i)
        return 0

    for j in J:
        carry_c[j] = conduction(q[5, 3, j])
        cond = conduction(q[5, 2, j]) + carry_c[j]
        weight = 0.0625 * (q[2, 2, j] + q[2, 3, j])
        for f in range(F):
            a, b, c, d = [q[f, k, j] for k in range(1, 5)]
            across = c - b
            left = (b + b) + minmod(b - a, across)
            slope = minmod(across, d - c)
            state = jnp.where(weight > 0.0, left, (c + c) - slope)
            carry_p[f, j] = (c + c) + slope
            carry_n[f, j] = (scale[f] * cond) * across - weight * state
    lax.fori_loop(0, 3, starting, 0)
    lax.fori_loop(3, count + 3, plane, 0)
    lax.fori_loop(count + 3, count + LEAD, ending, 0)
    for copy in leaving(count // chunk - 1):
        copy.start()
    for k in range(count // chunk):
        for copy in leaving(k):
            copy.wait()


def step(first, count, chunk, spread, q, out=None):
    planes = lambda *lead: pltpu.VMEM((*lead, ROWS, LANES), F32)
    return pl.pallas_call(
        functools.partial(step_body, first, count, chunk),
        name="step",
        out_shape=(
            jax.ShapeDtypeStruct((F, B, ROWS, CAP, 1, LANES), F32),
            jax.ShapeDtypeStruct((ROWS, LANES), F32),
        ),
        in_specs=[SMEM, VMEM] + ([] if out is None else [HBM]),
        out_specs=(HBM, VMEM),
        input_output_aliases={} if out is None else {2: 0},
        scratch_shapes=[
            planes(CAP, F, count + LEAD),
            planes(F, 4),
            planes(F, 4),
            planes(4),
            planes(2, F, 4),
            planes(2, 4),
            planes(F, 4),
            planes(F, 4),
            planes(F, 4),
            planes(F, 4),
            planes(F, 4),
            pltpu.SemaphoreType.DMA((count // chunk, CAP)),
        ],
        compiler_params=pltpu.CompilerParams(vmem_limit_bytes=24 << 20),
        cost_estimate=pl.CostEstimate(flops=0, bytes_accessed=20000000, transcendentals=0),
    )(spread, q, *(() if out is None else (out,)))


def change(far, out_1, in_0, in_1, u_out, u_0, u_1, c_out, c_0, scale):
    d = in_0 - out_1
    slope = minmod(d, in_1 - in_0)
    inner = -jnp.maximum(0.0625 * (u_0 + u_1), 0.0) * slope
    weight = 0.0625 * (u_out + u_0)
    left = (out_1 + out_1) + minmod(out_1 - far, d)
    right = (in_0 + in_0) - slope
    net = (scale * (c_out + c_0)) * d - weight * jnp.where(weight > 0.0, left, right)
    outer = net + (0.125 * u_0) * (in_0 + in_0)
    return inner - outer, -inner


def both_ends(below, own, above, velocity, has_below, has_above, scale):
    u = [below(velocity, 1)] + [own(velocity, k) for k in range(4)] + [above(velocity, 0)]
    c = [conduction(v) for v in (below(5, 1), own(5, 0), own(5, 3), above(5, 0))]
    result = []
    for f in range(F):
        layers = [own(f, k) for k in range(4)]
        a, b = change(
            below(f, 0), below(f, 1), layers[0], layers[1], u[0], u[1], u[2], c[0], c[1], scale[f]
        )
        e, d = change(
            above(f, 1), above(f, 0), layers[3], layers[2], -u[5], -u[4], -u[3], c[3], c[2], scale[f]
        )
        a, b = jnp.where(has_below, a, 0.0), jnp.where(has_below, b, 0.0)
        d, e = jnp.where(has_above, d, 0.0), jnp.where(has_above, e, 0.0)
        result.append([a, b, d, e])
    return result


def ends_body(
    spread, z_own, y_own, z_pair, z_cross, y_near, y_far, before, out,
    z_add, y_add, planes, first, last, sem, sem_in, sem_out,
):
    gx, gy = lax.axis_index("gx"), lax.axis_index("gy")
    odd_z, odd_y = odd("gx"), odd("gy")
    lane = lax.broadcasted_iota(jnp.int32, (8, LANES), 1)
    sub = lax.broadcasted_iota(jnp.int32, (8, LANES), 0)
    scale = [0.5 * spread[f] for f in range(F)]

    def moves(inward):
        rows, whole = [], []
        for c in range(CAP):
            parts = [
                (out.at[:, :, 0, c, 0], first.at[c], rows),
                (out.at[:, :, 7, c, 0], last.at[c], rows),
                (out.at[:, 0:2, :, c, 0], planes.at[c, :, 0:2], whole),
                (out.at[:, 30:32, :, c, 0], planes.at[c, :, 2:4], whole),
            ]
            for k, (there, here, kind) in enumerate(parts):
                source, target = (there, here) if inward else (here, there)
                kind.append(
                    pltpu.make_async_copy(source, target, (sem_in if inward else sem_out).at[c, k])
                )
        return rows, whole

    rows, whole = moves(True)
    for copy in rows + whole:
        copy.start()

    for j in range(4):
        changes = both_ends(
            lambda f, k: jnp.where(odd_z, z_pair[f, k, j], z_cross[f, k, j]),
            lambda f, k: z_own[f, k, j],
            lambda f, k: jnp.where(odd_z, z_cross[f, k, j], z_pair[f, k, j]),
            2, gx > 0, gx < lax.axis_size("gx") - 1, scale,
        )
        for f in range(F):
            for k in range(4):
                z_add[f, k, j] = changes[f][k]
    for b in range(4):
        span = slice(8 * b, 8 * b + 8)
        changes = both_ends(
            lambda f, k: jnp.where(odd_y, y_near[f, k, span, :], y_far[f, k, span, :]),
            lambda f, k: y_own[f, k, span, :],
            lambda f, k: jnp.where(odd_y, y_far[f, k, span, :], y_near[f, k, span, :]),
            1, gy > 0, gy < lax.axis_size("gy") - 1, scale,
        )
        for f in range(F):
            for c, value in enumerate(turned_to_layers(changes[f], lane)):
                y_add[c, f, span, :] = value

    for copy in rows + whole:
        copy.wait()
    rows_out, whole_out = moves(False)
    for c in range(CAP):
        for f in range(F):
            for b in range(4):
                span = slice(8 * b, 8 * b + 8)
                value = y_add[c, f, span, :]
                first[c, f, span, :] += jnp.where(lane < 64, value, 0.0)
                last[c, f, span, :] += jnp.where(lane >= 64, value, 0.0)
        rows_out[2 * c].start()
        rows_out[2 * c + 1].start()
    corner = ((sub == 0) & (lane < 64)) | ((sub == 7) & (lane >= 64))
    for f in range(F):
        for k, z in enumerate((0, 1, 30, 31)):
            values = turned_to_layers([z_add[f, k, j] for j in range(4)], lane)
            for c in range(CAP):
                planes[c, f, k] += values[c] + jnp.where(corner, y_add[c, f, z : z + 1, :], 0.0)
    for copy in rows_out:
        copy.wait()
    run_all(whole_out)


def ends(spread, *arrays):
    rows = pltpu.VMEM((CAP, F, B, LANES), F32)
    planes = pltpu.VMEM((CAP, F, 4, ROWS, LANES), F32)
    return pl.pallas_call(
        ends_body,
        name="ends",
        out_shape=jax.ShapeDtypeStruct((F, B, ROWS, CAP, 1, LANES), F32),
        in_specs=[SMEM] + [VMEM] * (len(arrays) - 1) + [HBM],
        out_specs=HBM,
        input_output_aliases={len(arrays): 0},
        scratch_shapes=[
            pltpu.VMEM((F, 4, 4, ROWS, LANES), F32),
            rows,
            planes,
            rows,
            rows,
            pltpu.SemaphoreType.DMA((1,)),
            pltpu.SemaphoreType.DMA((CAP, 4)),
            pltpu.SemaphoreType.DMA((CAP, 4)),
        ],
        compiler_params=pltpu.CompilerParams(vmem_limit_bytes=24 << 20),
        cost_estimate=pl.CostEstimate(flops=0, bytes_accessed=6000000, transcendentals=0),
    )(spread, *arrays)


def exchange(block, axes, first, wrap=False):
    count = lax.axis_size(axes)
    pairs = []
    for i in range(first, count, 2):
        j = (i + 1) % count
        if i + 1 < count or wrap:
            pairs += [(i, j), (j, i)]
    return lax.ppermute(block, axes, pairs)


def local(old_state, old_owner, old_slot, diffusivity):
    x = old_state.reshape(8, F, B, ROWS, LANES).transpose(1, 2, 3, 0, 4)[..., None, :]
    far_low, token = far_boxes(x)
    far_high, *nears, hold_low, hold_high = near_boxes(x, token)
    far_low = exchange(far_low, AXES, 1, wrap=True)
    far_high = exchange(far_high, AXES, 1, wrap=True)
    nears = [exchange(near, AXES, 0) for near in nears]
    q_low = turn_low(old_owner, hold_low, *nears[:2], far_low)
    out, token = step(0, LOW, 7, diffusivity, q_low)
    q_high, z_own, y_own, z_pair, z_cross, y_near, y_far = turn_high(
        old_owner, token, hold_high, *nears[2:], far_high, q_low
    )
    y_near = exchange(y_near, "gy", 0)
    y_far = exchange(y_far, "gy", 1)
    z_pair = exchange(z_pair, "gx", 0)
    z_cross = exchange(z_cross, "gx", 1)
    out, _ = step(LOW, B - LOW, 6, diffusivity, q_high, out)
    out = ends(diffusivity, z_own, y_own, z_pair, z_cross, y_near, y_far, out)
    return out[..., 0, :].transpose(3, 0, 1, 2, 4).reshape(CAP, F, B * B * B)


def solution(mesh):
    placed = (P(AXES, None, None), P(), P(), P())
    return jax.shard_map(
        local, mesh=mesh, in_specs=placed, out_specs=P(AXES, None, None), check_vma=False
    )
```

```python
import functools

import jax
import jax.numpy as jnp
from jax import lax
from jax.experimental import pallas as pl
from jax.experimental.pallas import tpu as pltpu
from jax.sharding import PartitionSpec as P

B = 32
F = 6
CAP = 4
HALF = 20
LOW = HALF - 2
PARTS = ((0, HALF // 2), (HALF // 2, HALF), (HALF, (HALF + B) // 2), ((HALF + B) // 2, B))
ROWS = 8
LANES = 128
AXES = ("gx", "gy")
F32 = jnp.float32
HBM = pl.BlockSpec(memory_space=pl.ANY)
VMEM = pl.BlockSpec(memory_space=pltpu.VMEM)
SMEM = pl.BlockSpec(memory_space=pltpu.SMEM)
WIDE = 56 << 20


def run_all(copies):
    for copy in copies:
        copy.start()
    for copy in copies:
        copy.wait()


def odd(axis):
    return lax.axis_index(axis) % 2 == 1


def leaving_copies(x, near, target, planes, sem):
    first = jnp.where(odd("gy"), 0, 6) if near else jnp.where(odd("gy"), 6, 0)
    return [
        pltpu.make_async_copy(x.at[:, planes, :, first + j, 0], target.at[j], sem.at[j])
        for j in range(2)
    ]


def far_body(x, low, token, sem):
    token[...] = jnp.zeros_like(token)
    run_all(leaving_copies(x, False, low, slice(0, HALF), sem))


def near_body(x, after, high, *rest):
    nears, (hold_low, hold_high, sem) = rest[: len(PARTS)], rest[len(PARTS) :]
    copies = leaving_copies(x, False, high, slice(HALF, B), sem.at[2 + len(PARTS)])
    for k, near in enumerate(nears):
        copies += leaving_copies(x, True, near, slice(*PARTS[k]), sem.at[2 + k])
    for k, hold in enumerate((hold_low, hold_high)):
        for c in range(CAP):
            planes = slice(HALF, B) if k else slice(0, HALF)
            copies.append(
                pltpu.make_async_copy(x.at[:, planes, :, 2 + c, 0], hold.at[c], sem.at[k, c])
            )
    run_all(copies)


def from_slots(body, name, arrays, shapes, sems, limit):
    shapes = tuple(jax.ShapeDtypeStruct(shape, F32) for shape in shapes)
    return pl.pallas_call(
        body,
        name=name,
        out_shape=shapes,
        in_specs=[HBM] * len(arrays),
        out_specs=(VMEM,) * len(shapes),
        scratch_shapes=[pltpu.SemaphoreType.DMA(sems)],
        compiler_params=pltpu.CompilerParams(vmem_limit_bytes=limit),
        cost_estimate=pl.CostEstimate(flops=0, bytes_accessed=1000, transcendentals=0),
    )(*arrays)


def far_boxes(x):
    return from_slots(far_body, "far", [x], [(2, F, HALF, ROWS, LANES), (ROWS, LANES)], (2,), WIDE)


def near_boxes(x, after):
    boxes = lambda count, planes: (count, F, planes, ROWS, LANES)
    shapes = [boxes(2, B - HALF)] + [boxes(2, end - start) for start, end in PARTS]
    shapes += [boxes(CAP, HALF), boxes(CAP, B - HALF)]
    return from_slots(near_body, "near", [x, after], shapes, (3 + len(PARTS), CAP), 24 << 20)


def device_number():
    return lax.axis_index("gx") * lax.axis_size("gy") + lax.axis_index("gy")


def kept_flags(owner):
    device = device_number()
    return [owner[device * CAP + c] == device for c in range(CAP)]


def arrived(kept, here, c, far, near):
    from_far = odd("gy") if c >= 2 else jnp.logical_not(odd("gy"))
    return jnp.where(kept, here, jnp.where(from_far, far, near))


def swap_64(a, b, lane):
    low = lane < 64
    m = pltpu.roll(jnp.where(low, b, a), 64, 1)
    return jnp.where(low, a, m), jnp.where(low, m, b)


def swap_32(a, b, lane):
    even = (lane & 32) == 0
    m = jnp.where(even, b, a)
    return jnp.where(even, a, pltpu.roll(m, 32, 1)), jnp.where(even, pltpu.roll(m, 96, 1), b)


def turned_to_layers(v, lane):
    a, c = swap_64(v[0], v[2], lane)
    b, d = swap_64(v[1], v[3], lane)
    return *swap_32(a, b, lane), *swap_32(c, d, lane)


def turn_part(kept, count, hold, nears, far, target, index, half):
    lane = lax.broadcasted_iota(jnp.int32, (8, LANES), 1)

    def first_half(z):
        near = nears[z // (count // 2)]
        for f in range(F):
            v = [
                arrived(kept[c], hold[c, f, z], c, far[c % 2, f, z], near[c % 2, f, z % (count // 2)])
                for c in range(CAP)
            ]
            half[z % 8, f, 0], half[z % 8, f, 2] = swap_64(v[0], v[2], lane)
            half[z % 8, f, 1], half[z % 8, f, 3] = swap_64(v[1], v[3], lane)

    def second_half(z):
        for f in range(F):
            a, b, c, d = [half[z % 8, f, j] for j in range(4)]
            target[f, index + z, 0], target[f, index + z, 1] = swap_32(a, b, lane)
            target[f, index + z, 2], target[f, index + z, 3] = swap_32(c, d, lane)

    for z in range(count + 4):
        if z < count:
            first_half(z)
        if z >= 4:
            second_half(z - 4)


def turn_low_body(owner, hold, near_0, near_1, far, q, half):
    turn_part(kept_flags(owner), HALF, hold, (near_0, near_1), far, q, 3, half)
    for f in range(F):
        q[f, 0] = q[f, 3]
        q[f, 1] = q[f, 3]
        q[f, 2] = q[f, 3]


def turn_high_body(
    owner, hold, near_0, near_1, far, q_low, after, q, z_own, y_own, z_pair, z_cross, y_near, y_far, half
):
    turn_part(kept_flags(owner), B - HALF, hold, (near_0, near_1), far, q, 5, half)
    odd_z, odd_y = odd("gx"), odd("gy")
    for f in range(F):
        for k in range(5):
            q[f, k] = q_low[f, k + LOW]
        top = B + 2 - LOW
        q[f, top + 1] = q[f, top]
        q[f, top + 2] = q[f, top]
        ends = [q_low[f, 3], q_low[f, 4], q[f, top - 1], q[f, top]]
        for k in range(4):
            z_own[f, k] = ends[k]
        for k in range(2):
            z_pair[f, k] = jnp.where(odd_z, ends[k], ends[2 + k])
            z_cross[f, k] = jnp.where(odd_z, ends[2 + k], ends[k])
        for b in range(4):
            span = slice(8 * b, 8 * b + 8)
            source, z = (q_low, 8 * b + 3) if b < 2 else (q, 8 * b + 3 - LOW)
            ends = [source[f, z : z + 8, j, 0 if j < 2 else 7, :] for j in range(4)]
            for k in range(4):
                y_own[f, k, span, :] = ends[k]
            for k in range(2):
                y_near[f, k, span, :] = jnp.where(odd_y, ends[k], ends[2 + k])
                y_far[f, k, span, :] = jnp.where(odd_y, ends[2 + k], ends[k])


def turn(body, name, planes, owner, arrays, others, after=()):
    shapes = [(F, planes, 4, ROWS, LANES)] + others
    return pl.pallas_call(
        body,
        name=name,
        out_shape=tuple(jax.ShapeDtypeStruct(shape, F32) for shape in shapes),
        in_specs=[SMEM] + [VMEM] * (len(arrays) + len(after)),
        out_specs=(VMEM,) * len(shapes),
        scratch_shapes=[pltpu.VMEM((8, F, 4, ROWS, LANES), F32)],
        compiler_params=pltpu.CompilerParams(vmem_limit_bytes=24 << 20),
        cost_estimate=pl.CostEstimate(flops=0, bytes_accessed=6000000, transcendentals=0),
    )(owner, *arrays, *after)


def turn_low(owner, *arrays):
    return turn(turn_low_body, "turn_low", LOW + 10, owner, arrays, [])[0]


def turn_high(owner, after, *arrays):
    z_own, y_own = (F, 4, 4, ROWS, LANES), (F, 4, B, LANES)
    z_half, y_half = (F, 2, 4, ROWS, LANES), (F, 2, B, LANES)
    others = [z_own, y_own, z_half, z_half, y_half, y_half]
    return turn(turn_high_body, "turn_high", B - LOW + 10, owner, arrays, others, (after,))


def minmod(a, b):
    return jnp.maximum(jnp.minimum(a, b), jnp.minimum(jnp.maximum(a, b), 0.0))


def conduction(v):
    return jnp.exp(0.5 * jnp.tanh(v))


LEAD = 5
J = range(4)


def step_body(
    first, count, chunk, spread, q, *rest,
):
    (
        out, token, result, carry_p, carry_n, carry_c, dx, cx, px, mx, nx, done, turned, sem_out,
    ) = rest[-14:]
    token[...] = jnp.zeros_like(token)
    lane = lax.broadcasted_iota(jnp.int32, (8, LANES), 1)
    sub = lax.broadcasted_iota(jnp.int32, (8, LANES), 0)
    scale = [0.5 * spread[f] for f in range(F)]

    def y_next(value, end):
        return jnp.where(sub == 7, end, pltpu.roll(value, 7, 0))

    def y_last(value, end):
        return jnp.where(sub == 0, end, pltpu.roll(value, 1, 0))

    def leaving(k):
        z = chunk * k
        return [
            pltpu.make_async_copy(
                result.at[c, :, pl.ds(z + LEAD, chunk)],
                out.at[:, pl.ds(first + z, chunk), :, c, 0],
                sem_out.at[k, c],
            )
            for c in range(CAP)
        ]

    def late(i):
        for f in range(F):
            for j in (0, 2):
                result[j, f, i], result[j + 1, f, i] = swap_32(turned[f, j], turned[f, j + 1], lane)
        for f in range(F):
            for j in (0, 1):
                turned[f, j], turned[f, j + 2] = swap_64(done[f, j], done[f, j + 2], lane)

    def middle(i):
        here = [carry_c[j] for j in J]
        above = [conduction(q[5, i + 1, j]) for j in J]
        cond_z = [a + b for a, b in zip(here, above)]
        for j in J:
            carry_c[j] = above[j]
        beyond = here[1:] + [y_next(here[0], here[3])]
        cond_y = [a + b for a, b in zip(here, beyond)]
        v = [q[1, i, j] for j in J]
        beyond = v[1:] + [y_next(v[0], v[3])]
        weight_y = [0.0625 * (a + b) for a, b in zip(v, beyond)]
        weight_z = [0.0625 * (q[2, i, j] + q[2, i + 1, j]) for j in J]
        edge_y = -0.125 * v[0]
        edge_x = [-0.125 * q[0, i, j] for j in J]
        for f in range(F):
            value = [q[f, i, j] for j in J]
            twice = [a + a for a in value]
            total = []
            for j in J:
                after = q[f, i + 1, j]
                d = after - value[j]
                slope = minmod(d, q[f, i + 2, j] - after)
                double = after + after
                state = jnp.where(weight_z[j] > 0.0, carry_p[f, j], double - slope)
                carry_p[f, j] = double + slope
                net = (scale[f] * cond_z[j]) * d - weight_z[j] * state
                total.append(value[j] + (net - carry_n[f, j]))
                carry_n[f, j] = net
            beyond = value[1:] + [y_next(value[0], value[3])]
            d = [b - a for a, b in zip(value, beyond)]
            before = [y_last(d[3], 0.0)] + d[:3]
            slope = [minmod(a, b) for a, b in zip(before, d)]
            right = [a - b for a, b in zip(twice, slope)]
            right = right[1:] + [y_next(right[0], twice[3])]
            net = []
            for j in J:
                state = jnp.where(weight_y[j] > 0.0, twice[j] + slope[j], right[j])
                net.append((scale[f] * cond_y[j]) * d[j] - weight_y[j] * state)
            before = [y_last(net[3], edge_y * twice[0])] + net[:3]
            for j in J:
                n = nx[f, j]
                t = total[j] + (net[j] - before[j])
                before_x = jnp.where(lane == 0, edge_x[j] * twice[j], pltpu.roll(n, 1, 1))
                done[f, j] = t + (n - before_x)
    def early(i):
        here, there = i & 1, (i + 1) & 1
        for j in J:
            u = q[0, i + 1, j]
            weight = 0.0625 * ((u + u) + dx[here, 0, j])
            from_left = (weight > 0.0) | (lane == 127)
            cond = cx[here, j]
            for f in range(F):
                state = jnp.where(from_left, px[f, j], pltpu.roll(mx[f, j], 127, 1))
                nx[f, j] = (scale[f] * cond) * dx[here, f, j] - weight * state
        for j in J:
            for f in range(F):
                a, d = q[f, i + 2, j], dx[there, f, j]
                slope = minmod(pltpu.roll(d, 1, 1), d)
                px[f, j], mx[f, j] = (a + a) + slope, (a + a) - slope
        for j in J:
            c = conduction(q[5, i + 3, j])
            cx[here, j] = c + jnp.where(lane == 127, c, pltpu.roll(c, 127, 1))
            for f in range(F):
                a = q[f, i + 3, j]
                dx[here, f, j] = jnp.where(lane == 127, 0.0, pltpu.roll(a, 127, 1) - a)

    def starting(i, _):
        early(i)
        return 0

    def plane(i, _):
        late(i)
        middle(i)
        early(i)

        @pl.when((i >= chunk + 4) & ((i - 4) % chunk == 0))
        def _():
            for copy in leaving((i - 4) // chunk - 1):
                copy.start()

        return 0

    def ending(i, _):
        late(i)
        return 0

    for j in J:
        carry_c[j] = conduction(q[5, 3, j])
        cond = conduction(q[5, 2, j]) + carry_c[j]
        weight = 0.0625 * (q[2, 2, j] + q[2, 3, j])
        for f in range(F):
            a, b, c, d = [q[f, k, j] for k in range(1, 5)]
            across = c - b
            left = (b + b) + minmod(b - a, across)
            slope = minmod(across, d - c)
            state = jnp.where(weight > 0.0, left, (c + c) - slope)
            carry_p[f, j] = (c + c) + slope
            carry_n[f, j] = (scale[f] * cond) * across - weight * state
    lax.fori_loop(0, 3, starting, 0)
    lax.fori_loop(3, count + 3, plane, 0)
    lax.fori_loop(count + 3, count + LEAD, ending, 0)
    for copy in leaving(count // chunk - 1):
        copy.start()
    for k in range(count // chunk):
        for copy in leaving(k):
            copy.wait()


def step(first, count, chunk, spread, q, out=None):
    planes = lambda *lead: pltpu.VMEM((*lead, ROWS, LANES), F32)
    return pl.pallas_call(
        functools.partial(step_body, first, count, chunk),
        name="step",
        out_shape=(
            jax.ShapeDtypeStruct((F, B, ROWS, CAP, 1, LANES), F32),
            jax.ShapeDtypeStruct((ROWS, LANES), F32),
        ),
        in_specs=[SMEM, VMEM] + ([] if out is None else [HBM]),
        out_specs=(HBM, VMEM),
        input_output_aliases={} if out is None else {2: 0},
        scratch_shapes=[
            planes(CAP, F, count + LEAD),
            planes(F, 4),
            planes(F, 4),
            planes(4),
            planes(2, F, 4),
            planes(2, 4),
            planes(F, 4),
            planes(F, 4),
            planes(F, 4),
            planes(F, 4),
            planes(F, 4),
            pltpu.SemaphoreType.DMA((count // chunk, CAP)),
        ],
        compiler_params=pltpu.CompilerParams(vmem_limit_bytes=24 << 20),
        cost_estimate=pl.CostEstimate(flops=0, bytes_accessed=20000000, transcendentals=0),
    )(spread, q, *(() if out is None else (out,)))


def change(far, out_1, in_0, in_1, u_out, u_0, u_1, c_out, c_0, scale):
    d = in_0 - out_1
    slope = minmod(d, in_1 - in_0)
    inner = -jnp.maximum(0.0625 * (u_0 + u_1), 0.0) * slope
    weight = 0.0625 * (u_out + u_0)
    left = (out_1 + out_1) + minmod(out_1 - far, d)
    right = (in_0 + in_0) - slope
    net = (scale * (c_out + c_0)) * d - weight * jnp.where(weight > 0.0, left, right)
    outer = net + (0.125 * u_0) * (in_0 + in_0)
    return inner - outer, -inner


def both_ends(below, own, above, velocity, has_below, has_above, scale):
    u = [below(velocity, 1)] + [own(velocity, k) for k in range(4)] + [above(velocity, 0)]
    c = [conduction(v) for v in (below(5, 1), own(5, 0), own(5, 3), above(5, 0))]
    result = []
    for f in range(F):
        layers = [own(f, k) for k in range(4)]
        a, b = change(
            below(f, 0), below(f, 1), layers[0], layers[1], u[0], u[1], u[2], c[0], c[1], scale[f]
        )
        e, d = change(
            above(f, 1), above(f, 0), layers[3], layers[2], -u[5], -u[4], -u[3], c[3], c[2], scale[f]
        )
        a, b = jnp.where(has_below, a, 0.0), jnp.where(has_below, b, 0.0)
        d, e = jnp.where(has_above, d, 0.0), jnp.where(has_above, e, 0.0)
        result.append([a, b, d, e])
    return result


def ends_body(
    spread, z_own, y_own, z_pair, z_cross, y_near, y_far, before, out,
    z_add, y_add, planes, first, last, sem, sem_in, sem_out,
):
    gx, gy = lax.axis_index("gx"), lax.axis_index("gy")
    odd_z, odd_y = odd("gx"), odd("gy")
    lane = lax.broadcasted_iota(jnp.int32, (8, LANES), 1)
    sub = lax.broadcasted_iota(jnp.int32, (8, LANES), 0)
    scale = [0.5 * spread[f] for f in range(F)]

    def moves(inward):
        rows, whole = [], []
        for c in range(CAP):
            parts = [
                (out.at[:, :, 0, c, 0], first.at[c], rows),
                (out.at[:, :, 7, c, 0], last.at[c], rows),
                (out.at[:, 0:2, :, c, 0], planes.at[c, :, 0:2], whole),
                (out.at[:, 30:32, :, c, 0], planes.at[c, :, 2:4], whole),
            ]
            for k, (there, here, kind) in enumerate(parts):
                source, target = (there, here) if inward else (here, there)
                kind.append(
                    pltpu.make_async_copy(source, target, (sem_in if inward else sem_out).at[c, k])
                )
        return rows, whole

    rows, whole = moves(True)
    for copy in rows + whole:
        copy.start()

    for j in range(4):
        changes = both_ends(
            lambda f, k: jnp.where(odd_z, z_pair[f, k, j], z_cross[f, k, j]),
            lambda f, k: z_own[f, k, j],
            lambda f, k: jnp.where(odd_z, z_cross[f, k, j], z_pair[f, k, j]),
            2, gx > 0, gx < lax.axis_size("gx") - 1, scale,
        )
        for f in range(F):
            for k in range(4):
                z_add[f, k, j] = changes[f][k]
    for b in range(4):
        span = slice(8 * b, 8 * b + 8)
        changes = both_ends(
            lambda f, k: jnp.where(odd_y, y_near[f, k, span, :], y_far[f, k, span, :]),
            lambda f, k: y_own[f, k, span, :],
            lambda f, k: jnp.where(odd_y, y_far[f, k, span, :], y_near[f, k, span, :]),
            1, gy > 0, gy < lax.axis_size("gy") - 1, scale,
        )
        for f in range(F):
            for c, value in enumerate(turned_to_layers(changes[f], lane)):
                y_add[c, f, span, :] = value

    for copy in rows + whole:
        copy.wait()
    rows_out, whole_out = moves(False)
    for c in range(CAP):
        for f in range(F):
            for b in range(4):
                span = slice(8 * b, 8 * b + 8)
                value = y_add[c, f, span, :]
                first[c, f, span, :] += jnp.where(lane < 64, value, 0.0)
                last[c, f, span, :] += jnp.where(lane >= 64, value, 0.0)
        rows_out[2 * c].start()
        rows_out[2 * c + 1].start()
    corner = ((sub == 0) & (lane < 64)) | ((sub == 7) & (lane >= 64))
    for f in range(F):
        for k, z in enumerate((0, 1, 30, 31)):
            values = turned_to_layers([z_add[f, k, j] for j in range(4)], lane)
            for c in range(CAP):
                planes[c, f, k] += values[c] + jnp.where(corner, y_add[c, f, z : z + 1, :], 0.0)
    for copy in rows_out:
        copy.wait()
    run_all(whole_out)


def ends(spread, *arrays):
    rows = pltpu.VMEM((CAP, F, B, LANES), F32)
    planes = pltpu.VMEM((CAP, F, 4, ROWS, LANES), F32)
    return pl.pallas_call(
        ends_body,
        name="ends",
        out_shape=jax.ShapeDtypeStruct((F, B, ROWS, CAP, 1, LANES), F32),
        in_specs=[SMEM] + [VMEM] * (len(arrays) - 1) + [HBM],
        out_specs=HBM,
        input_output_aliases={len(arrays): 0},
        scratch_shapes=[
            pltpu.VMEM((F, 4, 4, ROWS, LANES), F32),
            rows,
            planes,
            rows,
            rows,
            pltpu.SemaphoreType.DMA((1,)),
            pltpu.SemaphoreType.DMA((CAP, 4)),
            pltpu.SemaphoreType.DMA((CAP, 4)),
        ],
        compiler_params=pltpu.CompilerParams(vmem_limit_bytes=24 << 20),
        cost_estimate=pl.CostEstimate(flops=0, bytes_accessed=6000000, transcendentals=0),
    )(spread, *arrays)


def exchange(block, axes, first, wrap=False):
    count = lax.axis_size(axes)
    pairs = []
    for i in range(first, count, 2):
        j = (i + 1) % count
        if i + 1 < count or wrap:
            pairs += [(i, j), (j, i)]
    return lax.ppermute(block, axes, pairs)


def local(old_state, old_owner, old_slot, diffusivity):
    x = old_state.reshape(8, F, B, ROWS, LANES).transpose(1, 2, 3, 0, 4)[..., None, :]
    far_low, token = far_boxes(x)
    far_high, *nears, hold_low, hold_high = near_boxes(x, token)
    far_low = exchange(far_low, AXES, 1, wrap=True)
    far_high = exchange(far_high, AXES, 1, wrap=True)
    nears = [exchange(near, AXES, 0) for near in nears]
    q_low = turn_low(old_owner, hold_low, *nears[:2], far_low)
    out, token = step(0, LOW, 9, diffusivity, q_low)
    q_high, z_own, y_own, z_pair, z_cross, y_near, y_far = turn_high(
        old_owner, token, hold_high, *nears[2:], far_high, q_low
    )
    y_near = exchange(y_near, "gy", 0)
    y_far = exchange(y_far, "gy", 1)
    z_pair = exchange(z_pair, "gx", 0)
    z_cross = exchange(z_cross, "gx", 1)
    out, _ = step(LOW, B - LOW, 7, diffusivity, q_high, out)
    out = ends(diffusivity, z_own, y_own, z_pair, z_cross, y_near, y_far, out)
    return out[..., 0, :].transpose(3, 0, 1, 2, 4).reshape(CAP, F, B * B * B)


def solution(mesh):
    placed = (P(AXES, None, None), P(), P(), P())
    return jax.shard_map(
        local, mesh=mesh, in_specs=placed, out_specs=P(AXES, None, None), check_vma=False
    )
```

```python
import functools

import jax
import jax.numpy as jnp
from jax import lax
from jax.experimental import pallas as pl
from jax.experimental.pallas import tpu as pltpu
from jax.sharding import PartitionSpec as P

B = 32
F = 6
CAP = 4
HALF = 20
LOW = HALF - 2
PARTS = ((0, HALF // 2), (HALF // 2, HALF), (HALF, (HALF + B) // 2), ((HALF + B) // 2, B))
ROWS = 8
LANES = 128
AXES = ("gx", "gy")
F32 = jnp.float32
HBM = pl.BlockSpec(memory_space=pl.ANY)
VMEM = pl.BlockSpec(memory_space=pltpu.VMEM)
SMEM = pl.BlockSpec(memory_space=pltpu.SMEM)
WIDE = 56 << 20


def run_all(copies):
    for copy in copies:
        copy.start()
    for copy in copies:
        copy.wait()


def odd(axis):
    return lax.axis_index(axis) % 2 == 1


def leaving_copies(x, near, target, planes, sem):
    first = jnp.where(odd("gy"), 0, 6) if near else jnp.where(odd("gy"), 6, 0)
    return [
        pltpu.make_async_copy(x.at[:, planes, :, first + j, 0], target.at[j], sem.at[j])
        for j in range(2)
    ]


def far_body(x, low, token, sem):
    token[...] = jnp.zeros_like(token)
    run_all(leaving_copies(x, False, low, slice(0, HALF), sem))


def near_body(x, after, high, *rest):
    nears, (hold_low, hold_high, sem) = rest[: len(PARTS)], rest[len(PARTS) :]
    copies = leaving_copies(x, False, high, slice(HALF, B), sem.at[2 + len(PARTS)])
    for k, near in enumerate(nears):
        copies += leaving_copies(x, True, near, slice(*PARTS[k]), sem.at[2 + k])
    for k, hold in enumerate((hold_low, hold_high)):
        for c in range(CAP):
            planes = slice(HALF, B) if k else slice(0, HALF)
            copies.append(
                pltpu.make_async_copy(x.at[:, planes, :, 2 + c, 0], hold.at[c], sem.at[k, c])
            )
    run_all(copies)


def from_slots(body, name, arrays, shapes, sems, limit):
    shapes = tuple(jax.ShapeDtypeStruct(shape, F32) for shape in shapes)
    return pl.pallas_call(
        body,
        name=name,
        out_shape=shapes,
        in_specs=[HBM] * len(arrays),
        out_specs=(VMEM,) * len(shapes),
        scratch_shapes=[pltpu.SemaphoreType.DMA(sems)],
        compiler_params=pltpu.CompilerParams(vmem_limit_bytes=limit),
        cost_estimate=pl.CostEstimate(flops=0, bytes_accessed=1000, transcendentals=0),
    )(*arrays)


def far_boxes(x):
    return from_slots(far_body, "far", [x], [(2, F, HALF, ROWS, LANES), (ROWS, LANES)], (2,), WIDE)


def near_boxes(x, after):
    boxes = lambda count, planes: (count, F, planes, ROWS, LANES)
    shapes = [boxes(2, B - HALF)] + [boxes(2, end - start) for start, end in PARTS]
    shapes += [boxes(CAP, HALF), boxes(CAP, B - HALF)]
    return from_slots(near_body, "near", [x, after], shapes, (3 + len(PARTS), CAP), 24 << 20)


def device_number():
    return lax.axis_index("gx") * lax.axis_size("gy") + lax.axis_index("gy")


def kept_flags(owner):
    device = device_number()
    return [owner[device * CAP + c] == device for c in range(CAP)]


def arrived(kept, here, c, far, near):
    from_far = odd("gy") if c >= 2 else jnp.logical_not(odd("gy"))
    return jnp.where(kept, here, jnp.where(from_far, far, near))


def swap_64(a, b, lane):
    low = lane < 64
    m = pltpu.roll(jnp.where(low, b, a), 64, 1)
    return jnp.where(low, a, m), jnp.where(low, m, b)


def swap_32(a, b, lane):
    even = (lane & 32) == 0
    m = jnp.where(even, b, a)
    return jnp.where(even, a, pltpu.roll(m, 32, 1)), jnp.where(even, pltpu.roll(m, 96, 1), b)


def turned_to_layers(v, lane):
    a, c = swap_64(v[0], v[2], lane)
    b, d = swap_64(v[1], v[3], lane)
    return *swap_32(a, b, lane), *swap_32(c, d, lane)


def turn_part(kept, count, hold, nears, far, target, index, half):
    lane = lax.broadcasted_iota(jnp.int32, (8, LANES), 1)

    def first_half(z):
        near = nears[z // (count // 2)]
        for f in range(F):
            v = [
                arrived(kept[c], hold[c, f, z], c, far[c % 2, f, z], near[c % 2, f, z % (count // 2)])
                for c in range(CAP)
            ]
            half[z % 8, f, 0], half[z % 8, f, 2] = swap_64(v[0], v[2], lane)
            half[z % 8, f, 1], half[z % 8, f, 3] = swap_64(v[1], v[3], lane)

    def second_half(z):
        for f in range(F):
            a, b, c, d = [half[z % 8, f, j] for j in range(4)]
            target[f, index + z, 0], target[f, index + z, 1] = swap_32(a, b, lane)
            target[f, index + z, 2], target[f, index + z, 3] = swap_32(c, d, lane)

    for z in range(count + 4):
        if z < count:
            first_half(z)
        if z >= 4:
            second_half(z - 4)


def turn_low_body(owner, hold, near_0, near_1, far, q, half):
    turn_part(kept_flags(owner), HALF, hold, (near_0, near_1), far, q, 3, half)
    for f in range(F):
        q[f, 0] = q[f, 3]
        q[f, 1] = q[f, 3]
        q[f, 2] = q[f, 3]


def turn_high_body(
    owner, hold, near_0, near_1, far, q_low, after, q, z_own, y_own, z_pair, z_cross, y_near, y_far, half
):
    turn_part(kept_flags(owner), B - HALF, hold, (near_0, near_1), far, q, 5, half)
    odd_z, odd_y = odd("gx"), odd("gy")
    for f in range(F):
        for k in range(5):
            q[f, k] = q_low[f, k + LOW]
        top = B + 2 - LOW
        q[f, top + 1] = q[f, top]
        q[f, top + 2] = q[f, top]
        ends = [q_low[f, 3], q_low[f, 4], q[f, top - 1], q[f, top]]
        for k in range(4):
            z_own[f, k] = ends[k]
        for k in range(2):
            z_pair[f, k] = jnp.where(odd_z, ends[k], ends[2 + k])
            z_cross[f, k] = jnp.where(odd_z, ends[2 + k], ends[k])
        for b in range(4):
            span = slice(8 * b, 8 * b + 8)
            source, z = (q_low, 8 * b + 3) if b < 2 else (q, 8 * b + 3 - LOW)
            ends = [source[f, z : z + 8, j, 0 if j < 2 else 7, :] for j in range(4)]
            for k in range(4):
                y_own[f, k, span, :] = ends[k]
            for k in range(2):
                y_near[f, k, span, :] = jnp.where(odd_y, ends[k], ends[2 + k])
                y_far[f, k, span, :] = jnp.where(odd_y, ends[2 + k], ends[k])


def turn(body, name, planes, owner, arrays, others, after=()):
    shapes = [(F, planes, 4, ROWS, LANES)] + others
    return pl.pallas_call(
        body,
        name=name,
        out_shape=tuple(jax.ShapeDtypeStruct(shape, F32) for shape in shapes),
        in_specs=[SMEM] + [VMEM] * (len(arrays) + len(after)),
        out_specs=(VMEM,) * len(shapes),
        scratch_shapes=[pltpu.VMEM((8, F, 4, ROWS, LANES), F32)],
        compiler_params=pltpu.CompilerParams(vmem_limit_bytes=24 << 20),
        cost_estimate=pl.CostEstimate(flops=0, bytes_accessed=6000000, transcendentals=0),
    )(owner, *arrays, *after)


def turn_low(owner, *arrays):
    return turn(turn_low_body, "turn_low", LOW + 10, owner, arrays, [])[0]


def turn_high(owner, after, *arrays):
    z_own, y_own = (F, 4, 4, ROWS, LANES), (F, 4, B, LANES)
    z_half, y_half = (F, 2, 4, ROWS, LANES), (F, 2, B, LANES)
    others = [z_own, y_own, z_half, z_half, y_half, y_half]
    return turn(turn_high_body, "turn_high", B - LOW + 10, owner, arrays, others, (after,))


def minmod(a, b):
    return jnp.maximum(jnp.minimum(a, b), jnp.minimum(jnp.maximum(a, b), 0.0))


def conduction(v):
    return jnp.exp(0.5 * jnp.tanh(v))


LEAD = 5
J = range(4)


def step_body(
    first, count, chunk, spread, q, *rest,
):
    (
        out, token, result, carry_p, carry_n, carry_c, dx, cx, px, mx, nx, done, turned, sem_out,
    ) = rest[-14:]
    token[...] = jnp.zeros_like(token)
    lane = lax.broadcasted_iota(jnp.int32, (8, LANES), 1)
    sub = lax.broadcasted_iota(jnp.int32, (8, LANES), 0)
    scale = [0.5 * spread[f] for f in range(F)]

    def y_next(value, end):
        return jnp.where(sub == 7, end, pltpu.roll(value, 7, 0))

    def y_last(value, end):
        return jnp.where(sub == 0, end, pltpu.roll(value, 1, 0))

    def leaving(k):
        z = chunk * k
        return [
            pltpu.make_async_copy(
                result.at[c, :, pl.ds(z + LEAD, chunk)],
                out.at[:, pl.ds(first + z, chunk), :, c, 0],
                sem_out.at[k, c],
            )
            for c in range(CAP)
        ]

    def late(i):
        for f in range(F):
            for j in (0, 2):
                result[j, f, i], result[j + 1, f, i] = swap_32(turned[f, j], turned[f, j + 1], lane)
        for f in range(F):
            for j in (0, 1):
                turned[f, j], turned[f, j + 2] = swap_64(done[f, j], done[f, j + 2], lane)

    def middle(i):
        here = [carry_c[j] for j in J]
        above = [conduction(q[5, i + 1, j]) for j in J]
        cond_z = [a + b for a, b in zip(here, above)]
        for j in J:
            carry_c[j] = above[j]
        beyond = here[1:] + [y_next(here[0], here[3])]
        cond_y = [a + b for a, b in zip(here, beyond)]
        v = [q[1, i, j] for j in J]
        beyond = v[1:] + [y_next(v[0], v[3])]
        weight_y = [0.0625 * (a + b) for a, b in zip(v, beyond)]
        weight_z = [0.0625 * (q[2, i, j] + q[2, i + 1, j]) for j in J]
        edge_y = -0.125 * v[0]
        edge_x = [-0.125 * q[0, i, j] for j in J]
        for f in range(F):
            value = [q[f, i, j] for j in J]
            twice = [a + a for a in value]
            total = []
            for j in J:
                after = q[f, i + 1, j]
                d = after - value[j]
                slope = minmod(d, q[f, i + 2, j] - after)
                double = after + after
                state = jnp.where(weight_z[j] > 0.0, carry_p[f, j], double - slope)
                carry_p[f, j] = double + slope
                net = (scale[f] * cond_z[j]) * d - weight_z[j] * state
                total.append(value[j] + (net - carry_n[f, j]))
                carry_n[f, j] = net
            beyond = value[1:] + [y_next(value[0], value[3])]
            d = [b - a for a, b in zip(value, beyond)]
            before = [y_last(d[3], 0.0)] + d[:3]
            slope = [minmod(a, b) for a, b in zip(before, d)]
            right = [a - b for a, b in zip(twice, slope)]
            right = right[1:] + [y_next(right[0], twice[3])]
            net = []
            for j in J:
                state = jnp.where(weight_y[j] > 0.0, twice[j] + slope[j], right[j])
                net.append((scale[f] * cond_y[j]) * d[j] - weight_y[j] * state)
            before = [y_last(net[3], edge_y * twice[0])] + net[:3]
            for j in J:
                n = nx[f, j]
                t = total[j] + (net[j] - before[j])
                before_x = jnp.where(lane == 0, edge_x[j] * twice[j], pltpu.roll(n, 1, 1))
                done[f, j] = t + (n - before_x)
    def early(i):
        here, there = i & 1, (i + 1) & 1
        for j in J:
            u = q[0, i + 1, j]
            weight = 0.0625 * ((u + u) + dx[here, 0, j])
            from_left = (weight > 0.0) | (lane == 127)
            cond = cx[here, j]
            for f in range(F):
                state = jnp.where(from_left, px[f, j], pltpu.roll(mx[f, j], 127, 1))
                nx[f, j] = (scale[f] * cond) * dx[here, f, j] - weight * state
        for j in J:
            for f in range(F):
                a, d = q[f, i + 2, j], dx[there, f, j]
                slope = minmod(pltpu.roll(d, 1, 1), d)
                px[f, j], mx[f, j] = (a + a) + slope, (a + a) - slope
        for j in J:
            c = conduction(q[5, i + 3, j])
            cx[here, j] = c + jnp.where(lane == 127, c, pltpu.roll(c, 127, 1))
            for f in range(F):
                a = q[f, i + 3, j]
                dx[here, f, j] = jnp.where(lane == 127, 0.0, pltpu.roll(a, 127, 1) - a)

    def starting(i, _):
        early(i)
        return 0

    def plane(i, _):
        late(i)
        middle(i)
        early(i)

        @pl.when((i >= chunk + 4) & ((i - 4) % chunk == 0))
        def _():
            for copy in leaving((i - 4) // chunk - 1):
                copy.start()

        return 0

    def ending(i, _):
        late(i)
        return 0

    for j in J:
        carry_c[j] = conduction(q[5, 3, j])
        cond = conduction(q[5, 2, j]) + carry_c[j]
        weight = 0.0625 * (q[2, 2, j] + q[2, 3, j])
        for f in range(F):
            a, b, c, d = [q[f, k, j] for k in range(1, 5)]
            across = c - b
            left = (b + b) + minmod(b - a, across)
            slope = minmod(across, d - c)
            state = jnp.where(weight > 0.0, left, (c + c) - slope)
            carry_p[f, j] = (c + c) + slope
            carry_n[f, j] = (scale[f] * cond) * across - weight * state
    lax.fori_loop(0, 3, starting, 0)
    lax.fori_loop(3, count + 3, plane, 0)
    lax.fori_loop(count + 3, count + LEAD, ending, 0)
    for copy in leaving(count // chunk - 1):
        copy.start()
    for k in range(count // chunk):
        for copy in leaving(k):
            copy.wait()


def step(first, count, chunk, spread, q, out=None):
    planes = lambda *lead: pltpu.VMEM((*lead, ROWS, LANES), F32)
    return pl.pallas_call(
        functools.partial(step_body, first, count, chunk),
        name="step",
        out_shape=(
            jax.ShapeDtypeStruct((F, B, ROWS, CAP, 1, LANES), F32),
            jax.ShapeDtypeStruct((ROWS, LANES), F32),
        ),
        in_specs=[SMEM, VMEM] + ([] if out is None else [HBM]),
        out_specs=(HBM, VMEM),
        input_output_aliases={} if out is None else {2: 0},
        scratch_shapes=[
            planes(CAP, F, count + LEAD),
            planes(F, 4),
            planes(F, 4),
            planes(4),
            planes(2, F, 4),
            planes(2, 4),
            planes(F, 4),
            planes(F, 4),
            planes(F, 4),
            planes(F, 4),
            planes(F, 4),
            pltpu.SemaphoreType.DMA((count // chunk, CAP)),
        ],
        compiler_params=pltpu.CompilerParams(vmem_limit_bytes=24 << 20),
        cost_estimate=pl.CostEstimate(flops=0, bytes_accessed=20000000, transcendentals=0),
    )(spread, q, *(() if out is None else (out,)))


def change(far, out_1, in_0, in_1, u_out, u_0, u_1, c_out, c_0, scale):
    d = in_0 - out_1
    slope = minmod(d, in_1 - in_0)
    inner = -jnp.maximum(0.0625 * (u_0 + u_1), 0.0) * slope
    weight = 0.0625 * (u_out + u_0)
    left = (out_1 + out_1) + minmod(out_1 - far, d)
    right = (in_0 + in_0) - slope
    net = (scale * (c_out + c_0)) * d - weight * jnp.where(weight > 0.0, left, right)
    outer = net + (0.125 * u_0) * (in_0 + in_0)
    return inner - outer, -inner


def both_ends(below, own, above, velocity, has_below, has_above, scale):
    u = [below(velocity, 1)] + [own(velocity, k) for k in range(4)] + [above(velocity, 0)]
    c = [conduction(v) for v in (below(5, 1), own(5, 0), own(5, 3), above(5, 0))]
    result = []
    for f in range(F):
        layers = [own(f, k) for k in range(4)]
        a, b = change(
            below(f, 0), below(f, 1), layers[0], layers[1], u[0], u[1], u[2], c[0], c[1], scale[f]
        )
        e, d = change(
            above(f, 1), above(f, 0), layers[3], layers[2], -u[5], -u[4], -u[3], c[3], c[2], scale[f]
        )
        a, b = jnp.where(has_below, a, 0.0), jnp.where(has_below, b, 0.0)
        d, e = jnp.where(has_above, d, 0.0), jnp.where(has_above, e, 0.0)
        result.append([a, b, d, e])
    return result


def ends_body(
    spread, z_own, y_own, y_far, z_pair, z_cross, y_near, before, out,
    z_add, y_add, planes, first, last, sem, sem_in, sem_out,
):
    gx, gy = lax.axis_index("gx"), lax.axis_index("gy")
    odd_z, odd_y = odd("gx"), odd("gy")
    lane = lax.broadcasted_iota(jnp.int32, (8, LANES), 1)
    sub = lax.broadcasted_iota(jnp.int32, (8, LANES), 0)
    scale = [0.5 * spread[f] for f in range(F)]

    def moves(inward):
        rows, whole = [], []
        for c in range(CAP):
            parts = [
                (out.at[:, :, 0, c, 0], first.at[c], rows),
                (out.at[:, :, 7, c, 0], last.at[c], rows),
                (out.at[:, 0:2, :, c, 0], planes.at[c, :, 0:2], whole),
                (out.at[:, 30:32, :, c, 0], planes.at[c, :, 2:4], whole),
            ]
            for k, (there, here, kind) in enumerate(parts):
                source, target = (there, here) if inward else (here, there)
                kind.append(
                    pltpu.make_async_copy(source, target, (sem_in if inward else sem_out).at[c, k])
                )
        return rows, whole

    rows, whole = moves(True)
    for copy in rows + whole:
        copy.start()

    for j in range(4):
        changes = both_ends(
            lambda f, k: jnp.where(odd_z, z_pair[f, k, j], z_cross[f, k, j]),
            lambda f, k: z_own[f, k, j],
            lambda f, k: jnp.where(odd_z, z_cross[f, k, j], z_pair[f, k, j]),
            2, gx > 0, gx < lax.axis_size("gx") - 1, scale,
        )
        for f in range(F):
            for k in range(4):
                z_add[f, k, j] = changes[f][k]
    for b in range(4):
        span = slice(8 * b, 8 * b + 8)
        changes = both_ends(
            lambda f, k: jnp.where(odd_y, y_near[f, k, span, :], y_far[f, k, span, :]),
            lambda f, k: y_own[f, k, span, :],
            lambda f, k: jnp.where(odd_y, y_far[f, k, span, :], y_near[f, k, span, :]),
            1, gy > 0, gy < lax.axis_size("gy") - 1, scale,
        )
        for f in range(F):
            for c, value in enumerate(turned_to_layers(changes[f], lane)):
                y_add[c, f, span, :] = value

    for copy in rows + whole:
        copy.wait()
    rows_out, whole_out = moves(False)
    for c in range(CAP):
        for f in range(F):
            for b in range(4):
                span = slice(8 * b, 8 * b + 8)
                value = y_add[c, f, span, :]
                first[c, f, span, :] += jnp.where(lane < 64, value, 0.0)
                last[c, f, span, :] += jnp.where(lane >= 64, value, 0.0)
        rows_out[2 * c].start()
        rows_out[2 * c + 1].start()
    corner = ((sub == 0) & (lane < 64)) | ((sub == 7) & (lane >= 64))
    for f in range(F):
        for k, z in enumerate((0, 1, 30, 31)):
            values = turned_to_layers([z_add[f, k, j] for j in range(4)], lane)
            for c in range(CAP):
                planes[c, f, k] += values[c] + jnp.where(corner, y_add[c, f, z : z + 1, :], 0.0)
    for copy in rows_out:
        copy.wait()
    run_all(whole_out)


def ends(spread, *arrays):
    rows = pltpu.VMEM((CAP, F, B, LANES), F32)
    planes = pltpu.VMEM((CAP, F, 4, ROWS, LANES), F32)
    return pl.pallas_call(
        ends_body,
        name="ends",
        out_shape=jax.ShapeDtypeStruct((F, B, ROWS, CAP, 1, LANES), F32),
        in_specs=[SMEM] + [VMEM] * (len(arrays) - 1) + [HBM],
        out_specs=HBM,
        input_output_aliases={len(arrays): 0},
        scratch_shapes=[
            pltpu.VMEM((F, 4, 4, ROWS, LANES), F32),
            rows,
            planes,
            rows,
            rows,
            pltpu.SemaphoreType.DMA((1,)),
            pltpu.SemaphoreType.DMA((CAP, 4)),
            pltpu.SemaphoreType.DMA((CAP, 4)),
        ],
        compiler_params=pltpu.CompilerParams(vmem_limit_bytes=24 << 20),
        cost_estimate=pl.CostEstimate(flops=0, bytes_accessed=6000000, transcendentals=0),
    )(spread, *arrays)


def exchange(block, axes, first, wrap=False):
    count = lax.axis_size(axes)
    pairs = []
    for i in range(first, count, 2):
        j = (i + 1) % count
        if i + 1 < count or wrap:
            pairs += [(i, j), (j, i)]
    return lax.ppermute(block, axes, pairs)


def local(old_state, old_owner, old_slot, diffusivity):
    x = old_state.reshape(8, F, B, ROWS, LANES).transpose(1, 2, 3, 0, 4)[..., None, :]
    far_low, token = far_boxes(x)
    far_high, *nears, hold_low, hold_high = near_boxes(x, token)
    far_low = exchange(far_low, AXES, 1, wrap=True)
    far_high = exchange(far_high, AXES, 1, wrap=True)
    nears = [exchange(near, AXES, 0) for near in nears]
    q_low = turn_low(old_owner, hold_low, *nears[:2], far_low)
    out, token = step(0, LOW, 9, diffusivity, q_low)
    q_high, z_own, y_own, z_pair, z_cross, y_near, y_far = turn_high(
        old_owner, token, hold_high, *nears[2:], far_high, q_low
    )
    y_near = exchange(y_near, "gy", 0)
    y_far = exchange(y_far, "gy", 1)
    z_pair = exchange(z_pair, "gx", 0)
    z_cross = exchange(z_cross, "gx", 1)
    out, _ = step(LOW, B - LOW, 7, diffusivity, q_high, out)
    out = ends(diffusivity, z_own, y_own, y_far, z_pair, z_cross, y_near, out)
    return out[..., 0, :].transpose(3, 0, 1, 2, 4).reshape(CAP, F, B * B * B)


def solution(mesh):
    placed = (P(AXES, None, None), P(), P(), P())
    return jax.shard_map(
        local, mesh=mesh, in_specs=placed, out_specs=P(AXES, None, None), check_vma=False
    )
```

```python
import functools

import jax
import jax.numpy as jnp
from jax import lax
from jax.experimental import pallas as pl
from jax.experimental.pallas import tpu as pltpu
from jax.sharding import PartitionSpec as P

B = 32
F = 6
CAP = 4
HALF = 18
LOW = HALF - 2
PARTS = ((0, HALF // 2), (HALF // 2, HALF), (HALF, (HALF + B) // 2), ((HALF + B) // 2, B))
ROWS = 8
LANES = 128
AXES = ("gx", "gy")
F32 = jnp.float32
HBM = pl.BlockSpec(memory_space=pl.ANY)
VMEM = pl.BlockSpec(memory_space=pltpu.VMEM)
SMEM = pl.BlockSpec(memory_space=pltpu.SMEM)
WIDE = 56 << 20


def run_all(copies):
    for copy in copies:
        copy.start()
    for copy in copies:
        copy.wait()


def odd(axis):
    return lax.axis_index(axis) % 2 == 1


def leaving_copies(x, near, target, planes, sem):
    first = jnp.where(odd("gy"), 0, 6) if near else jnp.where(odd("gy"), 6, 0)
    return [
        pltpu.make_async_copy(x.at[:, planes, :, first + j, 0], target.at[j], sem.at[j])
        for j in range(2)
    ]


def far_body(x, low, token, sem):
    token[...] = jnp.zeros_like(token)
    run_all(leaving_copies(x, False, low, slice(0, HALF), sem))


def near_body(x, after, high, *rest):
    nears, (hold_low, hold_high, sem) = rest[: len(PARTS)], rest[len(PARTS) :]
    copies = leaving_copies(x, False, high, slice(HALF, B), sem.at[2 + len(PARTS)])
    for k, near in enumerate(nears):
        copies += leaving_copies(x, True, near, slice(*PARTS[k]), sem.at[2 + k])
    for k, hold in enumerate((hold_low, hold_high)):
        for c in range(CAP):
            planes = slice(HALF, B) if k else slice(0, HALF)
            copies.append(
                pltpu.make_async_copy(x.at[:, planes, :, 2 + c, 0], hold.at[c], sem.at[k, c])
            )
    run_all(copies)


def from_slots(body, name, arrays, shapes, sems, limit):
    shapes = tuple(jax.ShapeDtypeStruct(shape, F32) for shape in shapes)
    return pl.pallas_call(
        body,
        name=name,
        out_shape=shapes,
        in_specs=[HBM] * len(arrays),
        out_specs=(VMEM,) * len(shapes),
        scratch_shapes=[pltpu.SemaphoreType.DMA(sems)],
        compiler_params=pltpu.CompilerParams(vmem_limit_bytes=limit),
        cost_estimate=pl.CostEstimate(flops=0, bytes_accessed=1000, transcendentals=0),
    )(*arrays)


def far_boxes(x):
    return from_slots(far_body, "far", [x], [(2, F, HALF, ROWS, LANES), (ROWS, LANES)], (2,), WIDE)


def near_boxes(x, after):
    boxes = lambda count, planes: (count, F, planes, ROWS, LANES)
    shapes = [boxes(2, B - HALF)] + [boxes(2, end - start) for start, end in PARTS]
    shapes += [boxes(CAP, HALF), boxes(CAP, B - HALF)]
    return from_slots(near_body, "near", [x, after], shapes, (3 + len(PARTS), CAP), 24 << 20)


def device_number():
    return lax.axis_index("gx") * lax.axis_size("gy") + lax.axis_index("gy")


def kept_flags(owner):
    device = device_number()
    return [owner[device * CAP + c] == device for c in range(CAP)]


def arrived(kept, here, c, far, near):
    from_far = odd("gy") if c >= 2 else jnp.logical_not(odd("gy"))
    return jnp.where(kept, here, jnp.where(from_far, far, near))


def swap_64(a, b, lane):
    low = lane < 64
    m = pltpu.roll(jnp.where(low, b, a), 64, 1)
    return jnp.where(low, a, m), jnp.where(low, m, b)


def swap_32(a, b, lane):
    even = (lane & 32) == 0
    m = jnp.where(even, b, a)
    return jnp.where(even, a, pltpu.roll(m, 32, 1)), jnp.where(even, pltpu.roll(m, 96, 1), b)


def turned_to_layers(v, lane):
    a, c = swap_64(v[0], v[2], lane)
    b, d = swap_64(v[1], v[3], lane)
    return *swap_32(a, b, lane), *swap_32(c, d, lane)


def turn_part(kept, count, hold, nears, far, target, index, half):
    lane = lax.broadcasted_iota(jnp.int32, (8, LANES), 1)

    def first_half(z):
        near = nears[z // (count // 2)]
        for f in range(F):
            v = [
                arrived(kept[c], hold[c, f, z], c, far[c % 2, f, z], near[c % 2, f, z % (count // 2)])
                for c in range(CAP)
            ]
            half[z % 8, f, 0], half[z % 8, f, 2] = swap_64(v[0], v[2], lane)
            half[z % 8, f, 1], half[z % 8, f, 3] = swap_64(v[1], v[3], lane)

    def second_half(z):
        for f in range(F):
            a, b, c, d = [half[z % 8, f, j] for j in range(4)]
            target[f, index + z, 0], target[f, index + z, 1] = swap_32(a, b, lane)
            target[f, index + z, 2], target[f, index + z, 3] = swap_32(c, d, lane)

    for z in range(count + 4):
        if z < count:
            first_half(z)
        if z >= 4:
            second_half(z - 4)


def turn_low_body(owner, hold, near_0, near_1, far, q, half):
    turn_part(kept_flags(owner), HALF, hold, (near_0, near_1), far, q, 3, half)
    for f in range(F):
        q[f, 0] = q[f, 3]
        q[f, 1] = q[f, 3]
        q[f, 2] = q[f, 3]


def turn_high_body(
    owner, hold, near_0, near_1, far, q_low, after, q, z_own, y_own, z_pair, z_cross, y_near, y_far, half
):
    turn_part(kept_flags(owner), B - HALF, hold, (near_0, near_1), far, q, 5, half)
    odd_z, odd_y = odd("gx"), odd("gy")
    for f in range(F):
        for k in range(5):
            q[f, k] = q_low[f, k + LOW]
        top = B + 2 - LOW
        q[f, top + 1] = q[f, top]
        q[f, top + 2] = q[f, top]
        ends = [q_low[f, 3], q_low[f, 4], q[f, top - 1], q[f, top]]
        for k in range(4):
            z_own[f, k] = ends[k]
        for k in range(2):
            z_pair[f, k] = jnp.where(odd_z, ends[k], ends[2 + k])
            z_cross[f, k] = jnp.where(odd_z, ends[2 + k], ends[k])
        for b in range(4):
            span = slice(8 * b, 8 * b + 8)
            source, z = (q_low, 8 * b + 3) if b < 2 else (q, 8 * b + 3 - LOW)
            ends = [source[f, z : z + 8, j, 0 if j < 2 else 7, :] for j in range(4)]
            for k in range(4):
                y_own[f, k, span, :] = ends[k]
            for k in range(2):
                y_near[f, k, span, :] = jnp.where(odd_y, ends[k], ends[2 + k])
                y_far[f, k, span, :] = jnp.where(odd_y, ends[2 + k], ends[k])


def turn(body, name, planes, owner, arrays, others, after=()):
    shapes = [(F, planes, 4, ROWS, LANES)] + others
    return pl.pallas_call(
        body,
        name=name,
        out_shape=tuple(jax.ShapeDtypeStruct(shape, F32) for shape in shapes),
        in_specs=[SMEM] + [VMEM] * (len(arrays) + len(after)),
        out_specs=(VMEM,) * len(shapes),
        scratch_shapes=[pltpu.VMEM((8, F, 4, ROWS, LANES), F32)],
        compiler_params=pltpu.CompilerParams(vmem_limit_bytes=24 << 20),
        cost_estimate=pl.CostEstimate(flops=0, bytes_accessed=6000000, transcendentals=0),
    )(owner, *arrays, *after)


def turn_low(owner, *arrays):
    return turn(turn_low_body, "turn_low", LOW + 10, owner, arrays, [])[0]


def turn_high(owner, after, *arrays):
    z_own, y_own = (F, 4, 4, ROWS, LANES), (F, 4, B, LANES)
    z_half, y_half = (F, 2, 4, ROWS, LANES), (F, 2, B, LANES)
    others = [z_own, y_own, z_half, z_half, y_half, y_half]
    return turn(turn_high_body, "turn_high", B - LOW + 10, owner, arrays, others, (after,))


def minmod(a, b):
    return jnp.maximum(jnp.minimum(a, b), jnp.minimum(jnp.maximum(a, b), 0.0))


def conduction(v):
    return jnp.exp(0.5 * jnp.tanh(v))


LEAD = 5
J = range(4)


def step_body(
    first, count, chunk, spread, q, *rest,
):
    (
        out, token, firsts, lasts, ends, result, carry_p, carry_n, carry_c, dx, cx, px, mx, nx, done, turned, sem_out,
    ) = rest[-17:]
    token[...] = jnp.zeros_like(token)
    lane = lax.broadcasted_iota(jnp.int32, (8, LANES), 1)
    sub = lax.broadcasted_iota(jnp.int32, (8, LANES), 0)
    scale = [0.5 * spread[f] for f in range(F)]

    def y_next(value, end):
        return jnp.where(sub == 7, end, pltpu.roll(value, 7, 0))

    def y_last(value, end):
        return jnp.where(sub == 0, end, pltpu.roll(value, 1, 0))

    def leaving(k):
        z = chunk * k
        return [
            pltpu.make_async_copy(
                result.at[c, :, pl.ds(z + LEAD, chunk)],
                out.at[:, pl.ds(first + z, chunk), :, c, 0],
                sem_out.at[k, c],
            )
            for c in range(CAP)
        ]

    def late(i):
        for f in range(F):
            for j in (0, 2):
                result[j, f, i], result[j + 1, f, i] = swap_32(turned[f, j], turned[f, j + 1], lane)
        for f in range(F):
            for j in (0, 1):
                turned[f, j], turned[f, j + 2] = swap_64(done[f, j], done[f, j + 2], lane)

    def middle(i):
        here = [carry_c[j] for j in J]
        above = [conduction(q[5, i + 1, j]) for j in J]
        cond_z = [a + b for a, b in zip(here, above)]
        for j in J:
            carry_c[j] = above[j]
        beyond = here[1:] + [y_next(here[0], here[3])]
        cond_y = [a + b for a, b in zip(here, beyond)]
        v = [q[1, i, j] for j in J]
        beyond = v[1:] + [y_next(v[0], v[3])]
        weight_y = [0.0625 * (a + b) for a, b in zip(v, beyond)]
        weight_z = [0.0625 * (q[2, i, j] + q[2, i + 1, j]) for j in J]
        edge_y = -0.125 * v[0]
        edge_x = [-0.125 * q[0, i, j] for j in J]
        for f in range(F):
            value = [q[f, i, j] for j in J]
            twice = [a + a for a in value]
            total = []
            for j in J:
                after = q[f, i + 1, j]
                d = after - value[j]
                slope = minmod(d, q[f, i + 2, j] - after)
                double = after + after
                state = jnp.where(weight_z[j] > 0.0, carry_p[f, j], double - slope)
                carry_p[f, j] = double + slope
                net = (scale[f] * cond_z[j]) * d - weight_z[j] * state
                total.append(value[j] + (net - carry_n[f, j]))
                carry_n[f, j] = net
            beyond = value[1:] + [y_next(value[0], value[3])]
            d = [b - a for a, b in zip(value, beyond)]
            before = [y_last(d[3], 0.0)] + d[:3]
            slope = [minmod(a, b) for a, b in zip(before, d)]
            right = [a - b for a, b in zip(twice, slope)]
            right = right[1:] + [y_next(right[0], twice[3])]
            net = []
            for j in J:
                state = jnp.where(weight_y[j] > 0.0, twice[j] + slope[j], right[j])
                net.append((scale[f] * cond_y[j]) * d[j] - weight_y[j] * state)
            before = [y_last(net[3], edge_y * twice[0])] + net[:3]
            for j in J:
                n = nx[f, j]
                t = total[j] + (net[j] - before[j])
                before_x = jnp.where(lane == 0, edge_x[j] * twice[j], pltpu.roll(n, 1, 1))
                done[f, j] = t + (n - before_x)
    def early(i):
        here, there = i & 1, (i + 1) & 1
        for j in J:
            u = q[0, i + 1, j]
            weight = 0.0625 * ((u + u) + dx[here, 0, j])
            from_left = (weight > 0.0) | (lane == 127)
            cond = cx[here, j]
            for f in range(F):
                state = jnp.where(from_left, px[f, j], pltpu.roll(mx[f, j], 127, 1))
                nx[f, j] = (scale[f] * cond) * dx[here, f, j] - weight * state
        for j in J:
            for f in range(F):
                a, d = q[f, i + 2, j], dx[there, f, j]
                slope = minmod(pltpu.roll(d, 1, 1), d)
                px[f, j], mx[f, j] = (a + a) + slope, (a + a) - slope
        for j in J:
            c = conduction(q[5, i + 3, j])
            cx[here, j] = c + jnp.where(lane == 127, c, pltpu.roll(c, 127, 1))
            for f in range(F):
                a = q[f, i + 3, j]
                dx[here, f, j] = jnp.where(lane == 127, 0.0, pltpu.roll(a, 127, 1) - a)

    def starting(i, _):
        early(i)
        return 0

    def plane(i, _):
        late(i)
        middle(i)
        early(i)

        @pl.when((i >= chunk + 4) & ((i - 4) % chunk == 0))
        def _():
            for copy in leaving((i - 4) // chunk - 1):
                copy.start()

        return 0

    def ending(i, _):
        late(i)
        return 0

    for j in J:
        carry_c[j] = conduction(q[5, 3, j])
        cond = conduction(q[5, 2, j]) + carry_c[j]
        weight = 0.0625 * (q[2, 2, j] + q[2, 3, j])
        for f in range(F):
            a, b, c, d = [q[f, k, j] for k in range(1, 5)]
            across = c - b
            left = (b + b) + minmod(b - a, across)
            slope = minmod(across, d - c)
            state = jnp.where(weight > 0.0, left, (c + c) - slope)
            carry_p[f, j] = (c + c) + slope
            carry_n[f, j] = (scale[f] * cond) * across - weight * state
    lax.fori_loop(0, 3, starting, 0)
    lax.fori_loop(3, count + 3, plane, 0)
    lax.fori_loop(count + 3, count + LEAD, ending, 0)
    for copy in leaving(count // chunk - 1):
        copy.start()
    for c in range(CAP):
        for f in range(F):
            for z in range(0, count, 8):
                span = slice(LEAD + z, LEAD + z + 8)
                firsts[c, f, z : z + 8, :] = result[c, f, span, 0, :]
                lasts[c, f, z : z + 8, :] = result[c, f, span, 7, :]
            for k in range(2):
                ends[c, f, k] = result[c, f, LEAD + k + (count - 2 if first else 0)]
    for k in range(count // chunk):
        for copy in leaving(k):
            copy.wait()


def step(first, count, chunk, spread, q, out=None):
    planes = lambda *lead: pltpu.VMEM((*lead, ROWS, LANES), F32)
    return pl.pallas_call(
        functools.partial(step_body, first, count, chunk),
        name="step",
        out_shape=(
            jax.ShapeDtypeStruct((F, B, ROWS, CAP, 1, LANES), F32),
            jax.ShapeDtypeStruct((ROWS, LANES), F32),
            jax.ShapeDtypeStruct((CAP, F, count, LANES), F32),
            jax.ShapeDtypeStruct((CAP, F, count, LANES), F32),
            jax.ShapeDtypeStruct((CAP, F, 2, ROWS, LANES), F32),
        ),
        in_specs=[SMEM, VMEM] + ([] if out is None else [HBM]),
        out_specs=(HBM,) + (VMEM,) * 4,
        input_output_aliases={} if out is None else {2: 0},
        scratch_shapes=[
            planes(CAP, F, count + LEAD),
            planes(F, 4),
            planes(F, 4),
            planes(4),
            planes(2, F, 4),
            planes(2, 4),
            planes(F, 4),
            planes(F, 4),
            planes(F, 4),
            planes(F, 4),
            planes(F, 4),
            pltpu.SemaphoreType.DMA((count // chunk, CAP)),
        ],
        compiler_params=pltpu.CompilerParams(vmem_limit_bytes=24 << 20),
        cost_estimate=pl.CostEstimate(flops=0, bytes_accessed=20000000, transcendentals=0),
    )(spread, q, *(() if out is None else (out,)))


def change(far, out_1, in_0, in_1, u_out, u_0, u_1, c_out, c_0, scale):
    d = in_0 - out_1
    slope = minmod(d, in_1 - in_0)
    inner = -jnp.maximum(0.0625 * (u_0 + u_1), 0.0) * slope
    weight = 0.0625 * (u_out + u_0)
    left = (out_1 + out_1) + minmod(out_1 - far, d)
    right = (in_0 + in_0) - slope
    net = (scale * (c_out + c_0)) * d - weight * jnp.where(weight > 0.0, left, right)
    outer = net + (0.125 * u_0) * (in_0 + in_0)
    return inner - outer, -inner


def both_ends(below, own, above, velocity, has_below, has_above, scale):
    u = [below(velocity, 1)] + [own(velocity, k) for k in range(4)] + [above(velocity, 0)]
    c = [conduction(v) for v in (below(5, 1), own(5, 0), own(5, 3), above(5, 0))]
    result = []
    for f in range(F):
        layers = [own(f, k) for k in range(4)]
        a, b = change(
            below(f, 0), below(f, 1), layers[0], layers[1], u[0], u[1], u[2], c[0], c[1], scale[f]
        )
        e, d = change(
            above(f, 1), above(f, 0), layers[3], layers[2], -u[5], -u[4], -u[3], c[3], c[2], scale[f]
        )
        a, b = jnp.where(has_below, a, 0.0), jnp.where(has_below, b, 0.0)
        d, e = jnp.where(has_above, d, 0.0), jnp.where(has_above, e, 0.0)
        result.append([a, b, d, e])
    return result


def ends_body(
    spread, z_own, y_own, y_far, z_pair, z_cross, y_near,
    first_low, last_low, ends_low, first_high, last_high, ends_high, before, out,
    z_add, y_add, planes, first, last, sem_out,
):
    gx, gy = lax.axis_index("gx"), lax.axis_index("gy")
    odd_z, odd_y = odd("gx"), odd("gy")
    lane = lax.broadcasted_iota(jnp.int32, (8, LANES), 1)
    sub = lax.broadcasted_iota(jnp.int32, (8, LANES), 0)
    scale = [0.5 * spread[f] for f in range(F)]

    rows_out, whole_out = [], []
    for c in range(CAP):
        rows_out.append(pltpu.make_async_copy(first.at[c], out.at[:, :, 0, c, 0], sem_out.at[c, 0]))
        rows_out.append(pltpu.make_async_copy(last.at[c], out.at[:, :, 7, c, 0], sem_out.at[c, 1]))
        for k, z in enumerate((0, 30)):
            there = out.at[:, z : z + 2, :, c, 0]
            here = planes.at[c, :, 2 * k : 2 * k + 2]
            whole_out.append(pltpu.make_async_copy(here, there, sem_out.at[c, 2 + k]))

    for j in range(4):
        changes = both_ends(
            lambda f, k: jnp.where(odd_z, z_pair[f, k, j], z_cross[f, k, j]),
            lambda f, k: z_own[f, k, j],
            lambda f, k: jnp.where(odd_z, z_cross[f, k, j], z_pair[f, k, j]),
            2, gx > 0, gx < lax.axis_size("gx") - 1, scale,
        )
        for f in range(F):
            for k in range(4):
                z_add[f, k, j] = changes[f][k]
    for b in range(4):
        span = slice(8 * b, 8 * b + 8)
        changes = both_ends(
            lambda f, k: jnp.where(odd_y, y_near[f, k, span, :], y_far[f, k, span, :]),
            lambda f, k: y_own[f, k, span, :],
            lambda f, k: jnp.where(odd_y, y_far[f, k, span, :], y_near[f, k, span, :]),
            1, gy > 0, gy < lax.axis_size("gy") - 1, scale,
        )
        for f in range(F):
            for c, value in enumerate(turned_to_layers(changes[f], lane)):
                y_add[c, f, span, :] = value

    for c in range(CAP):
        for f in range(F):
            for b in range(4):
                span = slice(8 * b, 8 * b + 8)
                value = y_add[c, f, span, :]
                part = slice(8 * (b % 2), 8 * (b % 2) + 8)
                low = (first_low if b < 2 else first_high)[c, f, part, :]
                high = (last_low if b < 2 else last_high)[c, f, part, :]
                first[c, f, span, :] = low + jnp.where(lane < 64, value, 0.0)
                last[c, f, span, :] = high + jnp.where(lane >= 64, value, 0.0)
        rows_out[2 * c].start()
        rows_out[2 * c + 1].start()
    corner = ((sub == 0) & (lane < 64)) | ((sub == 7) & (lane >= 64))
    for f in range(F):
        for k, z in enumerate((0, 1, 30, 31)):
            values = turned_to_layers([z_add[f, k, j] for j in range(4)], lane)
            for c in range(CAP):
                plane = (ends_low if k < 2 else ends_high)[c, f, k % 2]
                add = values[c] + jnp.where(corner, y_add[c, f, z : z + 1, :], 0.0)
                planes[c, f, k] = plane + add
    for copy in rows_out:
        copy.wait()
    run_all(whole_out)


def ends(spread, *arrays):
    rows = pltpu.VMEM((CAP, F, B, LANES), F32)
    planes = pltpu.VMEM((CAP, F, 4, ROWS, LANES), F32)
    return pl.pallas_call(
        ends_body,
        name="ends",
        out_shape=jax.ShapeDtypeStruct((F, B, ROWS, CAP, 1, LANES), F32),
        in_specs=[SMEM] + [VMEM] * (len(arrays) - 1) + [HBM],
        out_specs=HBM,
        input_output_aliases={len(arrays): 0},
        scratch_shapes=[
            pltpu.VMEM((F, 4, 4, ROWS, LANES), F32),
            rows,
            planes,
            rows,
            rows,
            pltpu.SemaphoreType.DMA((CAP, 4)),
        ],
        compiler_params=pltpu.CompilerParams(vmem_limit_bytes=24 << 20),
        cost_estimate=pl.CostEstimate(flops=0, bytes_accessed=6000000, transcendentals=0),
    )(spread, *arrays)


def exchange(block, axes, first, wrap=False):
    count = lax.axis_size(axes)
    pairs = []
    for i in range(first, count, 2):
        j = (i + 1) % count
        if i + 1 < count or wrap:
            pairs += [(i, j), (j, i)]
    return lax.ppermute(block, axes, pairs)


def local(old_state, old_owner, old_slot, diffusivity):
    x = old_state.reshape(8, F, B, ROWS, LANES).transpose(1, 2, 3, 0, 4)[..., None, :]
    far_low, token = far_boxes(x)
    far_high, *nears, hold_low, hold_high = near_boxes(x, token)
    far_low = exchange(far_low, AXES, 1, wrap=True)
    far_high = exchange(far_high, AXES, 1, wrap=True)
    nears = [exchange(near, AXES, 0) for near in nears]
    q_low = turn_low(old_owner, hold_low, *nears[:2], far_low)
    out, token, *low_ends = step(0, LOW, 8, diffusivity, q_low)
    q_high, z_own, y_own, z_pair, z_cross, y_near, y_far = turn_high(
        old_owner, token, hold_high, *nears[2:], far_high, q_low
    )
    y_near = exchange(y_near, "gy", 0)
    y_far = exchange(y_far, "gy", 1)
    z_pair = exchange(z_pair, "gx", 0)
    z_cross = exchange(z_cross, "gx", 1)
    out, _, *high_ends = step(LOW, B - LOW, 8, diffusivity, q_high, out)
    out = ends(
        diffusivity, z_own, y_own, y_far, z_pair, z_cross, y_near, *low_ends, *high_ends, out
    )
    return out[..., 0, :].transpose(3, 0, 1, 2, 4).reshape(CAP, F, B * B * B)


def solution(mesh):
    placed = (P(AXES, None, None), P(), P(), P())
    return jax.shard_map(
        local, mesh=mesh, in_specs=placed, out_specs=P(AXES, None, None), check_vma=False
    )
```

```python
import functools

import jax
import jax.numpy as jnp
from jax import lax
from jax.experimental import pallas as pl
from jax.experimental.pallas import tpu as pltpu
from jax.sharding import PartitionSpec as P

B = 32
F = 6
CAP = 4
HALF = 18
LOW = HALF - 2
PARTS = ((0, HALF // 2), (HALF // 2, HALF), (HALF, (HALF + B) // 2), ((HALF + B) // 2, B))
ROWS = 8
LANES = 128
AXES = ("gx", "gy")
F32 = jnp.float32
HBM = pl.BlockSpec(memory_space=pl.ANY)
VMEM = pl.BlockSpec(memory_space=pltpu.VMEM)
SMEM = pl.BlockSpec(memory_space=pltpu.SMEM)
WIDE = 56 << 20


def run_all(copies):
    for copy in copies:
        copy.start()
    for copy in copies:
        copy.wait()


def odd(axis):
    return lax.axis_index(axis) % 2 == 1


def leaving_copies(x, near, target, planes, sem):
    first = jnp.where(odd("gy"), 0, 6) if near else jnp.where(odd("gy"), 6, 0)
    return [
        pltpu.make_async_copy(x.at[:, planes, :, first + j, 0], target.at[j], sem.at[j])
        for j in range(2)
    ]


def far_body(x, low, token, sem):
    token[...] = jnp.zeros_like(token)
    run_all(leaving_copies(x, False, low, slice(0, HALF), sem))


def near_body(x, after, high, *rest):
    nears, (hold_low, hold_high, sem) = rest[: len(PARTS)], rest[len(PARTS) :]
    copies = leaving_copies(x, False, high, slice(HALF, B), sem.at[2 + len(PARTS)])
    for k, near in enumerate(nears):
        copies += leaving_copies(x, True, near, slice(*PARTS[k]), sem.at[2 + k])
    for k, hold in enumerate((hold_low, hold_high)):
        for c in range(CAP):
            planes = slice(HALF, B) if k else slice(0, HALF)
            copies.append(
                pltpu.make_async_copy(x.at[:, planes, :, 2 + c, 0], hold.at[c], sem.at[k, c])
            )
    run_all(copies)


def from_slots(body, name, arrays, shapes, sems, limit):
    shapes = tuple(jax.ShapeDtypeStruct(shape, F32) for shape in shapes)
    return pl.pallas_call(
        body,
        name=name,
        out_shape=shapes,
        in_specs=[HBM] * len(arrays),
        out_specs=(VMEM,) * len(shapes),
        scratch_shapes=[pltpu.SemaphoreType.DMA(sems)],
        compiler_params=pltpu.CompilerParams(vmem_limit_bytes=limit),
        cost_estimate=pl.CostEstimate(flops=0, bytes_accessed=1000, transcendentals=0),
    )(*arrays)


def far_boxes(x):
    return from_slots(far_body, "far", [x], [(2, F, HALF, ROWS, LANES), (ROWS, LANES)], (2,), WIDE)


def near_boxes(x, after):
    boxes = lambda count, planes: (count, F, planes, ROWS, LANES)
    shapes = [boxes(2, B - HALF)] + [boxes(2, end - start) for start, end in PARTS]
    shapes += [boxes(CAP, HALF), boxes(CAP, B - HALF)]
    return from_slots(near_body, "near", [x, after], shapes, (3 + len(PARTS), CAP), 24 << 20)


def device_number():
    return lax.axis_index("gx") * lax.axis_size("gy") + lax.axis_index("gy")


def kept_flags(owner):
    device = device_number()
    return [owner[device * CAP + c] == device for c in range(CAP)]


def arrived(kept, here, c, far, near):
    from_far = odd("gy") if c >= 2 else jnp.logical_not(odd("gy"))
    return jnp.where(kept, here, jnp.where(from_far, far, near))


def swap_64(a, b, lane):
    low = lane < 64
    m = pltpu.roll(jnp.where(low, b, a), 64, 1)
    return jnp.where(low, a, m), jnp.where(low, m, b)


def swap_32(a, b, lane):
    even = (lane & 32) == 0
    m = jnp.where(even, b, a)
    return jnp.where(even, a, pltpu.roll(m, 32, 1)), jnp.where(even, pltpu.roll(m, 96, 1), b)


def turned_to_layers(v, lane):
    a, c = swap_64(v[0], v[2], lane)
    b, d = swap_64(v[1], v[3], lane)
    return *swap_32(a, b, lane), *swap_32(c, d, lane)


def turn_part(kept, count, hold, nears, far, target, index, half):
    lane = lax.broadcasted_iota(jnp.int32, (8, LANES), 1)

    def first_half(z):
        near = nears[z // (count // 2)]
        for f in range(F):
            v = [
                arrived(kept[c], hold[c, f, z], c, far[c % 2, f, z], near[c % 2, f, z % (count // 2)])
                for c in range(CAP)
            ]
            half[z % 8, f, 0], half[z % 8, f, 2] = swap_64(v[0], v[2], lane)
            half[z % 8, f, 1], half[z % 8, f, 3] = swap_64(v[1], v[3], lane)

    def second_half(z):
        for f in range(F):
            a, b, c, d = [half[z % 8, f, j] for j in range(4)]
            target[f, index + z, 0], target[f, index + z, 1] = swap_32(a, b, lane)
            target[f, index + z, 2], target[f, index + z, 3] = swap_32(c, d, lane)

    for z in range(count + 4):
        if z < count:
            first_half(z)
        if z >= 4:
            second_half(z - 4)


def turn_low_body(owner, hold, near_0, near_1, far, q, half):
    turn_part(kept_flags(owner), HALF, hold, (near_0, near_1), far, q, 3, half)
    for f in range(F):
        q[f, 0] = q[f, 3]
        q[f, 1] = q[f, 3]
        q[f, 2] = q[f, 3]


def turn_high_body(
    owner, hold, near_0, near_1, far, q_low, after, q, z_own, y_own, z_pair, z_cross, y_near, y_far, half
):
    turn_part(kept_flags(owner), B - HALF, hold, (near_0, near_1), far, q, 5, half)
    odd_z, odd_y = odd("gx"), odd("gy")
    for f in range(F):
        for k in range(5):
            q[f, k] = q_low[f, k + LOW]
        top = B + 2 - LOW
        q[f, top + 1] = q[f, top]
        q[f, top + 2] = q[f, top]
        ends = [q_low[f, 3], q_low[f, 4], q[f, top - 1], q[f, top]]
        for k in range(4):
            z_own[f, k] = ends[k]
        for k in range(2):
            z_pair[f, k] = jnp.where(odd_z, ends[k], ends[2 + k])
            z_cross[f, k] = jnp.where(odd_z, ends[2 + k], ends[k])
        for b in range(4):
            span = slice(8 * b, 8 * b + 8)
            source, z = (q_low, 8 * b + 3) if b < 2 else (q, 8 * b + 3 - LOW)
            ends = [source[f, z : z + 8, j, 0 if j < 2 else 7, :] for j in range(4)]
            for k in range(4):
                y_own[f, k, span, :] = ends[k]
            for k in range(2):
                y_near[f, k, span, :] = jnp.where(odd_y, ends[k], ends[2 + k])
                y_far[f, k, span, :] = jnp.where(odd_y, ends[2 + k], ends[k])


def turn(body, name, planes, owner, arrays, others, after=()):
    shapes = [(F, planes, 4, ROWS, LANES)] + others
    return pl.pallas_call(
        body,
        name=name,
        out_shape=tuple(jax.ShapeDtypeStruct(shape, F32) for shape in shapes),
        in_specs=[SMEM] + [VMEM] * (len(arrays) + len(after)),
        out_specs=(VMEM,) * len(shapes),
        scratch_shapes=[pltpu.VMEM((8, F, 4, ROWS, LANES), F32)],
        compiler_params=pltpu.CompilerParams(vmem_limit_bytes=24 << 20),
        cost_estimate=pl.CostEstimate(flops=0, bytes_accessed=6000000, transcendentals=0),
    )(owner, *arrays, *after)


def turn_low(owner, *arrays):
    return turn(turn_low_body, "turn_low", LOW + 10, owner, arrays, [])[0]


def turn_high(owner, after, *arrays):
    z_own, y_own = (F, 4, 4, ROWS, LANES), (F, 4, B, LANES)
    z_half, y_half = (F, 2, 4, ROWS, LANES), (F, 2, B, LANES)
    others = [z_own, y_own, z_half, z_half, y_half, y_half]
    return turn(turn_high_body, "turn_high", B - LOW + 10, owner, arrays, others, (after,))


def minmod(a, b):
    return jnp.maximum(jnp.minimum(a, b), jnp.minimum(jnp.maximum(a, b), 0.0))


def conduction(v):
    return jnp.exp(0.5 * jnp.tanh(v))


LEAD = 5
J = range(4)


def step_body(
    first, count, chunk, spread, q, *rest,
):
    (
        out, token, firsts, lasts, ends, result, carry_p, carry_n, carry_c, dx, cx, px, mx, nx, done, turned, sem_out,
    ) = rest[-17:]
    token[...] = jnp.zeros_like(token)
    lane = lax.broadcasted_iota(jnp.int32, (8, LANES), 1)
    sub = lax.broadcasted_iota(jnp.int32, (8, LANES), 0)
    scale = [0.5 * spread[f] for f in range(F)]

    def y_next(value, end):
        return jnp.where(sub == 7, end, pltpu.roll(value, 7, 0))

    def y_last(value, end):
        return jnp.where(sub == 0, end, pltpu.roll(value, 1, 0))

    def leaving(k):
        z = chunk * k
        return [
            pltpu.make_async_copy(
                result.at[c, :, pl.ds(z + LEAD, chunk)],
                out.at[:, pl.ds(first + z, chunk), :, c, 0],
                sem_out.at[k, c],
            )
            for c in range(CAP)
        ]

    def late(i):
        for f in range(F):
            for j in (0, 2):
                result[j, f, i], result[j + 1, f, i] = swap_32(turned[f, j], turned[f, j + 1], lane)
        for f in range(F):
            for j in (0, 1):
                turned[f, j], turned[f, j + 2] = swap_64(done[f, j], done[f, j + 2], lane)

    def middle(i):
        here = [carry_c[j] for j in J]
        above = [conduction(q[5, i + 1, j]) for j in J]
        cond_z = [a + b for a, b in zip(here, above)]
        for j in J:
            carry_c[j] = above[j]
        beyond = here[1:] + [y_next(here[0], here[3])]
        cond_y = [a + b for a, b in zip(here, beyond)]
        v = [q[1, i, j] for j in J]
        beyond = v[1:] + [y_next(v[0], v[3])]
        weight_y = [0.0625 * (a + b) for a, b in zip(v, beyond)]
        weight_z = [0.0625 * (q[2, i, j] + q[2, i + 1, j]) for j in J]
        edge_y = -0.125 * v[0]
        edge_x = [-0.125 * q[0, i, j] for j in J]
        for f in range(F):
            value = [q[f, i, j] for j in J]
            twice = [a + a for a in value]
            total = []
            for j in J:
                after = q[f, i + 1, j]
                d = after - value[j]
                slope = minmod(d, q[f, i + 2, j] - after)
                double = after + after
                state = jnp.where(weight_z[j] > 0.0, carry_p[f, j], double - slope)
                carry_p[f, j] = double + slope
                net = (scale[f] * cond_z[j]) * d - weight_z[j] * state
                total.append(value[j] + (net - carry_n[f, j]))
                carry_n[f, j] = net
            beyond = value[1:] + [y_next(value[0], value[3])]
            d = [b - a for a, b in zip(value, beyond)]
            before = [y_last(d[3], 0.0)] + d[:3]
            slope = [minmod(a, b) for a, b in zip(before, d)]
            right = [a - b for a, b in zip(twice, slope)]
            right = right[1:] + [y_next(right[0], twice[3])]
            net = []
            for j in J:
                state = jnp.where(weight_y[j] > 0.0, twice[j] + slope[j], right[j])
                net.append((scale[f] * cond_y[j]) * d[j] - weight_y[j] * state)
            before = [y_last(net[3], edge_y * twice[0])] + net[:3]
            for j in J:
                n = nx[f, j]
                t = total[j] + (net[j] - before[j])
                before_x = jnp.where(lane == 0, edge_x[j] * twice[j], pltpu.roll(n, 1, 1))
                done[f, j] = t + (n - before_x)
    def early(i):
        here, there = i & 1, (i + 1) & 1
        for j in J:
            u = q[0, i + 1, j]
            weight = 0.0625 * ((u + u) + dx[here, 0, j])
            from_left = (weight > 0.0) | (lane == 127)
            cond = cx[here, j]
            for f in range(F):
                state = jnp.where(from_left, px[f, j], pltpu.roll(mx[f, j], 127, 1))
                nx[f, j] = (scale[f] * cond) * dx[here, f, j] - weight * state
        for j in J:
            for f in range(F):
                a, d = q[f, i + 2, j], dx[there, f, j]
                slope = minmod(pltpu.roll(d, 1, 1), d)
                px[f, j], mx[f, j] = (a + a) + slope, (a + a) - slope
        for j in J:
            c = conduction(q[5, i + 3, j])
            cx[here, j] = c + jnp.where(lane == 127, c, pltpu.roll(c, 127, 1))
            for f in range(F):
                a = q[f, i + 3, j]
                dx[here, f, j] = jnp.where(lane == 127, 0.0, pltpu.roll(a, 127, 1) - a)

    def starting(i, _):
        early(i)
        return 0

    def plane(i, _):
        late(i)
        middle(i)
        early(i)

        @pl.when((i >= chunk + 4) & ((i - 4) % chunk == 0))
        def _():
            for copy in leaving((i - 4) // chunk - 1):
                copy.start()

        return 0

    def ending(i, _):
        late(i)
        return 0

    for j in J:
        carry_c[j] = conduction(q[5, 3, j])
        cond = conduction(q[5, 2, j]) + carry_c[j]
        weight = 0.0625 * (q[2, 2, j] + q[2, 3, j])
        for f in range(F):
            a, b, c, d = [q[f, k, j] for k in range(1, 5)]
            across = c - b
            left = (b + b) + minmod(b - a, across)
            slope = minmod(across, d - c)
            state = jnp.where(weight > 0.0, left, (c + c) - slope)
            carry_p[f, j] = (c + c) + slope
            carry_n[f, j] = (scale[f] * cond) * across - weight * state
    lax.fori_loop(0, 3, starting, 0)
    lax.fori_loop(3, count + 3, plane, 0)
    lax.fori_loop(count + 3, count + LEAD, ending, 0)
    for copy in leaving(count // chunk - 1):
        copy.start()
    for c in range(CAP):
        for f in range(F):
            for z in range(0, count, 8):
                span = slice(LEAD + z, LEAD + z + 8)
                firsts[c, f, z : z + 8, :] = result[c, f, span, 0, :]
                lasts[c, f, z : z + 8, :] = result[c, f, span, 7, :]
            for k in range(2):
                ends[c, f, k] = result[c, f, LEAD + k + (count - 2 if first else 0)]
    for k in range(count // chunk):
        for copy in leaving(k):
            copy.wait()


def step(first, count, chunk, spread, q, out=None):
    planes = lambda *lead: pltpu.VMEM((*lead, ROWS, LANES), F32)
    return pl.pallas_call(
        functools.partial(step_body, first, count, chunk),
        name="step",
        out_shape=(
            jax.ShapeDtypeStruct((F, B, ROWS, CAP, 1, LANES), F32),
            jax.ShapeDtypeStruct((ROWS, LANES), F32),
            jax.ShapeDtypeStruct((CAP, F, count, LANES), F32),
            jax.ShapeDtypeStruct((CAP, F, count, LANES), F32),
            jax.ShapeDtypeStruct((CAP, F, 2, ROWS, LANES), F32),
        ),
        in_specs=[SMEM, VMEM] + ([] if out is None else [HBM]),
        out_specs=(HBM,) + (VMEM,) * 4,
        input_output_aliases={} if out is None else {2: 0},
        scratch_shapes=[
            planes(CAP, F, count + LEAD),
            planes(F, 4),
            planes(F, 4),
            planes(4),
            planes(2, F, 4),
            planes(2, 4),
            planes(F, 4),
            planes(F, 4),
            planes(F, 4),
            planes(F, 4),
            planes(F, 4),
            pltpu.SemaphoreType.DMA((count // chunk, CAP)),
        ],
        compiler_params=pltpu.CompilerParams(vmem_limit_bytes=24 << 20),
        cost_estimate=pl.CostEstimate(flops=0, bytes_accessed=20000000, transcendentals=0),
    )(spread, q, *(() if out is None else (out,)))


def change(far, out_1, in_0, in_1, u_out, u_0, u_1, c_out, c_0, scale):
    d = in_0 - out_1
    slope = minmod(d, in_1 - in_0)
    inner = -jnp.maximum(0.0625 * (u_0 + u_1), 0.0) * slope
    weight = 0.0625 * (u_out + u_0)
    left = (out_1 + out_1) + minmod(out_1 - far, d)
    right = (in_0 + in_0) - slope
    net = (scale * (c_out + c_0)) * d - weight * jnp.where(weight > 0.0, left, right)
    outer = net + (0.125 * u_0) * (in_0 + in_0)
    return inner - outer, -inner


def both_ends(below, own, above, velocity, has_below, has_above, scale):
    u = [below(velocity, 1)] + [own(velocity, k) for k in range(4)] + [above(velocity, 0)]
    c = [conduction(v) for v in (below(5, 1), own(5, 0), own(5, 3), above(5, 0))]
    result = []
    for f in range(F):
        layers = [own(f, k) for k in range(4)]
        a, b = change(
            below(f, 0), below(f, 1), layers[0], layers[1], u[0], u[1], u[2], c[0], c[1], scale[f]
        )
        e, d = change(
            above(f, 1), above(f, 0), layers[3], layers[2], -u[5], -u[4], -u[3], c[3], c[2], scale[f]
        )
        a, b = jnp.where(has_below, a, 0.0), jnp.where(has_below, b, 0.0)
        d, e = jnp.where(has_above, d, 0.0), jnp.where(has_above, e, 0.0)
        result.append([a, b, d, e])
    return result


def ends_body(
    spread, z_own, y_own, y_far, z_pair, z_cross, y_near,
    first_low, last_low, ends_low, first_high, last_high, ends_high, before, out,
    z_add, y_add, planes, first, last, sem_out,
):
    gx, gy = lax.axis_index("gx"), lax.axis_index("gy")
    odd_z, odd_y = odd("gx"), odd("gy")
    lane = lax.broadcasted_iota(jnp.int32, (8, LANES), 1)
    sub = lax.broadcasted_iota(jnp.int32, (8, LANES), 0)
    scale = [0.5 * spread[f] for f in range(F)]

    rows_out, whole_out = [], []
    for c in range(CAP):
        rows_out.append(pltpu.make_async_copy(first.at[c], out.at[:, :, 0, c, 0], sem_out.at[c, 0]))
        rows_out.append(pltpu.make_async_copy(last.at[c], out.at[:, :, 7, c, 0], sem_out.at[c, 1]))
        for k, z in enumerate((0, 30)):
            there = out.at[:, z : z + 2, :, c, 0]
            here = planes.at[c, :, 2 * k : 2 * k + 2]
            whole_out.append(pltpu.make_async_copy(here, there, sem_out.at[c, 2 + k]))

    for j in range(4):
        changes = both_ends(
            lambda f, k: jnp.where(odd_z, z_pair[f, k, j], z_cross[f, k, j]),
            lambda f, k: z_own[f, k, j],
            lambda f, k: jnp.where(odd_z, z_cross[f, k, j], z_pair[f, k, j]),
            2, gx > 0, gx < lax.axis_size("gx") - 1, scale,
        )
        for f in range(F):
            for k in range(4):
                z_add[f, k, j] = changes[f][k]
    for b in range(4):
        span = slice(8 * b, 8 * b + 8)
        changes = both_ends(
            lambda f, k: jnp.where(odd_y, y_near[f, k, span, :], y_far[f, k, span, :]),
            lambda f, k: y_own[f, k, span, :],
            lambda f, k: jnp.where(odd_y, y_far[f, k, span, :], y_near[f, k, span, :]),
            1, gy > 0, gy < lax.axis_size("gy") - 1, scale,
        )
        for f in range(F):
            for c, value in enumerate(turned_to_layers(changes[f], lane)):
                y_add[c, f, span, :] = value

    for c in range(CAP):
        for f in range(F):
            for b in range(4):
                span = slice(8 * b, 8 * b + 8)
                value = y_add[c, f, span, :]
                part = slice(8 * (b % 2), 8 * (b % 2) + 8)
                low = (first_low if b < 2 else first_high)[c, f, part, :]
                high = (last_low if b < 2 else last_high)[c, f, part, :]
                first[c, f, span, :] = low + jnp.where(lane < 64, value, 0.0)
                last[c, f, span, :] = high + jnp.where(lane >= 64, value, 0.0)
        rows_out[2 * c].start()
        rows_out[2 * c + 1].start()
    corner = ((sub == 0) & (lane < 64)) | ((sub == 7) & (lane >= 64))
    for f in range(F):
        for k, z in enumerate((0, 1, 30, 31)):
            values = turned_to_layers([z_add[f, k, j] for j in range(4)], lane)
            for c in range(CAP):
                plane = (ends_low if k < 2 else ends_high)[c, f, k % 2]
                add = values[c] + jnp.where(corner, y_add[c, f, z : z + 1, :], 0.0)
                planes[c, f, k] = plane + add
    for copy in rows_out:
        copy.wait()
    run_all(whole_out)


def ends(spread, *arrays):
    rows = pltpu.VMEM((CAP, F, B, LANES), F32)
    planes = pltpu.VMEM((CAP, F, 4, ROWS, LANES), F32)
    return pl.pallas_call(
        ends_body,
        name="ends",
        out_shape=jax.ShapeDtypeStruct((F, B, ROWS, CAP, 1, LANES), F32),
        in_specs=[SMEM] + [VMEM] * (len(arrays) - 1) + [HBM],
        out_specs=HBM,
        input_output_aliases={len(arrays): 0},
        scratch_shapes=[
            pltpu.VMEM((F, 4, 4, ROWS, LANES), F32),
            rows,
            planes,
            rows,
            rows,
            pltpu.SemaphoreType.DMA((CAP, 4)),
        ],
        compiler_params=pltpu.CompilerParams(vmem_limit_bytes=24 << 20),
        cost_estimate=pl.CostEstimate(flops=0, bytes_accessed=6000000, transcendentals=0),
    )(spread, *arrays)


def exchange(block, axes, first, wrap=False):
    count = lax.axis_size(axes)
    pairs = []
    for i in range(first, count, 2):
        j = (i + 1) % count
        if i + 1 < count or wrap:
            pairs += [(i, j), (j, i)]
    return lax.ppermute(block, axes, pairs)


def local(old_state, old_owner, old_slot, diffusivity):
    x = old_state.reshape(8, F, B, ROWS, LANES).transpose(1, 2, 3, 0, 4)[..., None, :]
    far_low, token = far_boxes(x)
    far_high, *nears, hold_low, hold_high = near_boxes(x, token)
    far_low = exchange(far_low, AXES, 1, wrap=True)
    far_high = exchange(far_high, AXES, 1, wrap=True)
    nears = [exchange(near, AXES, 0) for near in nears]
    q_low = turn_low(old_owner, hold_low, *nears[:2], far_low)
    out, token, *low_ends = step(0, LOW, 4, diffusivity, q_low)
    q_high, z_own, y_own, z_pair, z_cross, y_near, y_far = turn_high(
        old_owner, token, hold_high, *nears[2:], far_high, q_low
    )
    y_near = exchange(y_near, "gy", 0)
    y_far = exchange(y_far, "gy", 1)
    z_pair = exchange(z_pair, "gx", 0)
    z_cross = exchange(z_cross, "gx", 1)
    out, _, *high_ends = step(LOW, B - LOW, 4, diffusivity, q_high, out)
    out = ends(
        diffusivity, z_own, y_own, y_far, z_pair, z_cross, y_near, *low_ends, *high_ends, out
    )
    return out[..., 0, :].transpose(3, 0, 1, 2, 4).reshape(CAP, F, B * B * B)


def solution(mesh):
    placed = (P(AXES, None, None), P(), P(), P())
    return jax.shard_map(
        local, mesh=mesh, in_specs=placed, out_specs=P(AXES, None, None), check_vma=False
    )
```

```python
import functools

import jax
import jax.numpy as jnp
from jax import lax
from jax.experimental import pallas as pl
from jax.experimental.pallas import tpu as pltpu
from jax.sharding import PartitionSpec as P

B = 32
F = 6
CAP = 4
HALF = 18
LOW = HALF - 2
PARTS = ((0, HALF // 2), (HALF // 2, HALF), (HALF, (HALF + B) // 2), ((HALF + B) // 2, B))
ROWS = 8
LANES = 128
AXES = ("gx", "gy")
F32 = jnp.float32
HBM = pl.BlockSpec(memory_space=pl.ANY)
VMEM = pl.BlockSpec(memory_space=pltpu.VMEM)
SMEM = pl.BlockSpec(memory_space=pltpu.SMEM)
WIDE = 56 << 20


def run_all(copies):
    for copy in copies:
        copy.start()
    for copy in copies:
        copy.wait()


def odd(axis):
    return lax.axis_index(axis) % 2 == 1


def leaving_copies(x, near, target, planes, sem):
    first = jnp.where(odd("gy"), 0, 6) if near else jnp.where(odd("gy"), 6, 0)
    return [
        pltpu.make_async_copy(x.at[:, planes, :, first + j, 0], target.at[j], sem.at[j])
        for j in range(2)
    ]


def far_body(x, low, high, token, sem):
    token[...] = jnp.zeros_like(token)
    run_all(
        leaving_copies(x, False, low, slice(0, HALF), sem.at[0])
        + leaving_copies(x, False, high, slice(HALF, B), sem.at[1])
    )


def near_body(x, after, *rest):
    nears, (hold_low, hold_high, sem) = rest[: len(PARTS)], rest[len(PARTS) :]
    copies = []
    for k, near in enumerate(nears):
        copies += leaving_copies(x, True, near, slice(*PARTS[k]), sem.at[2 + k])
    for k, hold in enumerate((hold_low, hold_high)):
        for c in range(CAP):
            planes = slice(HALF, B) if k else slice(0, HALF)
            copies.append(
                pltpu.make_async_copy(x.at[:, planes, :, 2 + c, 0], hold.at[c], sem.at[k, c])
            )
    run_all(copies)


def from_slots(body, name, arrays, shapes, sems, limit):
    shapes = tuple(jax.ShapeDtypeStruct(shape, F32) for shape in shapes)
    return pl.pallas_call(
        body,
        name=name,
        out_shape=shapes,
        in_specs=[HBM] * len(arrays),
        out_specs=(VMEM,) * len(shapes),
        scratch_shapes=[pltpu.SemaphoreType.DMA(sems)],
        compiler_params=pltpu.CompilerParams(vmem_limit_bytes=limit),
        cost_estimate=pl.CostEstimate(flops=0, bytes_accessed=1000, transcendentals=0),
    )(*arrays)


def far_boxes(x):
    boxes = lambda planes: (2, F, planes, ROWS, LANES)
    shapes = [boxes(HALF), boxes(B - HALF), (ROWS, LANES)]
    return from_slots(far_body, "far", [x], shapes, (2, 2), WIDE)


def near_boxes(x, after):
    boxes = lambda count, planes: (count, F, planes, ROWS, LANES)
    shapes = [boxes(2, end - start) for start, end in PARTS]
    shapes += [boxes(CAP, HALF), boxes(CAP, B - HALF)]
    return from_slots(near_body, "near", [x, after], shapes, (2 + len(PARTS), CAP), 24 << 20)


def device_number():
    return lax.axis_index("gx") * lax.axis_size("gy") + lax.axis_index("gy")


def kept_flags(owner):
    device = device_number()
    return [owner[device * CAP + c] == device for c in range(CAP)]


def arrived(kept, here, c, far, near):
    from_far = odd("gy") if c >= 2 else jnp.logical_not(odd("gy"))
    return jnp.where(kept, here, jnp.where(from_far, far, near))


def swap_64(a, b, lane):
    low = lane < 64
    m = pltpu.roll(jnp.where(low, b, a), 64, 1)
    return jnp.where(low, a, m), jnp.where(low, m, b)


def swap_32(a, b, lane):
    even = (lane & 32) == 0
    m = jnp.where(even, b, a)
    return jnp.where(even, a, pltpu.roll(m, 32, 1)), jnp.where(even, pltpu.roll(m, 96, 1), b)


def turned_to_layers(v, lane):
    a, c = swap_64(v[0], v[2], lane)
    b, d = swap_64(v[1], v[3], lane)
    return *swap_32(a, b, lane), *swap_32(c, d, lane)


def turn_part(kept, count, hold, nears, far, target, index, half):
    lane = lax.broadcasted_iota(jnp.int32, (8, LANES), 1)

    def first_half(z):
        near = nears[z // (count // 2)]
        for f in range(F):
            v = [
                arrived(kept[c], hold[c, f, z], c, far[c % 2, f, z], near[c % 2, f, z % (count // 2)])
                for c in range(CAP)
            ]
            half[z % 8, f, 0], half[z % 8, f, 2] = swap_64(v[0], v[2], lane)
            half[z % 8, f, 1], half[z % 8, f, 3] = swap_64(v[1], v[3], lane)

    def second_half(z):
        for f in range(F):
            a, b, c, d = [half[z % 8, f, j] for j in range(4)]
            target[f, index + z, 0], target[f, index + z, 1] = swap_32(a, b, lane)
            target[f, index + z, 2], target[f, index + z, 3] = swap_32(c, d, lane)

    for z in range(count + 4):
        if z < count:
            first_half(z)
        if z >= 4:
            second_half(z - 4)


def turn_low_body(owner, hold, near_0, near_1, far, q, half):
    turn_part(kept_flags(owner), HALF, hold, (near_0, near_1), far, q, 3, half)
    for f in range(F):
        q[f, 0] = q[f, 3]
        q[f, 1] = q[f, 3]
        q[f, 2] = q[f, 3]


def turn_high_body(
    owner, hold, near_0, near_1, far, q_low, after, q, z_own, y_own, z_pair, z_cross, y_near, y_far, half
):
    turn_part(kept_flags(owner), B - HALF, hold, (near_0, near_1), far, q, 5, half)
    odd_z, odd_y = odd("gx"), odd("gy")
    for f in range(F):
        for k in range(5):
            q[f, k] = q_low[f, k + LOW]
        top = B + 2 - LOW
        q[f, top + 1] = q[f, top]
        q[f, top + 2] = q[f, top]
        ends = [q_low[f, 3], q_low[f, 4], q[f, top - 1], q[f, top]]
        for k in range(4):
            z_own[f, k] = ends[k]
        for k in range(2):
            z_pair[f, k] = jnp.where(odd_z, ends[k], ends[2 + k])
            z_cross[f, k] = jnp.where(odd_z, ends[2 + k], ends[k])
        for b in range(4):
            span = slice(8 * b, 8 * b + 8)
            source, z = (q_low, 8 * b + 3) if b < 2 else (q, 8 * b + 3 - LOW)
            ends = [source[f, z : z + 8, j, 0 if j < 2 else 7, :] for j in range(4)]
            for k in range(4):
                y_own[f, k, span, :] = ends[k]
            for k in range(2):
                y_near[f, k, span, :] = jnp.where(odd_y, ends[k], ends[2 + k])
                y_far[f, k, span, :] = jnp.where(odd_y, ends[2 + k], ends[k])


def turn(body, name, planes, owner, arrays, others, after=()):
    shapes = [(F, planes, 4, ROWS, LANES)] + others
    return pl.pallas_call(
        body,
        name=name,
        out_shape=tuple(jax.ShapeDtypeStruct(shape, F32) for shape in shapes),
        in_specs=[SMEM] + [VMEM] * (len(arrays) + len(after)),
        out_specs=(VMEM,) * len(shapes),
        scratch_shapes=[pltpu.VMEM((8, F, 4, ROWS, LANES), F32)],
        compiler_params=pltpu.CompilerParams(vmem_limit_bytes=24 << 20),
        cost_estimate=pl.CostEstimate(flops=0, bytes_accessed=6000000, transcendentals=0),
    )(owner, *arrays, *after)


def turn_low(owner, *arrays):
    return turn(turn_low_body, "turn_low", LOW + 10, owner, arrays, [])[0]


def turn_high(owner, after, *arrays):
    z_own, y_own = (F, 4, 4, ROWS, LANES), (F, 4, B, LANES)
    z_half, y_half = (F, 2, 4, ROWS, LANES), (F, 2, B, LANES)
    others = [z_own, y_own, z_half, z_half, y_half, y_half]
    return turn(turn_high_body, "turn_high", B - LOW + 10, owner, arrays, others, (after,))


def minmod(a, b):
    return jnp.maximum(jnp.minimum(a, b), jnp.minimum(jnp.maximum(a, b), 0.0))


def conduction(v):
    return jnp.exp(0.5 * jnp.tanh(v))


LEAD = 5
J = range(4)


def step_body(
    first, count, chunk, spread, q, *rest,
):
    (
        out, token, firsts, lasts, ends, result, carry_p, carry_n, carry_c, dx, cx, px, mx, nx, done, turned, sem_out,
    ) = rest[-17:]
    token[...] = jnp.zeros_like(token)
    lane = lax.broadcasted_iota(jnp.int32, (8, LANES), 1)
    sub = lax.broadcasted_iota(jnp.int32, (8, LANES), 0)
    scale = [0.5 * spread[f] for f in range(F)]

    def y_next(value, end):
        return jnp.where(sub == 7, end, pltpu.roll(value, 7, 0))

    def y_last(value, end):
        return jnp.where(sub == 0, end, pltpu.roll(value, 1, 0))

    def leaving(k):
        z = chunk * k
        return [
            pltpu.make_async_copy(
                result.at[c, :, pl.ds(z + LEAD, chunk)],
                out.at[:, pl.ds(first + z, chunk), :, c, 0],
                sem_out.at[k, c],
            )
            for c in range(CAP)
        ]

    def late(i):
        for f in range(F):
            for j in (0, 2):
                result[j, f, i], result[j + 1, f, i] = swap_32(turned[f, j], turned[f, j + 1], lane)
        for f in range(F):
            for j in (0, 1):
                turned[f, j], turned[f, j + 2] = swap_64(done[f, j], done[f, j + 2], lane)

    def middle(i):
        here = [carry_c[j] for j in J]
        above = [conduction(q[5, i + 1, j]) for j in J]
        cond_z = [a + b for a, b in zip(here, above)]
        for j in J:
            carry_c[j] = above[j]
        beyond = here[1:] + [y_next(here[0], here[3])]
        cond_y = [a + b for a, b in zip(here, beyond)]
        v = [q[1, i, j] for j in J]
        beyond = v[1:] + [y_next(v[0], v[3])]
        weight_y = [0.0625 * (a + b) for a, b in zip(v, beyond)]
        weight_z = [0.0625 * (q[2, i, j] + q[2, i + 1, j]) for j in J]
        edge_y = -0.125 * v[0]
        edge_x = [-0.125 * q[0, i, j] for j in J]
        for f in range(F):
            value = [q[f, i, j] for j in J]
            twice = [a + a for a in value]
            total = []
            for j in J:
                after = q[f, i + 1, j]
                d = after - value[j]
                slope = minmod(d, q[f, i + 2, j] - after)
                double = after + after
                state = jnp.where(weight_z[j] > 0.0, carry_p[f, j], double - slope)
                carry_p[f, j] = double + slope
                net = (scale[f] * cond_z[j]) * d - weight_z[j] * state
                total.append(value[j] + (net - carry_n[f, j]))
                carry_n[f, j] = net
            beyond = value[1:] + [y_next(value[0], value[3])]
            d = [b - a for a, b in zip(value, beyond)]
            before = [y_last(d[3], 0.0)] + d[:3]
            slope = [minmod(a, b) for a, b in zip(before, d)]
            right = [a - b for a, b in zip(twice, slope)]
            right = right[1:] + [y_next(right[0], twice[3])]
            net = []
            for j in J:
                state = jnp.where(weight_y[j] > 0.0, twice[j] + slope[j], right[j])
                net.append((scale[f] * cond_y[j]) * d[j] - weight_y[j] * state)
            before = [y_last(net[3], edge_y * twice[0])] + net[:3]
            for j in J:
                n = nx[f, j]
                t = total[j] + (net[j] - before[j])
                before_x = jnp.where(lane == 0, edge_x[j] * twice[j], pltpu.roll(n, 1, 1))
                done[f, j] = t + (n - before_x)
    def early(i):
        here, there = i & 1, (i + 1) & 1
        for j in J:
            u = q[0, i + 1, j]
            weight = 0.0625 * ((u + u) + dx[here, 0, j])
            from_left = (weight > 0.0) | (lane == 127)
            cond = cx[here, j]
            for f in range(F):
                state = jnp.where(from_left, px[f, j], pltpu.roll(mx[f, j], 127, 1))
                nx[f, j] = (scale[f] * cond) * dx[here, f, j] - weight * state
        for j in J:
            for f in range(F):
                a, d = q[f, i + 2, j], dx[there, f, j]
                slope = minmod(pltpu.roll(d, 1, 1), d)
                px[f, j], mx[f, j] = (a + a) + slope, (a + a) - slope
        for j in J:
            c = conduction(q[5, i + 3, j])
            cx[here, j] = c + jnp.where(lane == 127, c, pltpu.roll(c, 127, 1))
            for f in range(F):
                a = q[f, i + 3, j]
                dx[here, f, j] = jnp.where(lane == 127, 0.0, pltpu.roll(a, 127, 1) - a)

    def starting(i, _):
        early(i)
        return 0

    def plane(i, _):
        late(i)
        middle(i)
        early(i)

        @pl.when((i >= chunk + 4) & ((i - 4) % chunk == 0))
        def _():
            for copy in leaving((i - 4) // chunk - 1):
                copy.start()

        return 0

    def ending(i, _):
        late(i)
        return 0

    for j in J:
        carry_c[j] = conduction(q[5, 3, j])
        cond = conduction(q[5, 2, j]) + carry_c[j]
        weight = 0.0625 * (q[2, 2, j] + q[2, 3, j])
        for f in range(F):
            a, b, c, d = [q[f, k, j] for k in range(1, 5)]
            across = c - b
            left = (b + b) + minmod(b - a, across)
            slope = minmod(across, d - c)
            state = jnp.where(weight > 0.0, left, (c + c) - slope)
            carry_p[f, j] = (c + c) + slope
            carry_n[f, j] = (scale[f] * cond) * across - weight * state
    lax.fori_loop(0, 3, starting, 0)
    lax.fori_loop(3, count + 3, plane, 0)
    lax.fori_loop(count + 3, count + LEAD, ending, 0)
    for copy in leaving(count // chunk - 1):
        copy.start()
    for c in range(CAP):
        for f in range(F):
            for z in range(0, count, 8):
                span = slice(LEAD + z, LEAD + z + 8)
                firsts[c, f, z : z + 8, :] = result[c, f, span, 0, :]
                lasts[c, f, z : z + 8, :] = result[c, f, span, 7, :]
            for k in range(2):
                ends[c, f, k] = result[c, f, LEAD + k + (count - 2 if first else 0)]
    for k in range(count // chunk):
        for copy in leaving(k):
            copy.wait()


def step(first, count, chunk, spread, q, out=None):
    planes = lambda *lead: pltpu.VMEM((*lead, ROWS, LANES), F32)
    return pl.pallas_call(
        functools.partial(step_body, first, count, chunk),
        name="step",
        out_shape=(
            jax.ShapeDtypeStruct((F, B, ROWS, CAP, 1, LANES), F32),
            jax.ShapeDtypeStruct((ROWS, LANES), F32),
            jax.ShapeDtypeStruct((CAP, F, count, LANES), F32),
            jax.ShapeDtypeStruct((CAP, F, count, LANES), F32),
            jax.ShapeDtypeStruct((CAP, F, 2, ROWS, LANES), F32),
        ),
        in_specs=[SMEM, VMEM] + ([] if out is None else [HBM]),
        out_specs=(HBM,) + (VMEM,) * 4,
        input_output_aliases={} if out is None else {2: 0},
        scratch_shapes=[
            planes(CAP, F, count + LEAD),
            planes(F, 4),
            planes(F, 4),
            planes(4),
            planes(2, F, 4),
            planes(2, 4),
            planes(F, 4),
            planes(F, 4),
            planes(F, 4),
            planes(F, 4),
            planes(F, 4),
            pltpu.SemaphoreType.DMA((count // chunk, CAP)),
        ],
        compiler_params=pltpu.CompilerParams(vmem_limit_bytes=24 << 20),
        cost_estimate=pl.CostEstimate(flops=0, bytes_accessed=20000000, transcendentals=0),
    )(spread, q, *(() if out is None else (out,)))


def change(far, out_1, in_0, in_1, u_out, u_0, u_1, c_out, c_0, scale):
    d = in_0 - out_1
    slope = minmod(d, in_1 - in_0)
    inner = -jnp.maximum(0.0625 * (u_0 + u_1), 0.0) * slope
    weight = 0.0625 * (u_out + u_0)
    left = (out_1 + out_1) + minmod(out_1 - far, d)
    right = (in_0 + in_0) - slope
    net = (scale * (c_out + c_0)) * d - weight * jnp.where(weight > 0.0, left, right)
    outer = net + (0.125 * u_0) * (in_0 + in_0)
    return inner - outer, -inner


def both_ends(below, own, above, velocity, has_below, has_above, scale):
    u = [below(velocity, 1)] + [own(velocity, k) for k in range(4)] + [above(velocity, 0)]
    c = [conduction(v) for v in (below(5, 1), own(5, 0), own(5, 3), above(5, 0))]
    result = []
    for f in range(F):
        layers = [own(f, k) for k in range(4)]
        a, b = change(
            below(f, 0), below(f, 1), layers[0], layers[1], u[0], u[1], u[2], c[0], c[1], scale[f]
        )
        e, d = change(
            above(f, 1), above(f, 0), layers[3], layers[2], -u[5], -u[4], -u[3], c[3], c[2], scale[f]
        )
        a, b = jnp.where(has_below, a, 0.0), jnp.where(has_below, b, 0.0)
        d, e = jnp.where(has_above, d, 0.0), jnp.where(has_above, e, 0.0)
        result.append([a, b, d, e])
    return result


def ends_body(
    spread, z_own, y_own, y_far, z_pair, z_cross, y_near,
    first_low, last_low, ends_low, first_high, last_high, ends_high, before, out,
    z_add, y_add, planes, first, last, sem_out,
):
    gx, gy = lax.axis_index("gx"), lax.axis_index("gy")
    odd_z, odd_y = odd("gx"), odd("gy")
    lane = lax.broadcasted_iota(jnp.int32, (8, LANES), 1)
    sub = lax.broadcasted_iota(jnp.int32, (8, LANES), 0)
    scale = [0.5 * spread[f] for f in range(F)]

    rows_out, whole_out = [], []
    for c in range(CAP):
        rows_out.append(pltpu.make_async_copy(first.at[c], out.at[:, :, 0, c, 0], sem_out.at[c, 0]))
        rows_out.append(pltpu.make_async_copy(last.at[c], out.at[:, :, 7, c, 0], sem_out.at[c, 1]))
        for k, z in enumerate((0, 30)):
            there = out.at[:, z : z + 2, :, c, 0]
            here = planes.at[c, :, 2 * k : 2 * k + 2]
            whole_out.append(pltpu.make_async_copy(here, there, sem_out.at[c, 2 + k]))

    for j in range(4):
        changes = both_ends(
            lambda f, k: jnp.where(odd_z, z_pair[f, k, j], z_cross[f, k, j]),
            lambda f, k: z_own[f, k, j],
            lambda f, k: jnp.where(odd_z, z_cross[f, k, j], z_pair[f, k, j]),
            2, gx > 0, gx < lax.axis_size("gx") - 1, scale,
        )
        for f in range(F):
            for k in range(4):
                z_add[f, k, j] = changes[f][k]
    for b in range(4):
        span = slice(8 * b, 8 * b + 8)
        changes = both_ends(
            lambda f, k: jnp.where(odd_y, y_near[f, k, span, :], y_far[f, k, span, :]),
            lambda f, k: y_own[f, k, span, :],
            lambda f, k: jnp.where(odd_y, y_far[f, k, span, :], y_near[f, k, span, :]),
            1, gy > 0, gy < lax.axis_size("gy") - 1, scale,
        )
        for f in range(F):
            for c, value in enumerate(turned_to_layers(changes[f], lane)):
                y_add[c, f, span, :] = value

    for c in range(CAP):
        for f in range(F):
            for b in range(4):
                span = slice(8 * b, 8 * b + 8)
                value = y_add[c, f, span, :]
                part = slice(8 * (b % 2), 8 * (b % 2) + 8)
                low = (first_low if b < 2 else first_high)[c, f, part, :]
                high = (last_low if b < 2 else last_high)[c, f, part, :]
                first[c, f, span, :] = low + jnp.where(lane < 64, value, 0.0)
                last[c, f, span, :] = high + jnp.where(lane >= 64, value, 0.0)
        rows_out[2 * c].start()
        rows_out[2 * c + 1].start()
    corner = ((sub == 0) & (lane < 64)) | ((sub == 7) & (lane >= 64))
    for f in range(F):
        for k, z in enumerate((0, 1, 30, 31)):
            values = turned_to_layers([z_add[f, k, j] for j in range(4)], lane)
            for c in range(CAP):
                plane = (ends_low if k < 2 else ends_high)[c, f, k % 2]
                add = values[c] + jnp.where(corner, y_add[c, f, z : z + 1, :], 0.0)
                planes[c, f, k] = plane + add
    for copy in rows_out:
        copy.wait()
    run_all(whole_out)


def ends(spread, *arrays):
    rows = pltpu.VMEM((CAP, F, B, LANES), F32)
    planes = pltpu.VMEM((CAP, F, 4, ROWS, LANES), F32)
    return pl.pallas_call(
        ends_body,
        name="ends",
        out_shape=jax.ShapeDtypeStruct((F, B, ROWS, CAP, 1, LANES), F32),
        in_specs=[SMEM] + [VMEM] * (len(arrays) - 1) + [HBM],
        out_specs=HBM,
        input_output_aliases={len(arrays): 0},
        scratch_shapes=[
            pltpu.VMEM((F, 4, 4, ROWS, LANES), F32),
            rows,
            planes,
            rows,
            rows,
            pltpu.SemaphoreType.DMA((CAP, 4)),
        ],
        compiler_params=pltpu.CompilerParams(vmem_limit_bytes=24 << 20),
        cost_estimate=pl.CostEstimate(flops=0, bytes_accessed=6000000, transcendentals=0),
    )(spread, *arrays)


def exchange(block, axes, first, wrap=False):
    count = lax.axis_size(axes)
    pairs = []
    for i in range(first, count, 2):
        j = (i + 1) % count
        if i + 1 < count or wrap:
            pairs += [(i, j), (j, i)]
    return lax.ppermute(block, axes, pairs)


def local(old_state, old_owner, old_slot, diffusivity):
    x = old_state.reshape(8, F, B, ROWS, LANES).transpose(1, 2, 3, 0, 4)[..., None, :]
    far_low, far_high, token = far_boxes(x)
    *nears, hold_low, hold_high = near_boxes(x, token)
    far_low = exchange(far_low, AXES, 1, wrap=True)
    far_high = exchange(far_high, AXES, 1, wrap=True)
    nears = [exchange(near, AXES, 0) for near in nears]
    q_low = turn_low(old_owner, hold_low, *nears[:2], far_low)
    out, token, *low_ends = step(0, LOW, 8, diffusivity, q_low)
    q_high, z_own, y_own, z_pair, z_cross, y_near, y_far = turn_high(
        old_owner, token, hold_high, *nears[2:], far_high, q_low
    )
    y_near = exchange(y_near, "gy", 0)
    y_far = exchange(y_far, "gy", 1)
    z_pair = exchange(z_pair, "gx", 0)
    z_cross = exchange(z_cross, "gx", 1)
    out, _, *high_ends = step(LOW, B - LOW, 8, diffusivity, q_high, out)
    out = ends(
        diffusivity, z_own, y_own, y_far, z_pair, z_cross, y_near, *low_ends, *high_ends, out
    )
    return out[..., 0, :].transpose(3, 0, 1, 2, 4).reshape(CAP, F, B * B * B)


def solution(mesh):
    placed = (P(AXES, None, None), P(), P(), P())
    return jax.shard_map(
        local, mesh=mesh, in_specs=placed, out_specs=P(AXES, None, None), check_vma=False
    )
```

```python
import functools

import jax
import jax.numpy as jnp
from jax import lax
from jax.experimental import pallas as pl
from jax.experimental.pallas import tpu as pltpu
from jax.sharding import PartitionSpec as P

B = 32
F = 6
CAP = 4
HALF = 18
LOW = HALF - 2
PARTS = ((0, HALF // 2), (HALF // 2, HALF), (HALF, (HALF + B) // 2), ((HALF + B) // 2, B))
ROWS = 8
LANES = 128
AXES = ("gx", "gy")
F32 = jnp.float32
HBM = pl.BlockSpec(memory_space=pl.ANY)
VMEM = pl.BlockSpec(memory_space=pltpu.VMEM)
SMEM = pl.BlockSpec(memory_space=pltpu.SMEM)
WIDE = 56 << 20


def run_all(copies):
    for copy in copies:
        copy.start()
    for copy in copies:
        copy.wait()


def odd(axis):
    return lax.axis_index(axis) % 2 == 1


def leaving_copies(x, near, target, planes, sem):
    first = jnp.where(odd("gy"), 0, 6) if near else jnp.where(odd("gy"), 6, 0)
    return [
        pltpu.make_async_copy(x.at[:, planes, :, first + j, 0], target.at[j], sem.at[j])
        for j in range(2)
    ]


def far_body(x, low, token, sem):
    token[...] = jnp.zeros_like(token)
    run_all(leaving_copies(x, False, low, slice(0, HALF), sem))


def near_body(x, after, high, *rest):
    nears, (hold_low, hold_high, sem) = rest[: len(PARTS)], rest[len(PARTS) :]
    copies = leaving_copies(x, False, high, slice(HALF, B), sem.at[2 + len(PARTS)])
    for k, near in enumerate(nears):
        copies += leaving_copies(x, True, near, slice(*PARTS[k]), sem.at[2 + k])
    for k, hold in enumerate((hold_low, hold_high)):
        for c in range(CAP):
            planes = slice(HALF, B) if k else slice(0, HALF)
            copies.append(
                pltpu.make_async_copy(x.at[:, planes, :, 2 + c, 0], hold.at[c], sem.at[k, c])
            )
    run_all(copies)


def from_slots(body, name, arrays, shapes, sems, limit):
    shapes = tuple(jax.ShapeDtypeStruct(shape, F32) for shape in shapes)
    return pl.pallas_call(
        body,
        name=name,
        out_shape=shapes,
        in_specs=[HBM] * len(arrays),
        out_specs=(VMEM,) * len(shapes),
        scratch_shapes=[pltpu.SemaphoreType.DMA(sems)],
        compiler_params=pltpu.CompilerParams(vmem_limit_bytes=limit),
        cost_estimate=pl.CostEstimate(flops=0, bytes_accessed=1000, transcendentals=0),
    )(*arrays)


def far_boxes(x):
    return from_slots(far_body, "far", [x], [(2, F, HALF, ROWS, LANES), (ROWS, LANES)], (2,), WIDE)


def near_boxes(x, after):
    boxes = lambda count, planes: (count, F, planes, ROWS, LANES)
    shapes = [boxes(2, B - HALF)] + [boxes(2, end - start) for start, end in PARTS]
    shapes += [boxes(CAP, HALF), boxes(CAP, B - HALF)]
    return from_slots(near_body, "near", [x, after], shapes, (3 + len(PARTS), CAP), 24 << 20)


def device_number():
    return lax.axis_index("gx") * lax.axis_size("gy") + lax.axis_index("gy")


def kept_flags(owner):
    device = device_number()
    return [owner[device * CAP + c] == device for c in range(CAP)]


def arrived(kept, here, c, far, near):
    from_far = odd("gy") if c >= 2 else jnp.logical_not(odd("gy"))
    return jnp.where(kept, here, jnp.where(from_far, far, near))


def swap_64(a, b, lane):
    low = lane < 64
    m = pltpu.roll(jnp.where(low, b, a), 64, 1)
    return jnp.where(low, a, m), jnp.where(low, m, b)


def swap_32(a, b, lane):
    even = (lane & 32) == 0
    m = jnp.where(even, b, a)
    return jnp.where(even, a, pltpu.roll(m, 32, 1)), jnp.where(even, pltpu.roll(m, 96, 1), b)


def turned_to_layers(v, lane):
    a, c = swap_64(v[0], v[2], lane)
    b, d = swap_64(v[1], v[3], lane)
    return *swap_32(a, b, lane), *swap_32(c, d, lane)


def turn_part(kept, count, hold, nears, far, target, index, half):
    lane = lax.broadcasted_iota(jnp.int32, (8, LANES), 1)

    def first_half(z):
        near = nears[z // (count // 2)]
        for f in range(F):
            v = [
                arrived(kept[c], hold[c, f, z], c, far[c % 2, f, z], near[c % 2, f, z % (count // 2)])
                for c in range(CAP)
            ]
            half[z % 8, f, 0], half[z % 8, f, 2] = swap_64(v[0], v[2], lane)
            half[z % 8, f, 1], half[z % 8, f, 3] = swap_64(v[1], v[3], lane)

    def second_half(z):
        for f in range(F):
            a, b, c, d = [half[z % 8, f, j] for j in range(4)]
            target[f, index + z, 0], target[f, index + z, 1] = swap_32(a, b, lane)
            target[f, index + z, 2], target[f, index + z, 3] = swap_32(c, d, lane)

    for z in range(count + 4):
        if z < count:
            first_half(z)
        if z >= 4:
            second_half(z - 4)


def turn_low_body(owner, hold, near_0, near_1, far, q, half):
    turn_part(kept_flags(owner), HALF, hold, (near_0, near_1), far, q, 3, half)
    for f in range(F):
        q[f, 0] = q[f, 3]
        q[f, 1] = q[f, 3]
        q[f, 2] = q[f, 3]


def turn_high_body(
    owner, hold, near_0, near_1, far, q_low, after, q, z_own, y_own, z_pair, z_cross, y_near, y_far, half
):
    turn_part(kept_flags(owner), B - HALF, hold, (near_0, near_1), far, q, 5, half)
    odd_z, odd_y = odd("gx"), odd("gy")
    for f in range(F):
        for k in range(5):
            q[f, k] = q_low[f, k + LOW]
        top = B + 2 - LOW
        q[f, top + 1] = q[f, top]
        q[f, top + 2] = q[f, top]
        ends = [q_low[f, 3], q_low[f, 4], q[f, top - 1], q[f, top]]
        for k in range(4):
            z_own[f, k] = ends[k]
        for k in range(2):
            z_pair[f, k] = jnp.where(odd_z, ends[k], ends[2 + k])
            z_cross[f, k] = jnp.where(odd_z, ends[2 + k], ends[k])
        for b in range(4):
            span = slice(8 * b, 8 * b + 8)
            source, z = (q_low, 8 * b + 3) if b < 2 else (q, 8 * b + 3 - LOW)
            ends = [source[f, z : z + 8, j, 0 if j < 2 else 7, :] for j in range(4)]
            for k in range(4):
                y_own[f, k, span, :] = ends[k]
            for k in range(2):
                y_near[f, k, span, :] = jnp.where(odd_y, ends[k], ends[2 + k])
                y_far[f, k, span, :] = jnp.where(odd_y, ends[2 + k], ends[k])


def turn(body, name, planes, owner, arrays, others, after=()):
    shapes = [(F, planes, 4, ROWS, LANES)] + others
    return pl.pallas_call(
        body,
        name=name,
        out_shape=tuple(jax.ShapeDtypeStruct(shape, F32) for shape in shapes),
        in_specs=[SMEM] + [VMEM] * (len(arrays) + len(after)),
        out_specs=(VMEM,) * len(shapes),
        scratch_shapes=[pltpu.VMEM((8, F, 4, ROWS, LANES), F32)],
        compiler_params=pltpu.CompilerParams(vmem_limit_bytes=24 << 20),
        cost_estimate=pl.CostEstimate(flops=0, bytes_accessed=6000000, transcendentals=0),
    )(owner, *arrays, *after)


def turn_low(owner, *arrays):
    return turn(turn_low_body, "turn_low", LOW + 10, owner, arrays, [])[0]


def turn_high(owner, after, *arrays):
    z_own, y_own = (F, 4, 4, ROWS, LANES), (F, 4, B, LANES)
    z_half, y_half = (F, 2, 4, ROWS, LANES), (F, 2, B, LANES)
    others = [z_own, y_own, z_half, z_half, y_half, y_half]
    return turn(turn_high_body, "turn_high", B - LOW + 10, owner, arrays, others, (after,))


def minmod(a, b):
    return jnp.maximum(jnp.minimum(a, b), jnp.minimum(jnp.maximum(a, b), 0.0))


def conduction(v):
    return jnp.exp(0.5 * jnp.tanh(v))


LEAD = 5
J = range(4)


def step_body(
    first, count, chunk, spread, q, *rest,
):
    (
        out, token, firsts, lasts, ends, result, carry_p, carry_n, carry_c, dx, cx, px, mx, nx, done, turned, sem_out,
    ) = rest[-17:]
    token[...] = jnp.zeros_like(token)
    lane = lax.broadcasted_iota(jnp.int32, (8, LANES), 1)
    sub = lax.broadcasted_iota(jnp.int32, (8, LANES), 0)
    scale = [0.5 * spread[f] for f in range(F)]

    def y_next(value, end):
        return jnp.where(sub == 7, end, pltpu.roll(value, 7, 0))

    def y_last(value, end):
        return jnp.where(sub == 0, end, pltpu.roll(value, 1, 0))

    def leaving(k):
        z = chunk * k
        return [
            pltpu.make_async_copy(
                result.at[c, :, pl.ds(z + LEAD, chunk)],
                out.at[:, pl.ds(first + z, chunk), :, c, 0],
                sem_out.at[k, c],
            )
            for c in range(CAP)
        ]

    def late(i):
        for f in range(F):
            for j in (0, 2):
                result[j, f, i], result[j + 1, f, i] = swap_32(turned[f, j], turned[f, j + 1], lane)
        for f in range(F):
            for j in (0, 1):
                turned[f, j], turned[f, j + 2] = swap_64(done[f, j], done[f, j + 2], lane)

    def middle(i):
        here = [carry_c[j] for j in J]
        above = [conduction(q[5, i + 1, j]) for j in J]
        cond_z = [a + b for a, b in zip(here, above)]
        for j in J:
            carry_c[j] = above[j]
        beyond = here[1:] + [y_next(here[0], here[3])]
        cond_y = [a + b for a, b in zip(here, beyond)]
        v = [q[1, i, j] for j in J]
        beyond = v[1:] + [y_next(v[0], v[3])]
        weight_y = [0.0625 * (a + b) for a, b in zip(v, beyond)]
        weight_z = [0.0625 * (q[2, i, j] + q[2, i + 1, j]) for j in J]
        edge_y = -0.125 * v[0]
        edge_x = [-0.125 * q[0, i, j] for j in J]
        for f in range(F):
            value = [q[f, i, j] for j in J]
            twice = [a + a for a in value]
            total = []
            for j in J:
                after = q[f, i + 1, j]
                d = after - value[j]
                slope = minmod(d, q[f, i + 2, j] - after)
                double = after + after
                state = jnp.where(weight_z[j] > 0.0, carry_p[f, j], double - slope)
                carry_p[f, j] = double + slope
                net = (scale[f] * cond_z[j]) * d - weight_z[j] * state
                total.append(value[j] + (net - carry_n[f, j]))
                carry_n[f, j] = net
            beyond = value[1:] + [y_next(value[0], value[3])]
            d = [b - a for a, b in zip(value, beyond)]
            before = [y_last(d[3], 0.0)] + d[:3]
            slope = [minmod(a, b) for a, b in zip(before, d)]
            right = [a - b for a, b in zip(twice, slope)]
            right = right[1:] + [y_next(right[0], twice[3])]
            net = []
            for j in J:
                state = jnp.where(weight_y[j] > 0.0, twice[j] + slope[j], right[j])
                net.append((scale[f] * cond_y[j]) * d[j] - weight_y[j] * state)
            before = [y_last(net[3], edge_y * twice[0])] + net[:3]
            for j in J:
                n = nx[f, j]
                t = total[j] + (net[j] - before[j])
                before_x = jnp.where(lane == 0, edge_x[j] * twice[j], pltpu.roll(n, 1, 1))
                done[f, j] = t + (n - before_x)
    def early(i):
        here, there = i & 1, (i + 1) & 1
        for j in J:
            u = q[0, i + 1, j]
            weight = 0.0625 * ((u + u) + dx[here, 0, j])
            from_left = (weight > 0.0) | (lane == 127)
            cond = cx[here, j]
            for f in range(F):
                state = jnp.where(from_left, px[f, j], pltpu.roll(mx[f, j], 127, 1))
                nx[f, j] = (scale[f] * cond) * dx[here, f, j] - weight * state
        for j in J:
            for f in range(F):
                a, d = q[f, i + 2, j], dx[there, f, j]
                slope = minmod(pltpu.roll(d, 1, 1), d)
                px[f, j], mx[f, j] = (a + a) + slope, (a + a) - slope
        for j in J:
            c = conduction(q[5, i + 3, j])
            cx[here, j] = c + jnp.where(lane == 127, c, pltpu.roll(c, 127, 1))
            for f in range(F):
                a = q[f, i + 3, j]
                dx[here, f, j] = jnp.where(lane == 127, 0.0, pltpu.roll(a, 127, 1) - a)

    def starting(i, _):
        early(i)
        return 0

    def plane(i, _):
        late(i)
        middle(i)
        early(i)

        @pl.when((i >= chunk + 4) & ((i - 4) % chunk == 0))
        def _():
            for copy in leaving((i - 4) // chunk - 1):
                copy.start()

        return 0

    def ending(i, _):
        late(i)
        return 0

    for j in J:
        carry_c[j] = conduction(q[5, 3, j])
        cond = conduction(q[5, 2, j]) + carry_c[j]
        weight = 0.0625 * (q[2, 2, j] + q[2, 3, j])
        for f in range(F):
            a, b, c, d = [q[f, k, j] for k in range(1, 5)]
            across = c - b
            left = (b + b) + minmod(b - a, across)
            slope = minmod(across, d - c)
            state = jnp.where(weight > 0.0, left, (c + c) - slope)
            carry_p[f, j] = (c + c) + slope
            carry_n[f, j] = (scale[f] * cond) * across - weight * state
    lax.fori_loop(0, 3, starting, 0)
    lax.fori_loop(3, count + 3, plane, 0)
    lax.fori_loop(count + 3, count + LEAD, ending, 0)
    for copy in leaving(count // chunk - 1):
        copy.start()
    for c in range(CAP):
        for f in range(F):
            for z in range(0, count, 8):
                span = slice(LEAD + z, LEAD + z + 8)
                firsts[c, f, z : z + 8, :] = result[c, f, span, 0, :]
                lasts[c, f, z : z + 8, :] = result[c, f, span, 7, :]
            for k in range(2):
                ends[c, f, k] = result[c, f, LEAD + k + (count - 2 if first else 0)]
    for k in range(count // chunk):
        for copy in leaving(k):
            copy.wait()


def step(first, count, chunk, spread, q, out=None):
    planes = lambda *lead: pltpu.VMEM((*lead, ROWS, LANES), F32)
    return pl.pallas_call(
        functools.partial(step_body, first, count, chunk),
        name="step",
        out_shape=(
            jax.ShapeDtypeStruct((F, B, ROWS, CAP, 1, LANES), F32),
            jax.ShapeDtypeStruct((ROWS, LANES), F32),
            jax.ShapeDtypeStruct((CAP, F, count, LANES), F32),
            jax.ShapeDtypeStruct((CAP, F, count, LANES), F32),
            jax.ShapeDtypeStruct((CAP, F, 2, ROWS, LANES), F32),
        ),
        in_specs=[SMEM, VMEM] + ([] if out is None else [HBM]),
        out_specs=(HBM,) + (VMEM,) * 4,
        input_output_aliases={} if out is None else {2: 0},
        scratch_shapes=[
            planes(CAP, F, count + LEAD),
            planes(F, 4),
            planes(F, 4),
            planes(4),
            planes(2, F, 4),
            planes(2, 4),
            planes(F, 4),
            planes(F, 4),
            planes(F, 4),
            planes(F, 4),
            planes(F, 4),
            pltpu.SemaphoreType.DMA((count // chunk, CAP)),
        ],
        compiler_params=pltpu.CompilerParams(vmem_limit_bytes=24 << 20),
        cost_estimate=pl.CostEstimate(flops=0, bytes_accessed=20000000, transcendentals=0),
    )(spread, q, *(() if out is None else (out,)))


def change(far, out_1, in_0, in_1, u_out, u_0, u_1, c_out, c_0, scale):
    d = in_0 - out_1
    slope = minmod(d, in_1 - in_0)
    inner = -jnp.maximum(0.0625 * (u_0 + u_1), 0.0) * slope
    weight = 0.0625 * (u_out + u_0)
    left = (out_1 + out_1) + minmod(out_1 - far, d)
    right = (in_0 + in_0) - slope
    net = (scale * (c_out + c_0)) * d - weight * jnp.where(weight > 0.0, left, right)
    outer = net + (0.125 * u_0) * (in_0 + in_0)
    return inner - outer, -inner


def both_ends(below, own, above, velocity, has_below, has_above, scale):
    u = [below(velocity, 1)] + [own(velocity, k) for k in range(4)] + [above(velocity, 0)]
    c = [conduction(v) for v in (below(5, 1), own(5, 0), own(5, 3), above(5, 0))]
    result = []
    for f in range(F):
        layers = [own(f, k) for k in range(4)]
        a, b = change(
            below(f, 0), below(f, 1), layers[0], layers[1], u[0], u[1], u[2], c[0], c[1], scale[f]
        )
        e, d = change(
            above(f, 1), above(f, 0), layers[3], layers[2], -u[5], -u[4], -u[3], c[3], c[2], scale[f]
        )
        a, b = jnp.where(has_below, a, 0.0), jnp.where(has_below, b, 0.0)
        d, e = jnp.where(has_above, d, 0.0), jnp.where(has_above, e, 0.0)
        result.append([a, b, d, e])
    return result


def ends_body(
    spread, z_own, y_own, z_pair, z_cross, y_far, y_near,
    first_low, last_low, ends_low, first_high, last_high, ends_high, before, out,
    z_add, y_add, planes, first, last, sem_out,
):
    gx, gy = lax.axis_index("gx"), lax.axis_index("gy")
    odd_z, odd_y = odd("gx"), odd("gy")
    lane = lax.broadcasted_iota(jnp.int32, (8, LANES), 1)
    sub = lax.broadcasted_iota(jnp.int32, (8, LANES), 0)
    scale = [0.5 * spread[f] for f in range(F)]

    rows_out, whole_out = [], []
    for c in range(CAP):
        rows_out.append(pltpu.make_async_copy(first.at[c], out.at[:, :, 0, c, 0], sem_out.at[c, 0]))
        rows_out.append(pltpu.make_async_copy(last.at[c], out.at[:, :, 7, c, 0], sem_out.at[c, 1]))
        for k, z in enumerate((0, 30)):
            there = out.at[:, z : z + 2, :, c, 0]
            here = planes.at[c, :, 2 * k : 2 * k + 2]
            whole_out.append(pltpu.make_async_copy(here, there, sem_out.at[c, 2 + k]))

    for j in range(4):
        changes = both_ends(
            lambda f, k: jnp.where(odd_z, z_pair[f, k, j], z_cross[f, k, j]),
            lambda f, k: z_own[f, k, j],
            lambda f, k: jnp.where(odd_z, z_cross[f, k, j], z_pair[f, k, j]),
            2, gx > 0, gx < lax.axis_size("gx") - 1, scale,
        )
        for f in range(F):
            for k in range(4):
                z_add[f, k, j] = changes[f][k]
    for b in range(4):
        span = slice(8 * b, 8 * b + 8)
        changes = both_ends(
            lambda f, k: jnp.where(odd_y, y_near[f, k, span, :], y_far[f, k, span, :]),
            lambda f, k: y_own[f, k, span, :],
            lambda f, k: jnp.where(odd_y, y_far[f, k, span, :], y_near[f, k, span, :]),
            1, gy > 0, gy < lax.axis_size("gy") - 1, scale,
        )
        for f in range(F):
            for c, value in enumerate(turned_to_layers(changes[f], lane)):
                y_add[c, f, span, :] = value

    for c in range(CAP):
        for f in range(F):
            for b in range(4):
                span = slice(8 * b, 8 * b + 8)
                value = y_add[c, f, span, :]
                part = slice(8 * (b % 2), 8 * (b % 2) + 8)
                low = (first_low if b < 2 else first_high)[c, f, part, :]
                high = (last_low if b < 2 else last_high)[c, f, part, :]
                first[c, f, span, :] = low + jnp.where(lane < 64, value, 0.0)
                last[c, f, span, :] = high + jnp.where(lane >= 64, value, 0.0)
        rows_out[2 * c].start()
        rows_out[2 * c + 1].start()
    corner = ((sub == 0) & (lane < 64)) | ((sub == 7) & (lane >= 64))
    for f in range(F):
        for k, z in enumerate((0, 1, 30, 31)):
            values = turned_to_layers([z_add[f, k, j] for j in range(4)], lane)
            for c in range(CAP):
                plane = (ends_low if k < 2 else ends_high)[c, f, k % 2]
                add = values[c] + jnp.where(corner, y_add[c, f, z : z + 1, :], 0.0)
                planes[c, f, k] = plane + add
    for copy in rows_out:
        copy.wait()
    run_all(whole_out)


def ends(spread, *arrays):
    rows = pltpu.VMEM((CAP, F, B, LANES), F32)
    planes = pltpu.VMEM((CAP, F, 4, ROWS, LANES), F32)
    return pl.pallas_call(
        ends_body,
        name="ends",
        out_shape=jax.ShapeDtypeStruct((F, B, ROWS, CAP, 1, LANES), F32),
        in_specs=[SMEM] + [VMEM] * (len(arrays) - 1) + [HBM],
        out_specs=HBM,
        input_output_aliases={len(arrays): 0},
        scratch_shapes=[
            pltpu.VMEM((F, 4, 4, ROWS, LANES), F32),
            rows,
            planes,
            rows,
            rows,
            pltpu.SemaphoreType.DMA((CAP, 4)),
        ],
        compiler_params=pltpu.CompilerParams(vmem_limit_bytes=24 << 20),
        cost_estimate=pl.CostEstimate(flops=0, bytes_accessed=6000000, transcendentals=0),
    )(spread, *arrays)


def exchange(block, axes, first, wrap=False):
    count = lax.axis_size(axes)
    pairs = []
    for i in range(first, count, 2):
        j = (i + 1) % count
        if i + 1 < count or wrap:
            pairs += [(i, j), (j, i)]
    return lax.ppermute(block, axes, pairs)


def local(old_state, old_owner, old_slot, diffusivity):
    x = old_state.reshape(8, F, B, ROWS, LANES).transpose(1, 2, 3, 0, 4)[..., None, :]
    far_low, token = far_boxes(x)
    far_high, *nears, hold_low, hold_high = near_boxes(x, token)
    far_low = exchange(far_low, AXES, 1, wrap=True)
    far_high = exchange(far_high, AXES, 1, wrap=True)
    nears = [exchange(near, AXES, 0) for near in nears]
    q_low = turn_low(old_owner, hold_low, *nears[:2], far_low)
    out, token, *low_ends = step(0, LOW, 8, diffusivity, q_low)
    q_high, z_own, y_own, z_pair, z_cross, y_near, y_far = turn_high(
        old_owner, token, hold_high, *nears[2:], far_high, q_low
    )
    y_near = exchange(y_near, "gy", 0)
    y_far = exchange(y_far, "gy", 1)
    z_pair = exchange(z_pair, "gx", 0)
    z_cross = exchange(z_cross, "gx", 1)
    out, _, *high_ends = step(LOW, B - LOW, 8, diffusivity, q_high, out)
    out = ends(
        diffusivity, z_own, y_own, z_pair, z_cross, y_far, y_near, *low_ends, *high_ends, out
    )
    return out[..., 0, :].transpose(3, 0, 1, 2, 4).reshape(CAP, F, B * B * B)


def solution(mesh):
    placed = (P(AXES, None, None), P(), P(), P())
    return jax.shard_map(
        local, mesh=mesh, in_specs=placed, out_specs=P(AXES, None, None), check_vma=False
    )
```
